32 devices in a mesh: ea: 16 (over z, y, x), ta: 2 (over core).
Axes of the slice: x: 2, y: 2, z: 4, core: 2. Of those that a mesh axis runs over, the one named last changes fastest.
Arguments:
- sample_inphase: float32 [128, 256, 256], P('ea'), may hold values from 0.2 to 1.2
- sample_quadrature: float32 [128, 256, 256], P('ea'), may hold values from -3 to 3
- beam_inphase: float32 [128, 3, 32, 32], P('ea'), may hold values from -3 to 3
- beam_quadrature: float32 [128, 3, 32, 32], P('ea'), may hold values from -3 to 3
- recorded_diffraction: float32 [128, 2, 16, 32, 32], P('ea', 'ta'), may hold values from 0.05 to 4
- window_corners: int32 [128, 2, 16, 2], P('ea', 'ta'), may hold values from 0 to 224
- filled_tallies: int32 [128, 2], P('ea', 'ta'), may hold values from 1 to 16, 24 in all within a row
- absorption_templates: float32 [16, 128], replicated, may hold values from -6 to 6
Outputs:
- fitted: float32 [2, 128, 16, 2, 2048], P(None, 'ea', None, 'ta')
- coefficients: float32 [2, 16, 65536], P(None, None, ('ea', 'ta'))
The draws below stay inside these ranges and needn't reach their ends.
Inputs may be any that keep to these rules, and one draw needn't show every extreme that they name: `filled_tallies`: in each energy the two tiles' counts sum to 24 and the larger is at most 16. `window_corners`: offsets of slots at or past their tile's count are not used.
All inputs are finite; a program needn't handle non-finite values. No bound on the sum of `filled_tallies` on one device may be relied on, other than what follows from the above.
Results may differ from the reference program's by a relative error of at most 0.0003.
Values sent between devices are 32-bit elements; how exact they have to be, the bound alone decides.
No kernel may reach another device: no remote copies, remote signals or barrier semaphores. Data moves between devices by JAX's collectives and lax.ppermute only.
A program may use at most 64 MiB of HBM per device.

```python
import math
import jax
import jax.numpy as jnp
import numpy as np
from jax import lax

OBJ = 256
WINDOW_SPAN = 32
MODES = 3
EDGES = 16
BEAM_QUANTA = 128
RASTER_SPOTS = 16
PIX = 2048
N_EA = 16
N_TA = 2


def place_ends(result, stream_key, low, largest):
    longest = result.shape.index(max(result.shape))
    spots = []
    for shift in (0, 1):
        where = [jax.random.randint(jax.random.fold_in(stream_key, axis), (), 0, length) for axis, length in enumerate(result.shape)]
        where[longest] = (where[longest] + shift) % result.shape[longest]
        spots.append(tuple(where))
    return result.at[spots[0]].set(low).at[spots[1]].set(largest)


def shard_levels(key, shape, split, smallest, largest):
    level = 1.0
    for dim, shards_of in split:
        heights = jax.random.uniform(jax.random.fold_in(jax.random.fold_in(key, 6), dim), (shards_of,), jnp.float32, smallest / len(split), largest / len(split))
        level = level * jnp.repeat(jnp.exp(heights), shape[dim] // shards_of).reshape((-1,) + (1,) * (len(shape) - 1 - dim))
    return level


def length_profile(amount, total, limit, skew):
    loads = [(1 << 20) // math.isqrt(grade ** skew) + 1 for grade in range(2, amount + 1)]
    spare, counts = total - limit - (amount - 1), [1] * (amount - 1)
    while spare > 0:
        movable = [i for i in range(amount - 1) if counts[i] < limit]
        whole, budget = sum([loads[i] for i in movable]), spare
        for i in movable:
            addition = min(limit - counts[i], max(1, budget * loads[i] // whole), spare)
            counts[i] = counts[i] + addition
            spare = spare - addition
    return np.array([limit] + counts)


def uneven_parts(own_key, number_of, total, bound, skew):
    if number_of == 2:
        one = jax.random.randint(own_key, (), max(1, total - bound), min(bound, total - 1) + 1)
        return jnp.stack([one, total - one])
    sizes = jnp.asarray(length_profile(number_of, total, bound, skew), jnp.int32)
    pairs = (number_of - 1) // 2
    donor, sink = sizes[1:1 + 2 * pairs:2], sizes[2:2 + 2 * pairs:2]
    margin = jnp.minimum(donor - 1, bound - sink)
    moved = jax.random.randint(jax.random.fold_in(own_key, 1), (pairs,), 0, 1 << 20) % (margin + 1)
    sizes = sizes.at[1:1 + 2 * pairs:2].set(donor - moved).at[2:2 + 2 * pairs:2].set(sink + moved)
    return sizes[jax.random.permutation(jax.random.fold_in(own_key, 2), number_of)]


def scatter_about(own_key, shape, scale, limit, cuts=(), kind=jnp.bfloat16):
    result = jax.random.normal(own_key, shape, jnp.float32) * scale
    if len(cuts) > 0:
        result = shard_levels(own_key, shape, cuts, -0.22, 0.18) * result
    return jnp.clip(result, min=-limit, max=limit).astype(kind)


def setup_inputs(seed: int = 0) -> dict:
    key_list = jax.random.split(jax.random.key(seed), 9)
    return {
        "sample_inphase": jnp.clip(0.2 + 1 * jax.random.uniform(key_list[0], (BEAM_QUANTA, OBJ, OBJ), jnp.float32) ** shard_levels(key_list[0], (BEAM_QUANTA, OBJ, OBJ), ((0, 16),), -0.2, 0.2), 0.2, 1.2),
        "sample_quadrature": scatter_about(key_list[1], (BEAM_QUANTA, OBJ, OBJ), 0.5, 3.0, ((0, 16),), jnp.float32),
        "beam_inphase": scatter_about(key_list[2], (BEAM_QUANTA, MODES, WINDOW_SPAN, WINDOW_SPAN), 0.5, 3.0, ((0, 16),), jnp.float32),
        "beam_quadrature": scatter_about(key_list[3], (BEAM_QUANTA, MODES, WINDOW_SPAN, WINDOW_SPAN), 0.5, 3.0, ((0, 16),), jnp.float32),
        "recorded_diffraction": jnp.clip(jnp.exp(math.log(4.0) - 4.3820266 * jax.random.uniform(key_list[4], (BEAM_QUANTA, N_TA, RASTER_SPOTS, WINDOW_SPAN, WINDOW_SPAN), jnp.float32) ** shard_levels(key_list[4], (BEAM_QUANTA, N_TA, RASTER_SPOTS, WINDOW_SPAN, WINDOW_SPAN), ((0, 16), (1, 2)), -0.2, 0.2)), 0.05, 4.0),
        "window_corners": place_ends(jax.random.randint(key_list[5], (BEAM_QUANTA, N_TA, RASTER_SPOTS, 2), 0, OBJ - WINDOW_SPAN + 1), jax.random.fold_in(key_list[5], 1), 0, OBJ - WINDOW_SPAN).astype(jnp.int32),
        "filled_tallies": jax.vmap(lambda own: uneven_parts(own, N_TA, RASTER_SPOTS * 3 // 2, RASTER_SPOTS, 0))(jax.random.split(key_list[6], BEAM_QUANTA)).reshape((BEAM_QUANTA, N_TA)).astype(jnp.int32),
        "absorption_templates": scatter_about(key_list[7], (EDGES, BEAM_QUANTA), 1.0, 6.0, (), jnp.float32),
    }


HIGHEST_PRECISION = lax.Precision.HIGHEST
FLOOR_POWER = 0.5
REGULARIZER = 1.0

def dft_tables(length):
    counter = jnp.arange(length, dtype=jnp.int32)
    product = counter[:, None] * counter[None, :] % length
    angles = 2.0 * jnp.pi / length * product.astype(jnp.float32)
    norming = 1.0 / jnp.sqrt(jnp.float32(length))
    return (jnp.cos(angles) * norming, -jnp.sin(angles) * norming)

def two_sided(field_re, field_im, table_re, table_im):
    left_re = jnp.einsum('jk,...kl->...jl', table_re, field_re, precision=HIGHEST_PRECISION) - jnp.einsum('jk,...kl->...jl', table_im, field_im, precision=HIGHEST_PRECISION)
    left_im = jnp.einsum('jk,...kl->...jl', table_re, field_im, precision=HIGHEST_PRECISION) + jnp.einsum('jk,...kl->...jl', table_im, field_re, precision=HIGHEST_PRECISION)
    right_re = jnp.einsum('...jk,kl->...jl', left_re, table_re, precision=HIGHEST_PRECISION) - jnp.einsum('...jk,kl->...jl', left_im, table_im, precision=HIGHEST_PRECISION)
    right_im = jnp.einsum('...jk,kl->...jl', left_re, table_im, precision=HIGHEST_PRECISION) + jnp.einsum('...jk,kl->...jl', left_im, table_re, precision=HIGHEST_PRECISION)
    return (right_re, right_im)

def slot_terms(sample_inphase, sample_quadrature, beam_inphase, beam_quadrature, intensity, corners, weight, table_re, table_im):
    width = beam_inphase.shape[-1]

    def extract(source, corner):
        return lax.dynamic_slice(source, (corner[0], corner[1]), (width, width))
    patch_re = jax.vmap(extract, (None, 0))(sample_inphase, corners)
    patch_im = jax.vmap(extract, (None, 0))(sample_quadrature, corners)
    exit_re = beam_inphase[None] * patch_re[:, None] - beam_quadrature[None] * patch_im[:, None]
    exit_im = beam_inphase[None] * patch_im[:, None] + beam_quadrature[None] * patch_re[:, None]
    far_re, far_im = two_sided(exit_re, exit_im, table_re, table_im)
    power = lax.optimization_barrier(jnp.sum(far_re * far_re + far_im * far_im, axis=1))
    factor = (1.0 - jnp.sqrt(intensity) / jnp.sqrt(jnp.maximum(power, FLOOR_POWER))) * weight[:, None, None]
    back_re, back_im = two_sided(far_re * factor[:, None], far_im * factor[:, None], table_re, -table_im)
    terms_re = lax.optimization_barrier(jnp.sum(beam_inphase[None] * back_re + beam_quadrature[None] * back_im, axis=1))
    terms_im = lax.optimization_barrier(jnp.sum(beam_inphase[None] * back_im - beam_quadrature[None] * back_re, axis=1))
    return (terms_re, terms_im)

def deposit(field, patch, corner):
    width = patch.shape[0]
    current = lax.dynamic_slice(field, (corner[0], corner[1]), (width, width))
    return lax.dynamic_update_slice(field, current + patch, (corner[0], corner[1]))

def reference(sample_inphase, sample_quadrature, beam_inphase, beam_quadrature, recorded_diffraction, window_corners, filled_tallies, absorption_templates):
    table_re, table_im = dft_tables(WINDOW_SPAN)

    def lone_wavelength(items):
        o_re, o_im, p_re, p_im, intensity_all, corner_all, tile_counts = items
        live = jnp.arange(RASTER_SPOTS, dtype=jnp.int32)[None, :] < tile_counts[:, None]
        weight = live.astype(jnp.float32).reshape(-1)
        intensity = intensity_all.reshape(N_TA * RASTER_SPOTS, WINDOW_SPAN, WINDOW_SPAN)
        corners = corner_all.reshape(N_TA * RASTER_SPOTS, 2)
        terms_re, terms_im = slot_terms(o_re, o_im, p_re, p_im, intensity, corners, weight, table_re, table_im)
        light_patch = lax.optimization_barrier(jnp.sum(p_re * p_re + p_im * p_im, axis=0))

        def add_one(index, carry):
            grad_re, grad_im, light = carry
            corner = corners[index]
            return (deposit(grad_re, terms_re[index], corner), deposit(grad_im, terms_im[index], corner), deposit(light, light_patch * weight[index], corner))
        zeros = jnp.zeros((OBJ, OBJ), jnp.float32)
        grad_re, grad_im, light = lax.fori_loop(0, N_TA * RASTER_SPOTS, add_one, (zeros, zeros, zeros))
        return (o_re - grad_re / (light + REGULARIZER), o_im - grad_im / (light + REGULARIZER))
    revised_inphase, revised_quadrature = lax.map(lone_wavelength, (sample_inphase, sample_quadrature, beam_inphase, beam_quadrature, recorded_diffraction, window_corners, filled_tallies))
    spectra = jnp.stack([revised_inphase.reshape(BEAM_QUANTA, OBJ * OBJ), revised_quadrature.reshape(BEAM_QUANTA, OBJ * OBJ)])
    gram = jnp.dot(absorption_templates, absorption_templates.T, precision=HIGHEST_PRECISION)
    project = jnp.linalg.solve(gram, absorption_templates)
    coefficients = jnp.einsum('ke,cep->ckp', project, spectra, precision=HIGHEST_PRECISION)
    fitted = jnp.einsum('ke,ckp->cep', absorption_templates, coefficients, precision=HIGHEST_PRECISION)
    return (fitted.reshape(2, BEAM_QUANTA, N_EA, N_TA, PIX), coefficients)
```

```python
import functools

import jax
import jax.numpy as jnp
import numpy as np
from jax import lax
from jax.experimental import pallas as pl
from jax.experimental.pallas import tpu as pltpu
from jax.sharding import PartitionSpec as P

HIGHEST = lax.Precision.HIGHEST
FLOOR_POWER = 0.5
REGULARIZER = 1.0
LANES = 128
SUBS = 8


def split_bf16(x):
    hi = x.astype(jnp.bfloat16)
    lo = (x - hi.astype(jnp.float32)).astype(jnp.bfloat16)
    return hi, lo


def transform_tables(width):
    fold = LANES // width
    i = np.arange(LANES) // width
    k = np.arange(LANES) % width
    phase = np.outer(i, i) / fold + np.outer(k, k) / width
    m = np.exp(-2j * np.pi * phase) / width
    real = np.block([[m.real, m.imag], [-m.imag, m.real]])
    q = np.arange(SUBS)
    tw = np.exp(-2j * np.pi * np.outer(q, i) / width)
    tw = np.concatenate([tw.real, tw.imag]).astype(np.float32)

    def halves(a):
        hi = a.astype(jnp.bfloat16)
        lo = (a - hi.astype(np.float64)).astype(jnp.bfloat16)
        return np.stack([hi, lo])

    return halves(real), halves(real.T.copy()), tw


def fft8(re, im, sign):
    def butterfly(a, b):
        return (a[0] + b[0], a[1] + b[1]), (a[0] - b[0], a[1] - b[1])

    def turn(a):
        return (-a[1], a[0]) if sign > 0 else (a[1], -a[0])

    h = np.float32(np.sqrt(0.5))

    def eighth(a):
        if sign > 0:
            return ((a[0] - a[1]) * h, (a[0] + a[1]) * h)
        return ((a[0] + a[1]) * h, (a[1] - a[0]) * h)

    def fft4(x):
        s0, d0 = butterfly(x[0], x[2])
        s1, d1 = butterfly(x[1], x[3])
        d1 = turn(d1)
        y0, y2 = butterfly(s0, s1)
        y1, y3 = butterfly(d0, d1)
        return [y0, y1, y2, y3]

    x = list(zip(re, im))
    e = fft4(x[0::2])
    o = fft4(x[1::2])
    o = [o[0], eighth(o[1]), turn(o[2]), turn(eighth(o[3]))]
    pairs = [butterfly(e[n], o[n]) for n in range(4)]
    out = [p[0] for p in pairs] + [p[1] for p in pairs]
    return [y[0] for y in out], [y[1] for y in out]


def step_kernel(
    n_e, spots, used, modes, width,
    first_ref, own_corner, par_corner, own_count,
    re0, re1, im0, im1, pr_ref, pi_ref, own_rec, par_rec, wf_ref, wb_ref, tw_ref,
    out_ref,
    rec, patch_re, patch_im, root, work, acc, light_row, sem,
):
    fold = LANES // width
    groups = used // SUBS
    per_group = modes * SUBS
    rows = groups * per_group
    first = first_ref[0]
    copies = [
        pltpu.make_async_copy(own_rec.at[pl.ds(first, n_e)], rec.at[:, pl.ds(0, spots)], sem.at[0]),
        pltpu.make_async_copy(par_rec, rec.at[:, pl.ds(spots, spots)], sem.at[1]),
    ]
    for c in copies:
        c.start()
    lane = lax.broadcasted_iota(jnp.int32, (SUBS, LANES), 1)
    block = lane // width
    acc[...] = jnp.zeros_like(acc)

    def place(e, index):
        count = own_count[first + e]
        mine = index < count
        slot = jnp.where(mine, index, index - count)
        slot = jnp.clip(slot, 0, spots - 1)
        at = ((first + e) * spots + slot) * 2
        row = jnp.where(mine, own_corner[at], par_corner[at])
        col = jnp.where(mine, own_corner[at + 1], par_corner[at + 1])
        return jnp.where(mine, slot, slot + spots), row, col

    def merge(parts):
        out = parts[0]
        for n in range(1, fold):
            out = jnp.where(block == n, parts[n], out)
        return out

    def extract(n, carry):
        e, g = n // groups, n % groups
        for s in range(SUBS):
            _, row, col = place(e, g * SUBS + s)
            low = lane >= col
            to = pl.multiple_of((n * SUBS + s) * SUBS, SUBS)
            for left, right, dst in ((re0, re1, patch_re), (im0, im1, patch_im)):
                parts = []
                for i in range(fold):
                    at = pl.ds(row + i, SUBS, stride=fold)
                    v = jnp.where(low, left[e, at, :], right[e, at, :])
                    parts.append(pltpu.roll(v, (i * width - col) & (LANES - 1), 1))
                dst[pl.ds(to, SUBS), :] = merge(parts)
        return carry

    lax.fori_loop(0, n_e * groups, extract, 0)
    for c in copies:
        c.wait()

    def roots(n, carry):
        e, g = n // groups, n % groups
        for s in range(SUBS):
            slot, _, _ = place(e, g * SUBS + s)
            to = pl.multiple_of((n * SUBS + s) * SUBS, SUBS)
            v = jnp.concatenate(
                [rec[e, slot, r * SUBS:(r + 1) * SUBS, :] for r in range(fold)], axis=1
            )
            root[pl.ds(to, SUBS), :] = jnp.sqrt(v)
        return carry

    lax.fori_loop(0, n_e * groups, roots, 0)

    def row_of(ref, *index):
        return jnp.broadcast_to(ref[index], (SUBS, LANES))

    def multiply(w_ref):
        for q in range(SUBS):
            hi, lo = split_bf16(work[q])
            dot = functools.partial(jnp.dot, preferred_element_type=jnp.float32)
            work[q] = dot(hi, w_ref[0]) + dot(lo, w_ref[0]) + dot(hi, w_ref[1])

    def energy(e, carry):
        def forward(g, carry):
            base = (e * groups + g) * SUBS * SUBS
            o_re, o_im = [], []
            for t in range(SUBS):
                at = pl.ds(base + t, SUBS, stride=SUBS)
                o_re.append(patch_re[at, :])
                o_im.append(patch_im[at, :])
            for m in range(modes):
                x_re, x_im = [], []
                for t in range(SUBS):
                    p_re = row_of(pr_ref, e, m, pl.ds(t, 1), slice(None))
                    p_im = row_of(pi_ref, e, m, pl.ds(t, 1), slice(None))
                    x_re.append(p_re * o_re[t] - p_im * o_im[t])
                    x_im.append(p_re * o_im[t] + p_im * o_re[t])
                y_re, y_im = fft8(x_re, x_im, -1)
                to = pl.ds(pl.multiple_of(g * per_group + m * SUBS, SUBS), SUBS)
                for q in range(SUBS):
                    a, b = y_re[q], y_im[q]
                    if q:
                        c = row_of(tw_ref, pl.ds(q, 1), slice(None))
                        d = row_of(tw_ref, pl.ds(SUBS + q, 1), slice(None))
                        a, b = a * c - b * d, a * d + b * c
                    work[q, to, 0:LANES] = a
                    work[q, to, LANES:2 * LANES] = b
            return carry

        lax.fori_loop(0, groups, forward, 0)
        multiply(wf_ref)

        def scale(g, carry):
            base = (e * groups + g) * SUBS * SUBS
            for q in range(SUBS):
                tos = [
                    pl.ds(pl.multiple_of(g * per_group + m * SUBS, SUBS), SUBS)
                    for m in range(modes)
                ]
                f = [(work[q, to, 0:LANES], work[q, to, LANES:2 * LANES]) for to in tos]
                power = f[0][0] * f[0][0] + f[0][1] * f[0][1]
                for a, b in f[1:]:
                    power = power + a * a + b * b
                sq = root[pl.ds(base + q, SUBS, stride=SUBS), :]
                factor = 1.0 - sq * lax.rsqrt(jnp.maximum(power, FLOOR_POWER))
                for to, (a, b) in zip(tos, f):
                    work[q, to, 0:LANES] = a * factor
                    work[q, to, LANES:2 * LANES] = b * factor
            return carry

        lax.fori_loop(0, groups, scale, 0)
        multiply(wb_ref)

        light = jnp.zeros((SUBS, LANES), jnp.float32)
        for m in range(modes):
            a, b = pr_ref[e, m], pi_ref[e, m]
            light = light + a * a + b * b

        def backward(g, carry):
            base = (e * groups + g) * SUBS * SUBS
            t_re = [None] * SUBS
            t_im = [None] * SUBS
            for m in range(modes):
                frm = pl.ds(pl.multiple_of(g * per_group + m * SUBS, SUBS), SUBS)
                x_re, x_im = [], []
                for q in range(SUBS):
                    a, b = work[q, frm, 0:LANES], work[q, frm, LANES:2 * LANES]
                    if q:
                        c = row_of(tw_ref, pl.ds(q, 1), slice(None))
                        d = row_of(tw_ref, pl.ds(SUBS + q, 1), slice(None))
                        a, b = a * c + b * d, b * c - a * d
                    x_re.append(a)
                    x_im.append(b)
                y_re, y_im = fft8(x_re, x_im, 1)
                for t in range(SUBS):
                    p_re = row_of(pr_ref, e, m, pl.ds(t, 1), slice(None))
                    p_im = row_of(pi_ref, e, m, pl.ds(t, 1), slice(None))
                    a = p_re * y_re[t] + p_im * y_im[t]
                    b = p_re * y_im[t] - p_im * y_re[t]
                    t_re[t] = a if m == 0 else t_re[t] + a
                    t_im[t] = b if m == 0 else t_im[t] + b
            for t in range(SUBS):
                at = pl.ds(base + t, SUBS, stride=SUBS)
                patch_re[at, :] = t_re[t]
                patch_im[at, :] = t_im[t]
            for s in range(SUBS):
                _, row, col = place(e, g * SUBS + s)
                frm = pl.ds(pl.multiple_of(base + s * SUBS, SUBS), SUBS)
                terms = (patch_re[frm, :], patch_im[frm, :], light)
                away = [lane + h * LANES - col for h in range(2)]
                inside = [(a >= 0) & (a < width) for a in away]
                for i in range(fold):
                    at = pl.ds(row + i, SUBS, stride=fold)
                    for n, term in enumerate(terms):
                        v = pltpu.roll(term, (col - i * width) & (LANES - 1), 1)
                        for h in range(2):
                            acc[n, h, e, at, :] = acc[n, h, e, at, :] + jnp.where(inside[h], v, 0.0)
            return carry

        lax.fori_loop(0, groups, backward, 0)
        return carry

    lax.fori_loop(0, n_e, energy, 0)

    side = re0.shape[1]

    def finish(n, carry):
        at = pl.ds(pl.multiple_of(n * SUBS, SUBS), SUBS)
        for e in range(n_e):
            for h, (o_re, o_im) in enumerate(((re0, im0), (re1, im1))):
                cols = slice(h * LANES, (h + 1) * LANES)
                share = 1.0 / (acc[2, h, e, at, :] + REGULARIZER)
                out_ref[n, 0, e, :, cols] = o_re[e, at, :] - acc[0, h, e, at, :] * share
                out_ref[n, 1, e, :, cols] = o_im[e, at, :] - acc[1, h, e, at, :] * share
        return carry

    lax.fori_loop(0, side // SUBS, finish, 0)


def gradient_step(objects, beams, own_rec, par_rec, own_corner, par_corner, own_count, first, n_e, used):
    o_re, o_im = objects
    local, side, _ = o_re.shape
    modes, width = beams[0].shape[1], beams[0].shape[-1]
    spots = own_rec.shape[1]
    flat = width * width // LANES
    assert flat == SUBS and side == 2 * LANES and used % SUBS == 0
    wf, wb, tw = transform_tables(width)
    shaped = [b.reshape(local, modes, flat, LANES) for b in beams]
    part = lambda i, f, *_: (f[0] // n_e, 0, 0, 0)
    half = [pl.BlockSpec((n_e, side, LANES), lambda i, f, *_, h=h: (f[0] // n_e, 0, h)) for h in range(2)]
    beam_spec = pl.BlockSpec((n_e, modes, flat, LANES), part)
    whole = pl.BlockSpec(memory_space=pltpu.VMEM)
    rows = used * modes
    n = n_e * used * SUBS
    return pl.pallas_call(
        functools.partial(step_kernel, n_e, spots, used, modes, width),
        out_shape=jax.ShapeDtypeStruct((side // SUBS, 2, n_e, SUBS, side), jnp.float32),
        grid_spec=pltpu.PrefetchScalarGridSpec(
            num_scalar_prefetch=4,
            grid=(1,),
            in_specs=[
                half[0], half[1], half[0], half[1], beam_spec, beam_spec,
                pl.BlockSpec(memory_space=pl.ANY), pl.BlockSpec(memory_space=pl.ANY),
                whole, whole, whole,
            ],
            out_specs=pl.BlockSpec(
                (side // SUBS, 2, n_e, SUBS, side), lambda i, *_: (0, 0, 0, 0, 0)
            ),
            scratch_shapes=[
                pltpu.VMEM((n_e, 2 * spots, width, width), jnp.float32),
                pltpu.VMEM((n, LANES), jnp.float32),
                pltpu.VMEM((n, LANES), jnp.float32),
                pltpu.VMEM((n, LANES), jnp.float32),
                pltpu.VMEM((SUBS, rows, 2 * LANES), jnp.float32),
                pltpu.VMEM((3, 2, n_e, side, LANES), jnp.float32),
                pltpu.VMEM((SUBS, LANES), jnp.float32),
                pltpu.SemaphoreType.DMA((2,)),
            ],
        ),
        name="gradient_step",
    )(
        first, own_corner, par_corner, own_count,
        o_re, o_re, o_im, o_im, *shaped, own_rec, par_rec, jnp.asarray(wf), jnp.asarray(wb), jnp.asarray(tw),
    )


def local(
    sample_inphase,
    sample_quadrature,
    beam_inphase,
    beam_quadrature,
    recorded_diffraction,
    window_corners,
    filled_tallies,
    absorption_templates,
):
    local_energies = sample_inphase.shape[0]
    side = sample_inphase.shape[1]
    spots = recorded_diffraction.shape[2]
    blocks = lax.axis_size("ea")
    tiles = lax.axis_size("ta")
    tile = lax.axis_index("ta")
    swap = [(0, 1), (1, 0)]
    assert tiles == 2
    used = spots * 3 // 2
    divided = local_energies % tiles == 0
    n_e = local_energies // tiles if divided else local_energies
    own_rec = recorded_diffraction[:, 0]
    first = tile * n_e if divided else jnp.zeros((), jnp.int32)
    give = lax.dynamic_slice_in_dim(own_rec, (1 - tile) * n_e, n_e, 0) if divided else own_rec
    par_rec = lax.ppermute(give, "ta", swap)
    own_corner = window_corners.reshape(-1)
    par_corner = lax.ppermute(own_corner, "ta", swap)
    stepped = gradient_step(
        (sample_inphase, sample_quadrature),
        (beam_inphase, beam_quadrature),
        own_rec,
        par_rec,
        own_corner,
        par_corner,
        filled_tallies.reshape(-1),
        first.astype(jnp.int32)[None],
        n_e,
        used,
    )
    gram = jnp.dot(absorption_templates, absorption_templates.T, precision=HIGHEST)
    factor_low = jnp.linalg.cholesky(gram)
    project = jax.scipy.linalg.cho_solve((factor_low, True), absorption_templates)
    edges = project.shape[0]
    pix = side * side // (blocks * tiles)
    if divided and pix == SUBS * side:
        got = lax.all_to_all(stepped, ("ea", "ta"), 0, 0, tiled=True)
        got = got.reshape(blocks * tiles, 2, n_e, pix)
        values = jnp.moveaxis(got, 1, 0).reshape(2, -1, pix)
    else:
        if divided:
            parts = blocks * tiles
            flat = jnp.moveaxis(stepped, 0, 2).reshape(2, n_e, parts, pix)
            got = lax.all_to_all(flat, ("ea", "ta"), 2, 1, tiled=True)
        else:
            flat = jnp.moveaxis(stepped, 0, 2).reshape(2, n_e, blocks, tiles, pix)
            flat = lax.dynamic_index_in_dim(flat, tile, 3, keepdims=False)
            got = lax.all_to_all(flat, "ea", 2, 1, tiled=True)
        values = got.reshape(2, -1, pix)
    coefs = jnp.einsum("ke,cen->ckn", project, values, precision=HIGHEST)
    fitted_here = jnp.einsum("ke,ckn->cen", absorption_templates, coefs, precision=HIGHEST)
    returned = lax.all_to_all(
        fitted_here[:, :, None, :], "ea", split_axis=1, concat_axis=2, tiled=True
    )
    return (returned[:, :, :, None, :], coefs)


def solution(mesh):
    in_specs = (
        P("ea", None, None),
        P("ea", None, None),
        P("ea", None, None, None),
        P("ea", None, None, None),
        P("ea", "ta", None, None, None),
        P("ea", "ta", None, None),
        P("ea", "ta"),
        P(),
    )
    out_specs = (P(None, "ea", None, "ta", None), P(None, None, ("ea", "ta")))
    return jax.shard_map(local, mesh=mesh, in_specs=in_specs, out_specs=out_specs, check_vma=False)
```

```python
import functools

import jax
import jax.numpy as jnp
import numpy as np
from jax import lax
from jax.experimental import pallas as pl
from jax.experimental.pallas import tpu as pltpu
from jax.sharding import Mesh
from jax.sharding import PartitionSpec as P

HIGHEST = lax.Precision.HIGHEST
FLOOR_POWER = 0.5
REGULARIZER = 1.0
LANES = 128
SUBS = 8


def split_bf16(x):
    hi = x.astype(jnp.bfloat16)
    lo = (x - hi.astype(jnp.float32)).astype(jnp.bfloat16)
    return hi, lo


def transform_tables(width):
    fold = LANES // width
    i = np.arange(LANES) // width
    k = np.arange(LANES) % width
    phase = np.outer(i, i) / fold + np.outer(k, k) / width
    m = np.exp(-2j * np.pi * phase) / width
    real = np.block([[m.real, m.imag], [-m.imag, m.real]])
    q = np.arange(SUBS)
    tw = np.exp(-2j * np.pi * np.outer(q, i) / width)
    tw = np.concatenate([tw.real, tw.imag]).astype(np.float32)

    def halves(a):
        hi = a.astype(jnp.bfloat16)
        lo = (a - hi.astype(np.float64)).astype(jnp.bfloat16)
        return np.stack([hi, lo])

    return halves(real), halves(real.T.copy()), tw


def fft8(re, im, sign):
    def butterfly(a, b):
        return (a[0] + b[0], a[1] + b[1]), (a[0] - b[0], a[1] - b[1])

    def turn(a):
        return (-a[1], a[0]) if sign > 0 else (a[1], -a[0])

    h = np.float32(np.sqrt(0.5))

    def eighth(a):
        if sign > 0:
            return ((a[0] - a[1]) * h, (a[0] + a[1]) * h)
        return ((a[0] + a[1]) * h, (a[1] - a[0]) * h)

    def fft4(x):
        s0, d0 = butterfly(x[0], x[2])
        s1, d1 = butterfly(x[1], x[3])
        d1 = turn(d1)
        y0, y2 = butterfly(s0, s1)
        y1, y3 = butterfly(d0, d1)
        return [y0, y1, y2, y3]

    x = list(zip(re, im))
    e = fft4(x[0::2])
    o = fft4(x[1::2])
    o = [o[0], eighth(o[1]), turn(o[2]), turn(eighth(o[3]))]
    pairs = [butterfly(e[n], o[n]) for n in range(4)]
    out = [p[0] for p in pairs] + [p[1] for p in pairs]
    return [y[0] for y in out], [y[1] for y in out]


def step_kernel(
    n_e, spots, used, modes, width,
    first_ref, own_corner, par_corner, own_count,
    re0, re1, im0, im1, pr_ref, pi_ref, own_rec, par_rec, wf_ref, wb_ref, tw_ref,
    out_re, out_im,
    rec, patch_re, patch_im, root, work, acc, light_row, sem,
):
    fold = LANES // width
    groups = used // SUBS
    per_group = modes * SUBS
    rows = groups * per_group
    first = first_ref[0]
    copies = [
        pltpu.make_async_copy(own_rec.at[pl.ds(first, n_e)], rec.at[:, pl.ds(0, spots)], sem.at[0]),
        pltpu.make_async_copy(par_rec, rec.at[:, pl.ds(spots, spots)], sem.at[1]),
    ]
    for c in copies:
        c.start()
    lane = lax.broadcasted_iota(jnp.int32, (SUBS, LANES), 1)
    block = lane // width
    acc[...] = jnp.zeros_like(acc)

    def place(e, index):
        count = own_count[first + e]
        mine = index < count
        slot = jnp.where(mine, index, index - count)
        slot = jnp.clip(slot, 0, spots - 1)
        at = ((first + e) * spots + slot) * 2
        row = jnp.where(mine, own_corner[at], par_corner[at])
        col = jnp.where(mine, own_corner[at + 1], par_corner[at + 1])
        return jnp.where(mine, slot, slot + spots), row, col

    def merge(parts):
        out = parts[0]
        for n in range(1, fold):
            out = jnp.where(block == n, parts[n], out)
        return out

    def extract(n, carry):
        e, g = n // groups, n % groups
        for s in range(SUBS):
            _, row, col = place(e, g * SUBS + s)
            low = lane >= col
            to = pl.multiple_of((n * SUBS + s) * SUBS, SUBS)
            for left, right, dst in ((re0, re1, patch_re), (im0, im1, patch_im)):
                parts = []
                for i in range(fold):
                    at = pl.ds(row + i, SUBS, stride=fold)
                    v = jnp.where(low, left[e, at, :], right[e, at, :])
                    parts.append(pltpu.roll(v, (i * width - col) & (LANES - 1), 1))
                dst[pl.ds(to, SUBS), :] = merge(parts)
        return carry

    lax.fori_loop(0, n_e * groups, extract, 0)
    for c in copies:
        c.wait()

    def roots(n, carry):
        e, g = n // groups, n % groups
        for s in range(SUBS):
            slot, _, _ = place(e, g * SUBS + s)
            to = pl.multiple_of((n * SUBS + s) * SUBS, SUBS)
            v = jnp.concatenate(
                [rec[e, slot, r * SUBS:(r + 1) * SUBS, :] for r in range(fold)], axis=1
            )
            root[pl.ds(to, SUBS), :] = jnp.sqrt(v)
        return carry

    lax.fori_loop(0, n_e * groups, roots, 0)

    def row_of(ref, *index):
        return jnp.broadcast_to(ref[index], (SUBS, LANES))

    def multiply(w_ref):
        for q in range(SUBS):
            hi, lo = split_bf16(work[q])
            dot = functools.partial(jnp.dot, preferred_element_type=jnp.float32)
            work[q] = dot(hi, w_ref[0]) + dot(lo, w_ref[0]) + dot(hi, w_ref[1])

    def energy(e, carry):
        def forward(g, carry):
            base = (e * groups + g) * SUBS * SUBS
            o_re, o_im = [], []
            for t in range(SUBS):
                at = pl.ds(base + t, SUBS, stride=SUBS)
                o_re.append(patch_re[at, :])
                o_im.append(patch_im[at, :])
            for m in range(modes):
                x_re, x_im = [], []
                for t in range(SUBS):
                    p_re = row_of(pr_ref, e, m, pl.ds(t, 1), slice(None))
                    p_im = row_of(pi_ref, e, m, pl.ds(t, 1), slice(None))
                    x_re.append(p_re * o_re[t] - p_im * o_im[t])
                    x_im.append(p_re * o_im[t] + p_im * o_re[t])
                y_re, y_im = fft8(x_re, x_im, -1)
                to = pl.ds(pl.multiple_of(g * per_group + m * SUBS, SUBS), SUBS)
                for q in range(SUBS):
                    a, b = y_re[q], y_im[q]
                    if q:
                        c = row_of(tw_ref, pl.ds(q, 1), slice(None))
                        d = row_of(tw_ref, pl.ds(SUBS + q, 1), slice(None))
                        a, b = a * c - b * d, a * d + b * c
                    work[q, to, 0:LANES] = a
                    work[q, to, LANES:2 * LANES] = b
            return carry

        lax.fori_loop(0, groups, forward, 0)
        multiply(wf_ref)

        def scale(g, carry):
            base = (e * groups + g) * SUBS * SUBS
            for q in range(SUBS):
                tos = [
                    pl.ds(pl.multiple_of(g * per_group + m * SUBS, SUBS), SUBS)
                    for m in range(modes)
                ]
                f = [(work[q, to, 0:LANES], work[q, to, LANES:2 * LANES]) for to in tos]
                power = f[0][0] * f[0][0] + f[0][1] * f[0][1]
                for a, b in f[1:]:
                    power = power + a * a + b * b
                sq = root[pl.ds(base + q, SUBS, stride=SUBS), :]
                factor = 1.0 - sq * lax.rsqrt(jnp.maximum(power, FLOOR_POWER))
                for to, (a, b) in zip(tos, f):
                    work[q, to, 0:LANES] = a * factor
                    work[q, to, LANES:2 * LANES] = b * factor
            return carry

        lax.fori_loop(0, groups, scale, 0)
        multiply(wb_ref)

        light = jnp.zeros((SUBS, LANES), jnp.float32)
        for m in range(modes):
            a, b = pr_ref[e, m], pi_ref[e, m]
            light = light + a * a + b * b

        def backward(g, carry):
            base = (e * groups + g) * SUBS * SUBS
            t_re = [None] * SUBS
            t_im = [None] * SUBS
            for m in range(modes):
                frm = pl.ds(pl.multiple_of(g * per_group + m * SUBS, SUBS), SUBS)
                x_re, x_im = [], []
                for q in range(SUBS):
                    a, b = work[q, frm, 0:LANES], work[q, frm, LANES:2 * LANES]
                    if q:
                        c = row_of(tw_ref, pl.ds(q, 1), slice(None))
                        d = row_of(tw_ref, pl.ds(SUBS + q, 1), slice(None))
                        a, b = a * c + b * d, b * c - a * d
                    x_re.append(a)
                    x_im.append(b)
                y_re, y_im = fft8(x_re, x_im, 1)
                for t in range(SUBS):
                    p_re = row_of(pr_ref, e, m, pl.ds(t, 1), slice(None))
                    p_im = row_of(pi_ref, e, m, pl.ds(t, 1), slice(None))
                    a = p_re * y_re[t] + p_im * y_im[t]
                    b = p_re * y_im[t] - p_im * y_re[t]
                    t_re[t] = a if m == 0 else t_re[t] + a
                    t_im[t] = b if m == 0 else t_im[t] + b
            for t in range(SUBS):
                at = pl.ds(base + t, SUBS, stride=SUBS)
                patch_re[at, :] = t_re[t]
                patch_im[at, :] = t_im[t]
            for s in range(SUBS):
                _, row, col = place(e, g * SUBS + s)
                frm = pl.ds(pl.multiple_of(base + s * SUBS, SUBS), SUBS)
                terms = (patch_re[frm, :], patch_im[frm, :], light)
                away = [lane + h * LANES - col for h in range(2)]
                inside = [(a >= 0) & (a < width) for a in away]
                for i in range(fold):
                    at = pl.ds(row + i, SUBS, stride=fold)
                    for n, term in enumerate(terms):
                        v = pltpu.roll(term, (col - i * width) & (LANES - 1), 1)
                        for h in range(2):
                            acc[n, h, e, at, :] = acc[n, h, e, at, :] + jnp.where(inside[h], v, 0.0)
            return carry

        lax.fori_loop(0, groups, backward, 0)
        return carry

    lax.fori_loop(0, n_e, energy, 0)

    side = re0.shape[1]

    dests = out_re.shape[0]

    def finish(n, carry):
        at = pl.ds(pl.multiple_of(n * SUBS, SUBS), SUBS)
        dest, far = n % dests, n // dests
        for e in range(n_e):
            for h, (o_re, o_im) in enumerate(((re0, im0), (re1, im1))):
                share = 1.0 / (acc[2, h, e, at, :] + REGULARIZER)
                out_re[dest, e, far, h] = o_re[e, at, :] - acc[0, h, e, at, :] * share
                out_im[dest, e, far, h] = o_im[e, at, :] - acc[1, h, e, at, :] * share
        return carry

    lax.fori_loop(0, side // SUBS, finish, 0)


def gradient_step(objects, beams, own_rec, par_rec, own_corner, par_corner, own_count, first, n_e, used, fars):
    o_re, o_im = objects
    local, side, _ = o_re.shape
    modes, width = beams[0].shape[1], beams[0].shape[-1]
    spots = own_rec.shape[1]
    flat = width * width // LANES
    assert flat == SUBS and side == 2 * LANES and used % SUBS == 0
    wf, wb, tw = transform_tables(width)
    shaped = [b.reshape(local, modes, flat, LANES) for b in beams]
    part = lambda i, f, *_: (f[0] // n_e, 0, 0, 0)
    half = [pl.BlockSpec((n_e, side, LANES), lambda i, f, *_, h=h: (f[0] // n_e, 0, h)) for h in range(2)]
    beam_spec = pl.BlockSpec((n_e, modes, flat, LANES), part)
    whole = pl.BlockSpec(memory_space=pltpu.VMEM)
    rows = used * modes
    n = n_e * used * SUBS
    out_shape = (side // SUBS // fars, n_e, fars, side // LANES, SUBS, LANES)
    return pl.pallas_call(
        functools.partial(step_kernel, n_e, spots, used, modes, width),
        out_shape=[jax.ShapeDtypeStruct(out_shape, jnp.float32)] * 2,
        grid_spec=pltpu.PrefetchScalarGridSpec(
            num_scalar_prefetch=4,
            grid=(1,),
            in_specs=[
                half[0], half[1], half[0], half[1], beam_spec, beam_spec,
                pl.BlockSpec(memory_space=pl.ANY), pl.BlockSpec(memory_space=pl.ANY),
                whole, whole, whole,
            ],
            out_specs=[pl.BlockSpec(out_shape, lambda i, *_: (0,) * len(out_shape))] * 2,
            scratch_shapes=[
                pltpu.VMEM((n_e, 2 * spots, width, width), jnp.float32),
                pltpu.VMEM((n, LANES), jnp.float32),
                pltpu.VMEM((n, LANES), jnp.float32),
                pltpu.VMEM((n, LANES), jnp.float32),
                pltpu.VMEM((SUBS, rows, 2 * LANES), jnp.float32),
                pltpu.VMEM((3, 2, n_e, side, LANES), jnp.float32),
                pltpu.VMEM((SUBS, LANES), jnp.float32),
                pltpu.SemaphoreType.DMA((2,)),
            ],
        ),
        name="gradient_step",
    )(
        first, own_corner, par_corner, own_count,
        o_re, o_re, o_im, o_im, *shaped, own_rec, par_rec, jnp.asarray(wf), jnp.asarray(wb), jnp.asarray(tw),
    )


def dot3(a, b):
    ah, al = split_bf16(a)
    bh, bl = split_bf16(b)
    left = jnp.concatenate([ah, al, ah], axis=1)
    right = jnp.concatenate([bh, bh, bl], axis=0)
    return jnp.dot(left, right, preferred_element_type=jnp.float32)


def project_kernel(fars, halves, project_ref, got_ref, out_ref):
    energies = project_ref.shape[1]
    stride = got_ref.shape[0] // energies
    for f in range(fars):
        for r in range(SUBS):
            parts = [
                got_ref[pl.ds((f * halves + h) * SUBS + r, energies, stride=stride), :]
                for h in range(halves)
            ]
            at = (f * SUBS + r) * halves * LANES
            values = jnp.concatenate(parts, axis=1)
            out_ref[:, at:at + halves * LANES] = dot3(project_ref[...], values)


def partial_coefs(project, got, fars, halves):
    rows = got.shape[0]
    edges, energies = project.shape
    pixels = rows // energies * LANES
    return pl.pallas_call(
        functools.partial(project_kernel, fars, halves),
        out_shape=jax.ShapeDtypeStruct((edges, pixels), jnp.float32),
        cost_estimate=pl.CostEstimate(
            flops=6 * edges * energies * pixels, bytes_accessed=rows * LANES * 4, transcendentals=0
        ),
        name="partial_coefs",
    )(project, got)


def fit_kernel(far_ref, mine_ref, theirs_ref, basis_ref, coef_ref, fit_ref):
    energies = basis_ref.shape[0]
    own = coef_ref.shape[1]
    stride = fit_ref.shape[0] // energies
    at = pl.ds(pl.multiple_of(far_ref[0] * own, own), own)
    coef_ref[...] = mine_ref[:, at] + theirs_ref[:, at]
    wide = 2 * LANES
    for j in range(mine_ref.shape[1] // wide):
        cols = slice(j * wide, (j + 1) * wide)
        values = dot3(basis_ref[...], mine_ref[:, cols] + theirs_ref[:, cols])
        for d in range(energies // SUBS):
            for u in range(2):
                to = pl.ds(d * SUBS * stride + j * 2 + u, SUBS, stride=stride)
                fit_ref[to, :] = values[d * SUBS:(d + 1) * SUBS, u * LANES:(u + 1) * LANES]


def fitted_values(far, mine, theirs, basis, own):
    edges, pixels = mine.shape
    energies = basis.shape[0]
    vmem = pl.BlockSpec(memory_space=pltpu.VMEM)
    return pl.pallas_call(
        fit_kernel,
        out_shape=[
            jax.ShapeDtypeStruct((edges, own), jnp.float32),
            jax.ShapeDtypeStruct((energies * pixels // LANES, LANES), jnp.float32),
        ],
        in_specs=[pl.BlockSpec(memory_space=pltpu.SMEM), vmem, vmem, vmem],
        out_specs=[vmem, vmem],
        cost_estimate=pl.CostEstimate(
            flops=6 * edges * energies * pixels, bytes_accessed=energies * pixels * 4, transcendentals=0
        ),
        name="fitted_values",
    )(far, mine, theirs, basis)


def gather_kernel(in_ref, *refs):
    out_ref = refs[-1]
    for s in range(in_ref.shape[0]):
        out_ref[0, :, :, s] = in_ref[s]


def gather_part(part, got, out):
    senders, energies, fars, subs, _ = got.shape
    step = senders // 2
    shape = (2, energies, fars, senders, subs, LANES)
    return pl.pallas_call(
        gather_kernel,
        out_shape=jax.ShapeDtypeStruct(shape, jnp.float32),
        grid=(2,),
        in_specs=[pl.BlockSpec((step, energies, fars, subs, LANES), lambda i: (i, 0, 0, 0, 0))]
        + ([] if out is None else [pl.BlockSpec(memory_space=pl.ANY)]),
        out_specs=pl.BlockSpec(
            (1, energies, fars, step, subs, LANES), lambda i: (part, 0, 0, i, 0, 0)
        ),
        input_output_aliases={} if out is None else {1: 0},
        name="gather_part",
    )(*([got] if out is None else [got, out]))


def local(
    sample_inphase,
    sample_quadrature,
    beam_inphase,
    beam_quadrature,
    recorded_diffraction,
    window_corners,
    filled_tallies,
    absorption_templates,
):
    local_energies = sample_inphase.shape[0]
    side = sample_inphase.shape[1]
    spots = recorded_diffraction.shape[2]
    fars = lax.axis_size("far")
    cube = lax.axis_size("cube")
    blocks = fars * cube
    tiles = lax.axis_size("ta")
    tile = lax.axis_index("ta")
    swap = [(0, 1), (1, 0)]
    assert tiles == 2 and fars == 2
    used = spots * 3 // 2
    divided = local_energies % tiles == 0
    n_e = local_energies // tiles if divided else local_energies
    pix = side * side // (blocks * tiles)
    two_level = divided and pix == SUBS * side and local_energies == SUBS
    own_rec = recorded_diffraction[:, 0]
    first = tile * n_e if divided else jnp.zeros((), jnp.int32)
    give = lax.dynamic_slice_in_dim(own_rec, (1 - tile) * n_e, n_e, 0) if divided else own_rec
    par_rec = lax.ppermute(give, "ta", swap)
    own_corner = window_corners.reshape(-1)
    par_corner = lax.ppermute(own_corner, "ta", swap)
    stepped = gradient_step(
        (sample_inphase, sample_quadrature),
        (beam_inphase, beam_quadrature),
        own_rec,
        par_rec,
        own_corner,
        par_corner,
        filled_tallies.reshape(-1),
        first.astype(jnp.int32)[None],
        n_e,
        used,
        fars if two_level else 1,
    )
    gram = jnp.dot(absorption_templates, absorption_templates.T, precision=HIGHEST)
    factor_low = jnp.linalg.cholesky(gram)
    project = jax.scipy.linalg.cho_solve((factor_low, True), absorption_templates)
    edges, energies = project.shape

    if two_level:
        far = lax.axis_index("far")
        near = energies // fars
        halves = side // LANES
        project_near = lax.dynamic_slice_in_dim(project, far * near, near, 1)
        basis_near = lax.dynamic_slice_in_dim(absorption_templates, far * near, near, 1).T
        far = far.astype(jnp.int32)[None]
        out, coefs = None, []
        got = [lax.all_to_all(x, ("cube", "ta"), 0, 0, tiled=True) for x in stepped]
        for part in range(2):
            mine = partial_coefs(project_near, got[part].reshape(-1, LANES), fars, halves)
            theirs = lax.ppermute(mine, "far", swap)
            coef, fit = fitted_values(far, mine, theirs, basis_near, pix)
            coefs.append(coef)
            back = lax.all_to_all(
                fit.reshape(cube, local_energies, fars, pix // LANES, LANES), "cube", 0, 0, tiled=True
            )
            out = gather_part(part, back, out)
        return (out.reshape(2, local_energies, blocks, 1, pix), jnp.stack(coefs))

    flat = jnp.stack([x.transpose(1, 0, 2, 4, 3, 5) for x in stepped])
    if divided:
        flat = flat.reshape(2, n_e, blocks * tiles, pix)
        got = lax.all_to_all(flat, ("far", "cube", "ta"), 2, 1, tiled=True)
    else:
        flat = flat.reshape(2, n_e, blocks, tiles, pix)
        flat = lax.dynamic_index_in_dim(flat, tile, 3, keepdims=False)
        got = lax.all_to_all(flat, ("far", "cube"), 2, 1, tiled=True)
    values = got.reshape(2, -1, pix)
    coefs = jnp.einsum("ke,cen->ckn", project, values, precision=HIGHEST)
    fitted_here = jnp.einsum("ke,ckn->cen", absorption_templates, coefs, precision=HIGHEST)
    returned = lax.all_to_all(
        fitted_here[:, :, None, :], ("far", "cube"), split_axis=1, concat_axis=2, tiled=True
    )
    return (returned[:, :, :, None, :], coefs)


def solution(mesh):
    blocks, tiles = mesh.shape["ea"], mesh.shape["ta"]
    mesh = Mesh(mesh.devices.reshape(2, blocks // 2, tiles), ("far", "cube", "ta"))
    ea = ("far", "cube")
    in_specs = (
        P(ea, None, None),
        P(ea, None, None),
        P(ea, None, None, None),
        P(ea, None, None, None),
        P(ea, "ta", None, None, None),
        P(ea, "ta", None, None),
        P(ea, "ta"),
        P(),
    )
    out_specs = (P(None, ea, None, "ta", None), P(None, None, (*ea, "ta")))
    return jax.shard_map(local, mesh=mesh, in_specs=in_specs, out_specs=out_specs, check_vma=False)
```

```python
import functools

import jax
import jax.numpy as jnp
import numpy as np
from jax import lax
from jax.experimental import pallas as pl
from jax.experimental.pallas import tpu as pltpu
from jax.sharding import Mesh
from jax.sharding import PartitionSpec as P

HIGHEST = lax.Precision.HIGHEST
FLOOR_POWER = 0.5
REGULARIZER = 1.0
LANES = 128
SUBS = 8
SMALL = 12 << 20


def split_bf16(x):
    hi = x.astype(jnp.bfloat16)
    lo = (x - hi.astype(jnp.float32)).astype(jnp.bfloat16)
    return hi, lo


def transform_tables(width):
    fold = LANES // width
    i = np.arange(LANES) // width
    k = np.arange(LANES) % width
    phase = np.outer(i, i) / fold + np.outer(k, k) / width
    m = np.exp(-2j * np.pi * phase) / width
    real = np.block([[m.real, m.imag], [-m.imag, m.real]])
    q = np.arange(SUBS)
    tw = np.exp(-2j * np.pi * np.outer(q, i) / width)
    tw = np.concatenate([tw.real, tw.imag]).astype(np.float32)

    def halves(a):
        hi = a.astype(jnp.bfloat16)
        lo = (a - hi.astype(np.float64)).astype(jnp.bfloat16)
        return np.stack([hi, lo])

    return halves(real), halves(real.T.copy()), tw


def fft8(re, im, sign):
    def butterfly(a, b):
        return (a[0] + b[0], a[1] + b[1]), (a[0] - b[0], a[1] - b[1])

    def turn(a):
        return (-a[1], a[0]) if sign > 0 else (a[1], -a[0])

    h = np.float32(np.sqrt(0.5))

    def eighth(a):
        if sign > 0:
            return ((a[0] - a[1]) * h, (a[0] + a[1]) * h)
        return ((a[0] + a[1]) * h, (a[1] - a[0]) * h)

    def fft4(x):
        s0, d0 = butterfly(x[0], x[2])
        s1, d1 = butterfly(x[1], x[3])
        d1 = turn(d1)
        y0, y2 = butterfly(s0, s1)
        y1, y3 = butterfly(d0, d1)
        return [y0, y1, y2, y3]

    x = list(zip(re, im))
    e = fft4(x[0::2])
    o = fft4(x[1::2])
    o = [o[0], eighth(o[1]), turn(o[2]), turn(eighth(o[3]))]
    pairs = [butterfly(e[n], o[n]) for n in range(4)]
    out = [p[0] for p in pairs] + [p[1] for p in pairs]
    return [y[0] for y in out], [y[1] for y in out]


def step_kernel(
    n_e, spots, used, modes, width,
    first_ref, own_corner, par_corner, own_count,
    re0, re1, im0, im1, pr_ref, pi_ref, own_rec, par_rec, wf_ref, wb_ref, tw_ref,
    out_re, out_im,
    rec, patch_re, patch_im, root, work, acc, light_row, sem,
):
    fold = LANES // width
    groups = used // SUBS
    per_group = modes * SUBS
    rows = groups * per_group
    first = first_ref[0]
    copies = [
        pltpu.make_async_copy(own_rec.at[pl.ds(first, n_e)], rec.at[:, pl.ds(0, spots)], sem.at[0]),
        pltpu.make_async_copy(par_rec, rec.at[:, pl.ds(spots, spots)], sem.at[1]),
    ]
    for c in copies:
        c.start()
    lane = lax.broadcasted_iota(jnp.int32, (SUBS, LANES), 1)
    block = lane // width
    acc[...] = jnp.zeros_like(acc)

    def place(e, index):
        count = own_count[first + e]
        mine = index < count
        slot = jnp.where(mine, index, index - count)
        slot = jnp.clip(slot, 0, spots - 1)
        at = ((first + e) * spots + slot) * 2
        row = jnp.where(mine, own_corner[at], par_corner[at])
        col = jnp.where(mine, own_corner[at + 1], par_corner[at + 1])
        return jnp.where(mine, slot, slot + spots), row, col

    def merge(parts):
        out = parts[0]
        for n in range(1, fold):
            out = jnp.where(block == n, parts[n], out)
        return out

    def extract(n, carry):
        e, g = n // groups, n % groups
        for s in range(SUBS):
            _, row, col = place(e, g * SUBS + s)
            low = lane >= col
            to = pl.multiple_of((n * SUBS + s) * SUBS, SUBS)
            for left, right, dst in ((re0, re1, patch_re), (im0, im1, patch_im)):
                parts = []
                for i in range(fold):
                    at = pl.ds(row + i, SUBS, stride=fold)
                    v = jnp.where(low, left[e, at, :], right[e, at, :])
                    parts.append(pltpu.roll(v, (i * width - col) & (LANES - 1), 1))
                dst[pl.ds(to, SUBS), :] = merge(parts)
        return carry

    lax.fori_loop(0, n_e * groups, extract, 0)
    for c in copies:
        c.wait()

    def roots(n, carry):
        e, g = n // groups, n % groups
        for s in range(SUBS):
            slot, _, _ = place(e, g * SUBS + s)
            to = pl.multiple_of((n * SUBS + s) * SUBS, SUBS)
            v = jnp.concatenate(
                [rec[e, slot, r * SUBS:(r + 1) * SUBS, :] for r in range(fold)], axis=1
            )
            root[pl.ds(to, SUBS), :] = jnp.sqrt(v)
        return carry

    lax.fori_loop(0, n_e * groups, roots, 0)

    def row_of(ref, *index):
        return jnp.broadcast_to(ref[index], (SUBS, LANES))

    def multiply(w_ref):
        for q in range(SUBS):
            hi, lo = split_bf16(work[q])
            dot = functools.partial(jnp.dot, preferred_element_type=jnp.float32)
            work[q] = dot(hi, w_ref[0]) + dot(lo, w_ref[0]) + dot(hi, w_ref[1])

    def energy(e, carry):
        def forward(g, carry):
            base = (e * groups + g) * SUBS * SUBS
            o_re, o_im = [], []
            for t in range(SUBS):
                at = pl.ds(base + t, SUBS, stride=SUBS)
                o_re.append(patch_re[at, :])
                o_im.append(patch_im[at, :])
            for m in range(modes):
                x_re, x_im = [], []
                for t in range(SUBS):
                    p_re = row_of(pr_ref, e, m, pl.ds(t, 1), slice(None))
                    p_im = row_of(pi_ref, e, m, pl.ds(t, 1), slice(None))
                    x_re.append(p_re * o_re[t] - p_im * o_im[t])
                    x_im.append(p_re * o_im[t] + p_im * o_re[t])
                y_re, y_im = fft8(x_re, x_im, -1)
                to = pl.ds(pl.multiple_of(g * per_group + m * SUBS, SUBS), SUBS)
                for q in range(SUBS):
                    a, b = y_re[q], y_im[q]
                    if q:
                        c = row_of(tw_ref, pl.ds(q, 1), slice(None))
                        d = row_of(tw_ref, pl.ds(SUBS + q, 1), slice(None))
                        a, b = a * c - b * d, a * d + b * c
                    work[q, to, 0:LANES] = a
                    work[q, to, LANES:2 * LANES] = b
            return carry

        lax.fori_loop(0, groups, forward, 0)
        multiply(wf_ref)

        def scale(g, carry):
            base = (e * groups + g) * SUBS * SUBS
            for q in range(SUBS):
                tos = [
                    pl.ds(pl.multiple_of(g * per_group + m * SUBS, SUBS), SUBS)
                    for m in range(modes)
                ]
                f = [(work[q, to, 0:LANES], work[q, to, LANES:2 * LANES]) for to in tos]
                power = f[0][0] * f[0][0] + f[0][1] * f[0][1]
                for a, b in f[1:]:
                    power = power + a * a + b * b
                sq = root[pl.ds(base + q, SUBS, stride=SUBS), :]
                factor = 1.0 - sq * lax.rsqrt(jnp.maximum(power, FLOOR_POWER))
                for to, (a, b) in zip(tos, f):
                    work[q, to, 0:LANES] = a * factor
                    work[q, to, LANES:2 * LANES] = b * factor
            return carry

        lax.fori_loop(0, groups, scale, 0)
        multiply(wb_ref)

        light = jnp.zeros((SUBS, LANES), jnp.float32)
        for m in range(modes):
            a, b = pr_ref[e, m], pi_ref[e, m]
            light = light + a * a + b * b

        def backward(g, carry):
            base = (e * groups + g) * SUBS * SUBS
            t_re = [None] * SUBS
            t_im = [None] * SUBS
            for m in range(modes):
                frm = pl.ds(pl.multiple_of(g * per_group + m * SUBS, SUBS), SUBS)
                x_re, x_im = [], []
                for q in range(SUBS):
                    a, b = work[q, frm, 0:LANES], work[q, frm, LANES:2 * LANES]
                    if q:
                        c = row_of(tw_ref, pl.ds(q, 1), slice(None))
                        d = row_of(tw_ref, pl.ds(SUBS + q, 1), slice(None))
                        a, b = a * c + b * d, b * c - a * d
                    x_re.append(a)
                    x_im.append(b)
                y_re, y_im = fft8(x_re, x_im, 1)
                for t in range(SUBS):
                    p_re = row_of(pr_ref, e, m, pl.ds(t, 1), slice(None))
                    p_im = row_of(pi_ref, e, m, pl.ds(t, 1), slice(None))
                    a = p_re * y_re[t] + p_im * y_im[t]
                    b = p_re * y_im[t] - p_im * y_re[t]
                    t_re[t] = a if m == 0 else t_re[t] + a
                    t_im[t] = b if m == 0 else t_im[t] + b
            for t in range(SUBS):
                at = pl.ds(base + t, SUBS, stride=SUBS)
                patch_re[at, :] = t_re[t]
                patch_im[at, :] = t_im[t]
            for s in range(SUBS):
                _, row, col = place(e, g * SUBS + s)
                frm = pl.ds(pl.multiple_of(base + s * SUBS, SUBS), SUBS)
                terms = (patch_re[frm, :], patch_im[frm, :], light)
                away = [lane + h * LANES - col for h in range(2)]
                inside = [(a >= 0) & (a < width) for a in away]
                for i in range(fold):
                    at = pl.ds(row + i, SUBS, stride=fold)
                    for n, term in enumerate(terms):
                        v = pltpu.roll(term, (col - i * width) & (LANES - 1), 1)
                        for h in range(2):
                            acc[n, h, e, at, :] = acc[n, h, e, at, :] + jnp.where(inside[h], v, 0.0)
            return carry

        lax.fori_loop(0, groups, backward, 0)
        return carry

    lax.fori_loop(0, n_e, energy, 0)

    side = re0.shape[1]

    dests = out_re.shape[0]

    def finish(n, carry):
        at = pl.ds(pl.multiple_of(n * SUBS, SUBS), SUBS)
        dest, far = n % dests, n // dests
        for e in range(n_e):
            for h, (o_re, o_im) in enumerate(((re0, im0), (re1, im1))):
                share = 1.0 / (acc[2, h, e, at, :] + REGULARIZER)
                out_re[dest, e, far, h] = o_re[e, at, :] - acc[0, h, e, at, :] * share
                out_im[dest, e, far, h] = o_im[e, at, :] - acc[1, h, e, at, :] * share
        return carry

    lax.fori_loop(0, side // SUBS, finish, 0)


def gradient_step(objects, beams, own_rec, par_rec, own_corner, par_corner, own_count, first, n_e, used, fars):
    o_re, o_im = objects
    local, side, _ = o_re.shape
    modes, width = beams[0].shape[1], beams[0].shape[-1]
    spots = own_rec.shape[1]
    flat = width * width // LANES
    assert flat == SUBS and side == 2 * LANES and used % SUBS == 0
    wf, wb, tw = transform_tables(width)
    shaped = [b.reshape(local, modes, flat, LANES) for b in beams]
    part = lambda i, f, *_: (f[0] // n_e, 0, 0, 0)
    half = [pl.BlockSpec((n_e, side, LANES), lambda i, f, *_, h=h: (f[0] // n_e, 0, h)) for h in range(2)]
    beam_spec = pl.BlockSpec((n_e, modes, flat, LANES), part)
    whole = pl.BlockSpec(memory_space=pltpu.VMEM)
    rows = used * modes
    n = n_e * used * SUBS
    out_shape = (side // SUBS // fars, n_e, fars, side // LANES, SUBS, LANES)
    return pl.pallas_call(
        functools.partial(step_kernel, n_e, spots, used, modes, width),
        out_shape=[jax.ShapeDtypeStruct(out_shape, jnp.float32)] * 2,
        grid_spec=pltpu.PrefetchScalarGridSpec(
            num_scalar_prefetch=4,
            grid=(1,),
            in_specs=[
                half[0], half[1], half[0], half[1], beam_spec, beam_spec,
                pl.BlockSpec(memory_space=pl.ANY), pl.BlockSpec(memory_space=pl.ANY),
                whole, whole, whole,
            ],
            out_specs=[pl.BlockSpec(out_shape, lambda i, *_: (0,) * len(out_shape))] * 2,
            scratch_shapes=[
                pltpu.VMEM((n_e, 2 * spots, width, width), jnp.float32),
                pltpu.VMEM((n, LANES), jnp.float32),
                pltpu.VMEM((n, LANES), jnp.float32),
                pltpu.VMEM((n, LANES), jnp.float32),
                pltpu.VMEM((SUBS, rows, 2 * LANES), jnp.float32),
                pltpu.VMEM((3, 2, n_e, side, LANES), jnp.float32),
                pltpu.VMEM((SUBS, LANES), jnp.float32),
                pltpu.SemaphoreType.DMA((2,)),
            ],
        ),
        name="gradient_step",
    )(
        first, own_corner, par_corner, own_count,
        o_re, o_re, o_im, o_im, *shaped, own_rec, par_rec, jnp.asarray(wf), jnp.asarray(wb), jnp.asarray(tw),
    )


def dot3(a, b):
    ah, al = split_bf16(a)
    bh, bl = split_bf16(b)
    left = jnp.concatenate([ah, al, ah], axis=1)
    right = jnp.concatenate([bh, bh, bl], axis=0)
    return jnp.dot(left, right, preferred_element_type=jnp.float32)


def project_kernel(fars, halves, project_ref, got_ref, out_ref):
    energies = project_ref.shape[1]
    stride = got_ref.shape[0] // energies
    for f in range(fars):
        for r in range(SUBS):
            parts = [
                got_ref[pl.ds((f * halves + h) * SUBS + r, energies, stride=stride), :]
                for h in range(halves)
            ]
            at = (f * SUBS + r) * halves * LANES
            values = jnp.concatenate(parts, axis=1)
            out_ref[:, at:at + halves * LANES] = dot3(project_ref[...], values)


def partial_coefs(project, got, fars, halves):
    rows = got.shape[0]
    edges, energies = project.shape
    pixels = rows // energies * LANES
    return pl.pallas_call(
        functools.partial(project_kernel, fars, halves),
        out_shape=jax.ShapeDtypeStruct((edges, pixels), jnp.float32),
        cost_estimate=pl.CostEstimate(
            flops=6 * edges * energies * pixels, bytes_accessed=rows * LANES * 4, transcendentals=0
        ),
        compiler_params=pltpu.CompilerParams(vmem_limit_bytes=SMALL),
        name="partial_coefs",
    )(project, got)


def fit_kernel(far_ref, mine_ref, theirs_ref, basis_ref, coef_ref, fit_ref):
    energies = basis_ref.shape[0]
    own = coef_ref.shape[1]
    stride = fit_ref.shape[0] // energies
    at = pl.ds(pl.multiple_of(far_ref[0] * own, own), own)
    coef_ref[...] = mine_ref[:, at] + theirs_ref[:, at]
    wide = 2 * LANES
    for j in range(mine_ref.shape[1] // wide):
        cols = slice(j * wide, (j + 1) * wide)
        values = dot3(basis_ref[...], mine_ref[:, cols] + theirs_ref[:, cols])
        for d in range(energies // SUBS):
            for u in range(2):
                to = pl.ds(d * SUBS * stride + j * 2 + u, SUBS, stride=stride)
                fit_ref[to, :] = values[d * SUBS:(d + 1) * SUBS, u * LANES:(u + 1) * LANES]


def fitted_values(far, mine, theirs, basis, own):
    edges, pixels = mine.shape
    energies = basis.shape[0]
    vmem = pl.BlockSpec(memory_space=pltpu.VMEM)
    return pl.pallas_call(
        fit_kernel,
        out_shape=[
            jax.ShapeDtypeStruct((edges, own), jnp.float32),
            jax.ShapeDtypeStruct((energies * pixels // LANES, LANES), jnp.float32),
        ],
        in_specs=[pl.BlockSpec(memory_space=pltpu.SMEM), vmem, vmem, vmem],
        out_specs=[vmem, vmem],
        cost_estimate=pl.CostEstimate(
            flops=6 * edges * energies * pixels, bytes_accessed=energies * pixels * 4, transcendentals=0
        ),
        compiler_params=pltpu.CompilerParams(vmem_limit_bytes=SMALL),
        name="fitted_values",
    )(far, mine, theirs, basis)


def gather_kernel(part, in_ref, *refs):
    out_ref, sem = refs[-2:]
    copies = [
        pltpu.make_async_copy(in_ref.at[s], out_ref.at[part, :, :, s], sem.at[s])
        for s in range(in_ref.shape[0])
    ]
    for c in copies:
        c.start()
    for c in copies:
        c.wait()


def gather_part(part, got, out):
    senders, energies, fars, subs, _ = got.shape
    shape = (2, energies, fars, senders, subs, LANES)
    hbm = pl.BlockSpec(memory_space=pl.ANY)
    return pl.pallas_call(
        functools.partial(gather_kernel, part),
        out_shape=jax.ShapeDtypeStruct(shape, jnp.float32),
        in_specs=[pl.BlockSpec(memory_space=pltpu.VMEM)] + ([] if out is None else [hbm]),
        out_specs=hbm,
        scratch_shapes=[pltpu.SemaphoreType.DMA((senders,))],
        input_output_aliases={} if out is None else {1: 0},
        compiler_params=pltpu.CompilerParams(vmem_limit_bytes=SMALL),
        name="gather_part",
    )(*([got] if out is None else [got, out]))


def local(
    sample_inphase,
    sample_quadrature,
    beam_inphase,
    beam_quadrature,
    recorded_diffraction,
    window_corners,
    filled_tallies,
    absorption_templates,
):
    local_energies = sample_inphase.shape[0]
    side = sample_inphase.shape[1]
    spots = recorded_diffraction.shape[2]
    fars = lax.axis_size("far")
    cube = lax.axis_size("cube")
    blocks = fars * cube
    tiles = lax.axis_size("ta")
    tile = lax.axis_index("ta")
    swap = [(0, 1), (1, 0)]
    assert tiles == 2 and fars == 2
    used = spots * 3 // 2
    divided = local_energies % tiles == 0
    n_e = local_energies // tiles if divided else local_energies
    pix = side * side // (blocks * tiles)
    two_level = divided and pix == SUBS * side and local_energies == SUBS
    own_rec = recorded_diffraction[:, 0]
    first = tile * n_e if divided else jnp.zeros((), jnp.int32)
    give = lax.dynamic_slice_in_dim(own_rec, (1 - tile) * n_e, n_e, 0) if divided else own_rec
    par_rec = lax.ppermute(give, "ta", swap)
    own_corner = window_corners.reshape(-1)
    par_corner = lax.ppermute(own_corner, "ta", swap)
    stepped = gradient_step(
        (sample_inphase, sample_quadrature),
        (beam_inphase, beam_quadrature),
        own_rec,
        par_rec,
        own_corner,
        par_corner,
        filled_tallies.reshape(-1),
        first.astype(jnp.int32)[None],
        n_e,
        used,
        fars if two_level else 1,
    )
    gram = jnp.dot(absorption_templates, absorption_templates.T, precision=HIGHEST)
    factor_low = jnp.linalg.cholesky(gram)
    project = jax.scipy.linalg.cho_solve((factor_low, True), absorption_templates)
    edges, energies = project.shape

    if two_level:
        far = lax.axis_index("far")
        near = energies // fars
        halves = side // LANES
        project_near = lax.dynamic_slice_in_dim(project, far * near, near, 1)
        basis_near = lax.dynamic_slice_in_dim(absorption_templates, far * near, near, 1).T
        far = far.astype(jnp.int32)[None]
        out, coefs = None, []
        later, project_near, basis_near = lax.optimization_barrier(
            (stepped[1], project_near, basis_near)
        )
        got = [lax.all_to_all(x, ("cube", "ta"), 0, 0, tiled=True) for x in (stepped[0], later)]
        for part in range(2):
            mine = partial_coefs(project_near, got[part].reshape(-1, LANES), fars, halves)
            theirs = lax.ppermute(mine, "far", swap)
            coef, fit = fitted_values(far, mine, theirs, basis_near, pix)
            coefs.append(coef)
            back = lax.all_to_all(
                fit.reshape(cube, local_energies, fars, pix // LANES, LANES), "cube", 0, 0, tiled=True
            )
            out = gather_part(part, back, out)
        return (out.reshape(2, local_energies, blocks, 1, pix), jnp.stack(coefs))

    flat = jnp.stack([x.transpose(1, 0, 2, 4, 3, 5) for x in stepped])
    if divided:
        flat = flat.reshape(2, n_e, blocks * tiles, pix)
        got = lax.all_to_all(flat, ("far", "cube", "ta"), 2, 1, tiled=True)
    else:
        flat = flat.reshape(2, n_e, blocks, tiles, pix)
        flat = lax.dynamic_index_in_dim(flat, tile, 3, keepdims=False)
        got = lax.all_to_all(flat, ("far", "cube"), 2, 1, tiled=True)
    values = got.reshape(2, -1, pix)
    coefs = jnp.einsum("ke,cen->ckn", project, values, precision=HIGHEST)
    fitted_here = jnp.einsum("ke,ckn->cen", absorption_templates, coefs, precision=HIGHEST)
    returned = lax.all_to_all(
        fitted_here[:, :, None, :], ("far", "cube"), split_axis=1, concat_axis=2, tiled=True
    )
    return (returned[:, :, :, None, :], coefs)


def solution(mesh):
    blocks, tiles = mesh.shape["ea"], mesh.shape["ta"]
    mesh = Mesh(mesh.devices.reshape(2, blocks // 2, tiles), ("far", "cube", "ta"))
    ea = ("far", "cube")
    in_specs = (
        P(ea, None, None),
        P(ea, None, None),
        P(ea, None, None, None),
        P(ea, None, None, None),
        P(ea, "ta", None, None, None),
        P(ea, "ta", None, None),
        P(ea, "ta"),
        P(),
    )
    out_specs = (P(None, ea, None, "ta", None), P(None, None, (*ea, "ta")))
    return jax.shard_map(local, mesh=mesh, in_specs=in_specs, out_specs=out_specs, check_vma=False)
```

```python
import functools

import jax
import jax.numpy as jnp
import numpy as np
from jax import lax
from jax.experimental import pallas as pl
from jax.experimental.pallas import tpu as pltpu
from jax.sharding import Mesh
from jax.sharding import PartitionSpec as P

HIGHEST = lax.Precision.HIGHEST
FLOOR_POWER = 0.5
REGULARIZER = 1.0
LANES = 128
SUBS = 8
SMALL = 12 << 20
LARGE = 60 << 20


def split_bf16(x):
    hi = x.astype(jnp.bfloat16)
    lo = (x - hi.astype(jnp.float32)).astype(jnp.bfloat16)
    return hi, lo


def transform_tables(width):
    fold = LANES // width
    i = np.arange(LANES) // width
    k = np.arange(LANES) % width
    phase = np.outer(i, i) / fold + np.outer(k, k) / width
    m = np.exp(-2j * np.pi * phase) / width
    real = np.block([[m.real, m.imag], [-m.imag, m.real]])
    q = np.arange(SUBS)
    tw = np.exp(-2j * np.pi * np.outer(q, i) / width)
    tw = np.concatenate([tw.real, tw.imag]).astype(np.float32)

    def halves(a):
        hi = a.astype(jnp.bfloat16)
        lo = (a - hi.astype(np.float64)).astype(jnp.bfloat16)
        return np.stack([hi, lo])

    return halves(real), halves(real.T.copy()), tw


def fft8(re, im, sign):
    def butterfly(a, b):
        return (a[0] + b[0], a[1] + b[1]), (a[0] - b[0], a[1] - b[1])

    def turn(a):
        return (-a[1], a[0]) if sign > 0 else (a[1], -a[0])

    h = np.float32(np.sqrt(0.5))

    def eighth(a):
        if sign > 0:
            return ((a[0] - a[1]) * h, (a[0] + a[1]) * h)
        return ((a[0] + a[1]) * h, (a[1] - a[0]) * h)

    def fft4(x):
        s0, d0 = butterfly(x[0], x[2])
        s1, d1 = butterfly(x[1], x[3])
        d1 = turn(d1)
        y0, y2 = butterfly(s0, s1)
        y1, y3 = butterfly(d0, d1)
        return [y0, y1, y2, y3]

    x = list(zip(re, im))
    e = fft4(x[0::2])
    o = fft4(x[1::2])
    o = [o[0], eighth(o[1]), turn(o[2]), turn(eighth(o[3]))]
    pairs = [butterfly(e[n], o[n]) for n in range(4)]
    out = [p[0] for p in pairs] + [p[1] for p in pairs]
    return [y[0] for y in out], [y[1] for y in out]


def step_kernel(
    n_e, spots, used, modes, width,
    first_ref, table_ref,
    o_re, o_im, pr_hbm, pi_hbm, own_rec, par_rec, wf_hbm, wb_hbm, tw_hbm,
    out_re, out_im,
    obj, rec, pr_ref, pi_ref, wf_ref, wb_ref, tw_ref, patch, term, root, work, acc, stage,
    obj_sem, rec_sem, shared_sem, out_sem,
):
    fold = LANES // width
    groups = used // SUBS
    per_group = modes * SUBS
    per_q = groups * per_group
    side = obj.shape[3]
    first = first_ref[0]
    dests = out_re.shape[0]

    def in_copies(e):
        return [
            pltpu.make_async_copy(
                ref.at[first + e, :, pl.ds(h * LANES, LANES)], obj.at[e, c, h], obj_sem.at[e, c, h]
            )
            for c, ref in enumerate((o_re, o_im))
            for h in range(2)
        ] + [
            pltpu.make_async_copy(own_rec.at[first + e], rec.at[e, pl.ds(0, spots)], rec_sem.at[e, 0]),
            pltpu.make_async_copy(par_rec.at[e], rec.at[e, pl.ds(spots, spots)], rec_sem.at[e, 1]),
        ]

    def out_copies(e):
        return [
            pltpu.make_async_copy(stage.at[e, c], ref.at[:, e], out_sem.at[e, c])
            for c, ref in enumerate((out_re, out_im))
        ]

    shared = [
        pltpu.make_async_copy(src, dst, shared_sem.at[n])
        for n, (src, dst) in enumerate(
            (
                (pr_hbm.at[pl.ds(first, n_e)], pr_ref),
                (pi_hbm.at[pl.ds(first, n_e)], pi_ref),
                (tw_hbm, tw_ref),
                (wf_hbm, wf_ref),
                (wb_hbm, wb_ref),
            )
        )
    ]
    for c in in_copies(0) + shared:
        c.start()
    for e in range(1, n_e):
        for c in in_copies(e):
            c.start()
    lane = lax.broadcasted_iota(jnp.int32, (SUBS, LANES), 1)
    block = lane // width
    for c in shared:
        c.wait()

    def place(e, index):
        packed = table_ref[(first + e) * used + index]
        rest = packed % (side * side)
        return packed // (side * side), rest // side, rest % side

    def merge(parts):
        out = parts[0]
        for n in range(1, fold):
            out = jnp.where(block == n, parts[n], out)
        return out

    def row_of(ref, *index):
        return jnp.broadcast_to(ref[index], (SUBS, LANES))

    def product(x, w_ref):
        hi, lo = split_bf16(x)
        dot = functools.partial(jnp.dot, preferred_element_type=jnp.float32)
        return dot(hi, w_ref[0]) + dot(lo, w_ref[0]) + dot(hi, w_ref[1])

    def energy(e, carry):
        acc[...] = jnp.zeros_like(acc)
        for c in in_copies(e):
            c.wait()
        for s in range(used):
            slot, row, col = place(e, s)
            low = lane >= col
            for c in range(2):
                parts = []
                for i in range(fold):
                    at = pl.ds(row + i, SUBS, stride=fold)
                    v = jnp.where(low, obj[e, c, 0, at, :], obj[e, c, 1, at, :])
                    parts.append(pltpu.roll(v, (i * width - col) & (LANES - 1), 1))
                patch[c, s * SUBS:(s + 1) * SUBS, :] = merge(parts)
            root[s * SUBS:(s + 1) * SUBS, :] = jnp.concatenate(
                [rec[e, slot, r * SUBS:(r + 1) * SUBS, :] for r in range(fold)], axis=1
            )

        for g in range(groups):
            base = g * SUBS * SUBS
            ats = [pl.ds(base + t, SUBS, stride=SUBS) for t in range(SUBS)]
            w_re = [patch[0, at, :] for at in ats]
            w_im = [patch[1, at, :] for at in ats]
            for m in range(modes):
                x_re, x_im = [], []
                for t in range(SUBS):
                    p_re = row_of(pr_ref, e, m, pl.ds(t, 1), slice(None))
                    p_im = row_of(pi_ref, e, m, pl.ds(t, 1), slice(None))
                    x_re.append(p_re * w_re[t] - p_im * w_im[t])
                    x_im.append(p_re * w_im[t] + p_im * w_re[t])
                y_re, y_im = fft8(x_re, x_im, -1)
                for q in range(SUBS):
                    a, b = y_re[q], y_im[q]
                    if q:
                        c = row_of(tw_ref, pl.ds(q, 1), slice(None))
                        d = row_of(tw_ref, pl.ds(SUBS + q, 1), slice(None))
                        a, b = a * c - b * d, a * d + b * c
                    to = q * per_q + g * per_group + m * SUBS
                    work[to:to + SUBS, 0:LANES] = a
                    work[to:to + SUBS, LANES:2 * LANES] = b

        for part in range(2):
            qs = range(part * SUBS // 2, (part + 1) * SUBS // 2)
            rows = slice(qs[0] * per_q, (qs[-1] + 1) * per_q)
            z = product(work[rows, :], wf_ref)
            scaled = []
            for q in qs:
                for g in range(groups):
                    f = []
                    for m in range(modes):
                        at = (q - qs[0]) * per_q + g * per_group + m * SUBS
                        f.append((z[at:at + SUBS, 0:LANES], z[at:at + SUBS, LANES:2 * LANES]))
                    power = f[0][0] * f[0][0] + f[0][1] * f[0][1]
                    for a, b in f[1:]:
                        power = power + a * a + b * b
                    measured = root[pl.ds(g * SUBS * SUBS + q, SUBS, stride=SUBS), :]
                    factor = 1.0 - jnp.sqrt(measured) * lax.rsqrt(jnp.maximum(power, FLOOR_POWER))
                    scaled += [
                        jnp.concatenate([a * factor, b * factor], axis=1) for a, b in f
                    ]
            work[rows, :] = product(jnp.concatenate(scaled, axis=0), wb_ref)

        light = jnp.zeros((SUBS, LANES), jnp.float32)
        for m in range(modes):
            a, b = pr_ref[e, m], pi_ref[e, m]
            light = light + a * a + b * b

        for g in range(groups):
            t_re = [None] * SUBS
            t_im = [None] * SUBS
            for m in range(modes):
                x_re, x_im = [], []
                for q in range(SUBS):
                    frm = q * per_q + g * per_group + m * SUBS
                    a, b = work[frm:frm + SUBS, 0:LANES], work[frm:frm + SUBS, LANES:2 * LANES]
                    if q:
                        c = row_of(tw_ref, pl.ds(q, 1), slice(None))
                        d = row_of(tw_ref, pl.ds(SUBS + q, 1), slice(None))
                        a, b = a * c + b * d, b * c - a * d
                    x_re.append(a)
                    x_im.append(b)
                y_re, y_im = fft8(x_re, x_im, 1)
                for t in range(SUBS):
                    p_re = row_of(pr_ref, e, m, pl.ds(t, 1), slice(None))
                    p_im = row_of(pi_ref, e, m, pl.ds(t, 1), slice(None))
                    a = p_re * y_re[t] + p_im * y_im[t]
                    b = p_re * y_im[t] - p_im * y_re[t]
                    t_re[t] = a if m == 0 else t_re[t] + a
                    t_im[t] = b if m == 0 else t_im[t] + b
            for t in range(SUBS):
                at = pl.ds(g * SUBS * SUBS + t, SUBS, stride=SUBS)
                term[0, at, :] = t_re[t]
                term[1, at, :] = t_im[t]

        for s in range(used):
            _, row, col = place(e, s)
            frm = slice(s * SUBS, (s + 1) * SUBS)
            terms = (term[0, frm, :], term[1, frm, :], light)
            which = jnp.where(col <= LANES - width, 0, jnp.where(col >= LANES, 1, 2))
            start = jnp.where(col <= LANES - width, col, jnp.where(col >= LANES, col - LANES, col - LANES // 2))
            inside = (lane >= start) & (lane < start + width)
            ats = [pl.ds(row + i, SUBS, stride=fold) for i in range(fold)]
            sums = []
            for n, t in enumerate(terms):
                for i in range(fold):
                    v = pltpu.roll(t, (start - i * width) & (LANES - 1), 1)
                    sums.append(acc[which, n, ats[i], :] + jnp.where(inside, v, 0.0))
            for n in range(3):
                for i in range(fold):
                    acc[which, n, ats[i], :] = sums[n * fold + i]

        high = lane >= LANES // 2

        def finish(k, carry):
            for u in range(2):
                n = k * 2 + u
                at = pl.ds(pl.multiple_of(n * SUBS, SUBS), SUBS)
                dest, far = n % dests, n // dests
                mid = [pltpu.roll(acc[2, c, at, :], LANES // 2, 1) for c in range(3)]
                for h in range(2):
                    mine = high if h == 0 else ~high
                    full = [acc[h, c, at, :] + jnp.where(mine, mid[c], 0.0) for c in range(3)]
                    share = 1.0 / (full[2] + REGULARIZER)
                    for c in range(2):
                        stage[e, c, dest, far, h] = obj[e, c, h, at, :] - full[c] * share
            return carry

        lax.fori_loop(0, side // SUBS // 2, finish, 0)
        for c in out_copies(e):
            c.start()
        return carry

    lax.fori_loop(0, n_e, energy, 0)
    for e in range(n_e):
        for c in out_copies(e):
            c.wait()


def gradient_step(objects, beams, own_rec, par_rec, table, first, n_e, used, fars):
    o_re, o_im = objects
    local, side, _ = o_re.shape
    modes, width = beams[0].shape[1], beams[0].shape[-1]
    spots = own_rec.shape[1]
    flat = width * width // LANES
    assert flat == SUBS and side == 2 * LANES and used % SUBS == 0
    wf, wb, tw = transform_tables(width)
    shaped = [b.reshape(local, modes, flat, LANES) for b in beams]
    hbm = pl.BlockSpec(memory_space=pl.ANY)
    out_shape = (side // SUBS // fars, n_e, fars, side // LANES, SUBS, LANES)
    return pl.pallas_call(
        functools.partial(step_kernel, n_e, spots, used, modes, width),
        out_shape=[jax.ShapeDtypeStruct(out_shape, jnp.float32)] * 2,
        grid_spec=pltpu.PrefetchScalarGridSpec(
            num_scalar_prefetch=2,
            grid=(1,),
            in_specs=[hbm] * 9,
            out_specs=[hbm, hbm],
            scratch_shapes=[
                pltpu.VMEM((n_e, 2, 2, side, LANES), jnp.float32),
                pltpu.VMEM((n_e, 2 * spots, width, width), jnp.float32),
                *[pltpu.VMEM((n_e, modes, flat, LANES), jnp.float32)] * 2,
                *[pltpu.VMEM(wf.shape, jnp.bfloat16)] * 2,
                pltpu.VMEM(tw.shape, jnp.float32),
                pltpu.VMEM((2, used * SUBS, LANES), jnp.float32),
                pltpu.VMEM((2, used * SUBS, LANES), jnp.float32),
                pltpu.VMEM((used * SUBS, LANES), jnp.float32),
                pltpu.VMEM((SUBS * used * modes, 2 * LANES), jnp.float32),
                pltpu.VMEM((3, 3, side, LANES), jnp.float32),
                pltpu.VMEM((n_e, 2, *(out_shape[:1] + out_shape[2:])), jnp.float32),
                pltpu.SemaphoreType.DMA((n_e, 2, 2)),
                pltpu.SemaphoreType.DMA((n_e, 2)),
                pltpu.SemaphoreType.DMA((5,)),
                pltpu.SemaphoreType.DMA((n_e, 2)),
            ],
        ),
        compiler_params=pltpu.CompilerParams(vmem_limit_bytes=LARGE),
        name="gradient_step",
    )(
        first, table, o_re, o_im, *shaped, own_rec, par_rec,
        jnp.asarray(wf), jnp.asarray(wb), jnp.asarray(tw),
    )


def slot_table(corners, counts, side, used, swap):
    local, spots, _ = corners.shape
    packed = corners[..., 0] * side + corners[..., 1]
    both = jnp.concatenate([packed, lax.ppermute(packed, "ta", swap)], axis=1)
    both = both + jnp.arange(2 * spots, dtype=jnp.int32) * (side * side)
    index = jnp.arange(used, dtype=jnp.int32)[None]
    index = index + jnp.where(index < counts, 0, spots - counts)
    chosen = index[:, :, None] == jnp.arange(2 * spots, dtype=jnp.int32)
    return jnp.sum(jnp.where(chosen, both[:, None, :], 0), axis=2).reshape(-1)


def dot3(a, b):
    ah, al = split_bf16(a)
    bh, bl = split_bf16(b)
    left = jnp.concatenate([ah, al, ah], axis=1)
    right = jnp.concatenate([bh, bh, bl], axis=0)
    return jnp.dot(left, right, preferred_element_type=jnp.float32)


def project_kernel(fars, halves, project_ref, got_ref, out_ref):
    energies = project_ref.shape[1]
    stride = got_ref.shape[0] // energies
    for f in range(fars):
        for r in range(SUBS):
            parts = [
                got_ref[pl.ds((f * halves + h) * SUBS + r, energies, stride=stride), :]
                for h in range(halves)
            ]
            at = (f * SUBS + r) * halves * LANES
            values = jnp.concatenate(parts, axis=1)
            out_ref[:, at:at + halves * LANES] = dot3(project_ref[...], values)


def partial_coefs(project, got, fars, halves):
    rows = got.shape[0]
    edges, energies = project.shape
    pixels = rows // energies * LANES
    return pl.pallas_call(
        functools.partial(project_kernel, fars, halves),
        out_shape=jax.ShapeDtypeStruct((edges, pixels), jnp.float32),
        cost_estimate=pl.CostEstimate(
            flops=6 * edges * energies * pixels, bytes_accessed=rows * LANES * 4, transcendentals=0
        ),
        compiler_params=pltpu.CompilerParams(vmem_limit_bytes=SMALL),
        name="partial_coefs",
    )(project, got)


def fit_kernel(far_ref, mine_ref, theirs_ref, basis_ref, coef_ref, fit_ref):
    energies = basis_ref.shape[0]
    own = coef_ref.shape[1]
    stride = fit_ref.shape[0] // energies
    at = pl.ds(pl.multiple_of(far_ref[0] * own, own), own)
    coef_ref[...] = mine_ref[:, at] + theirs_ref[:, at]
    wide = 2 * LANES
    for j in range(mine_ref.shape[1] // wide):
        cols = slice(j * wide, (j + 1) * wide)
        values = dot3(basis_ref[...], mine_ref[:, cols] + theirs_ref[:, cols])
        for d in range(energies // SUBS):
            for u in range(2):
                to = pl.ds(d * SUBS * stride + j * 2 + u, SUBS, stride=stride)
                fit_ref[to, :] = values[d * SUBS:(d + 1) * SUBS, u * LANES:(u + 1) * LANES]


def fitted_values(far, mine, theirs, basis, own):
    edges, pixels = mine.shape
    energies = basis.shape[0]
    vmem = pl.BlockSpec(memory_space=pltpu.VMEM)
    return pl.pallas_call(
        fit_kernel,
        out_shape=[
            jax.ShapeDtypeStruct((edges, own), jnp.float32),
            jax.ShapeDtypeStruct((energies * pixels // LANES, LANES), jnp.float32),
        ],
        in_specs=[pl.BlockSpec(memory_space=pltpu.SMEM), vmem, vmem, vmem],
        out_specs=[vmem, vmem],
        cost_estimate=pl.CostEstimate(
            flops=6 * edges * energies * pixels, bytes_accessed=energies * pixels * 4, transcendentals=0
        ),
        compiler_params=pltpu.CompilerParams(vmem_limit_bytes=SMALL),
        name="fitted_values",
    )(far, mine, theirs, basis)


def gather_kernel(part, in_ref, *refs):
    out_ref, sem = refs[-2:]
    copies = [
        pltpu.make_async_copy(in_ref.at[s], out_ref.at[part, :, :, s], sem.at[s])
        for s in range(in_ref.shape[0])
    ]
    for c in copies:
        c.start()
    for c in copies:
        c.wait()


def gather_part(part, got, out):
    senders, energies, fars, subs, _ = got.shape
    shape = (2, energies, fars, senders, subs, LANES)
    hbm = pl.BlockSpec(memory_space=pl.ANY)
    return pl.pallas_call(
        functools.partial(gather_kernel, part),
        out_shape=jax.ShapeDtypeStruct(shape, jnp.float32),
        in_specs=[pl.BlockSpec(memory_space=pltpu.VMEM)] + ([] if out is None else [hbm]),
        out_specs=hbm,
        scratch_shapes=[pltpu.SemaphoreType.DMA((senders,))],
        input_output_aliases={} if out is None else {1: 0},
        compiler_params=pltpu.CompilerParams(vmem_limit_bytes=SMALL),
        name="gather_part",
    )(*([got] if out is None else [got, out]))


def local(
    sample_inphase,
    sample_quadrature,
    beam_inphase,
    beam_quadrature,
    recorded_diffraction,
    window_corners,
    filled_tallies,
    absorption_templates,
):
    local_energies = sample_inphase.shape[0]
    side = sample_inphase.shape[1]
    spots = recorded_diffraction.shape[2]
    fars = lax.axis_size("far")
    cube = lax.axis_size("cube")
    blocks = fars * cube
    tiles = lax.axis_size("ta")
    tile = lax.axis_index("ta")
    swap = [(0, 1), (1, 0)]
    assert tiles == 2 and fars == 2
    used = spots * 3 // 2
    divided = local_energies % tiles == 0
    n_e = local_energies // tiles if divided else local_energies
    pix = side * side // (blocks * tiles)
    two_level = divided and pix == SUBS * side and local_energies == SUBS
    own_rec = recorded_diffraction[:, 0]
    first = tile * n_e if divided else jnp.zeros((), jnp.int32)
    give = lax.dynamic_slice_in_dim(own_rec, (1 - tile) * n_e, n_e, 0) if divided else own_rec
    par_rec = lax.ppermute(give, "ta", swap)
    table = slot_table(window_corners[:, 0], filled_tallies, side, used, swap)
    stepped = gradient_step(
        (sample_inphase, sample_quadrature),
        (beam_inphase, beam_quadrature),
        own_rec,
        par_rec,
        table,
        first.astype(jnp.int32)[None],
        n_e,
        used,
        fars if two_level else 1,
    )
    gram = jnp.dot(absorption_templates, absorption_templates.T, precision=HIGHEST)
    factor_low = jnp.linalg.cholesky(gram)
    project = jax.scipy.linalg.cho_solve((factor_low, True), absorption_templates)
    edges, energies = project.shape

    if two_level:
        far = lax.axis_index("far")
        near = energies // fars
        halves = side // LANES
        project_near = lax.dynamic_slice_in_dim(project, far * near, near, 1)
        basis_near = lax.dynamic_slice_in_dim(absorption_templates, far * near, near, 1).T
        far = far.astype(jnp.int32)[None]
        out, coefs = None, []
        later, project_near, basis_near = lax.optimization_barrier(
            (stepped[1], project_near, basis_near)
        )
        got = [lax.all_to_all(x, ("cube", "ta"), 0, 0, tiled=True) for x in (stepped[0], later)]
        for part in range(2):
            mine = partial_coefs(project_near, got[part].reshape(-1, LANES), fars, halves)
            theirs = lax.ppermute(mine, "far", swap)
            coef, fit = fitted_values(far, mine, theirs, basis_near, pix)
            coefs.append(coef)
            back = lax.all_to_all(
                fit.reshape(cube, local_energies, fars, pix // LANES, LANES), "cube", 0, 0, tiled=True
            )
            out = gather_part(part, back, out)
        return (out.reshape(2, local_energies, blocks, 1, pix), jnp.stack(coefs))

    flat = jnp.stack([x.transpose(1, 0, 2, 4, 3, 5) for x in stepped])
    if divided:
        flat = flat.reshape(2, n_e, blocks * tiles, pix)
        got = lax.all_to_all(flat, ("far", "cube", "ta"), 2, 1, tiled=True)
    else:
        flat = flat.reshape(2, n_e, blocks, tiles, pix)
        flat = lax.dynamic_index_in_dim(flat, tile, 3, keepdims=False)
        got = lax.all_to_all(flat, ("far", "cube"), 2, 1, tiled=True)
    values = got.reshape(2, -1, pix)
    coefs = jnp.einsum("ke,cen->ckn", project, values, precision=HIGHEST)
    fitted_here = jnp.einsum("ke,ckn->cen", absorption_templates, coefs, precision=HIGHEST)
    returned = lax.all_to_all(
        fitted_here[:, :, None, :], ("far", "cube"), split_axis=1, concat_axis=2, tiled=True
    )
    return (returned[:, :, :, None, :], coefs)


def solution(mesh):
    blocks, tiles = mesh.shape["ea"], mesh.shape["ta"]
    mesh = Mesh(mesh.devices.reshape(2, blocks // 2, tiles), ("far", "cube", "ta"))
    ea = ("far", "cube")
    in_specs = (
        P(ea, None, None),
        P(ea, None, None),
        P(ea, None, None, None),
        P(ea, None, None, None),
        P(ea, "ta", None, None, None),
        P(ea, "ta", None, None),
        P(ea, "ta"),
        P(),
    )
    out_specs = (P(None, ea, None, "ta", None), P(None, None, (*ea, "ta")))
    return jax.shard_map(local, mesh=mesh, in_specs=in_specs, out_specs=out_specs, check_vma=False)
```

```python
import functools

import jax
import jax.numpy as jnp
import numpy as np
from jax import lax
from jax.experimental import pallas as pl
from jax.experimental.pallas import tpu as pltpu
from jax.sharding import Mesh
from jax.sharding import PartitionSpec as P

HIGHEST = lax.Precision.HIGHEST
FLOOR_POWER = 0.5
REGULARIZER = 1.0
LANES = 128
SUBS = 8
SMALL = 12 << 20
LARGE = 60 << 20


def split_bf16(x):
    hi = x.astype(jnp.bfloat16)
    lo = (x - hi.astype(jnp.float32)).astype(jnp.bfloat16)
    return hi, lo


def transform_tables(width):
    fold = LANES // width
    i = np.arange(LANES) // width
    k = np.arange(LANES) % width
    phase = np.outer(i, i) / fold + np.outer(k, k) / width
    m = np.exp(-2j * np.pi * phase) / width
    real = np.block([[m.real, m.imag], [-m.imag, m.real]])
    q = np.arange(SUBS)
    tw = np.exp(-2j * np.pi * np.outer(q, i) / width)
    tw = np.concatenate([tw.real, tw.imag]).astype(np.float32)

    def halves(a):
        hi = a.astype(jnp.bfloat16)
        lo = (a - hi.astype(np.float64)).astype(jnp.bfloat16)
        return np.concatenate([hi, hi, lo])

    return halves(real), halves(real.T.copy()), tw


def fft8(re, im, sign):
    def butterfly(a, b):
        return (a[0] + b[0], a[1] + b[1]), (a[0] - b[0], a[1] - b[1])

    def turn(a):
        return (-a[1], a[0]) if sign > 0 else (a[1], -a[0])

    h = np.float32(np.sqrt(0.5))

    def eighth(a):
        if sign > 0:
            return ((a[0] - a[1]) * h, (a[0] + a[1]) * h)
        return ((a[0] + a[1]) * h, (a[1] - a[0]) * h)

    def fft4(x):
        s0, d0 = butterfly(x[0], x[2])
        s1, d1 = butterfly(x[1], x[3])
        d1 = turn(d1)
        y0, y2 = butterfly(s0, s1)
        y1, y3 = butterfly(d0, d1)
        return [y0, y1, y2, y3]

    x = list(zip(re, im))
    e = fft4(x[0::2])
    o = fft4(x[1::2])
    o = [o[0], eighth(o[1]), turn(o[2]), turn(eighth(o[3]))]
    pairs = [butterfly(e[n], o[n]) for n in range(4)]
    out = [p[0] for p in pairs] + [p[1] for p in pairs]
    return [y[0] for y in out], [y[1] for y in out]


def step_kernel(
    n_e, spots, used, modes, width,
    first_ref, table_ref,
    o_re, o_im, pr_hbm, pi_hbm, own_rec, par_rec, wf_hbm, wb_hbm, tw_hbm,
    out_re, out_im,
    obj, rec, pr_ref, pi_ref, wf_ref, wb_ref, tw_ref, patch, term, root, work, sum_re, sum_im, sum_light, stage,
    obj_sem, rec_sem, shared_sem, out_sem,
):
    fold = LANES // width
    groups = used // SUBS
    per_group = modes * SUBS
    per_q = groups * per_group
    side = obj.shape[3]
    first = first_ref[0]
    dests = out_re.shape[0]
    sums = (sum_re, sum_im, sum_light)

    def in_copies(e):
        return [
            pltpu.make_async_copy(
                ref.at[first + e, :, pl.ds(h * LANES, LANES)], obj.at[e, c, h], obj_sem.at[e, c, h]
            )
            for c, ref in enumerate((o_re, o_im))
            for h in range(2)
        ] + [
            pltpu.make_async_copy(own_rec.at[first + e], rec.at[e, pl.ds(0, spots)], rec_sem.at[e, 0]),
            pltpu.make_async_copy(par_rec.at[e], rec.at[e, pl.ds(spots, spots)], rec_sem.at[e, 1]),
        ]

    def out_copies(e):
        return [
            pltpu.make_async_copy(stage.at[e, c], ref.at[:, e], out_sem.at[e, c])
            for c, ref in enumerate((out_re, out_im))
        ]

    shared = [
        pltpu.make_async_copy(src, dst, shared_sem.at[n])
        for n, (src, dst) in enumerate(
            (
                (pr_hbm.at[pl.ds(first, n_e)], pr_ref),
                (pi_hbm.at[pl.ds(first, n_e)], pi_ref),
                (tw_hbm, tw_ref),
                (wf_hbm, wf_ref),
                (wb_hbm, wb_ref),
            )
        )
    ]
    for c in in_copies(0) + shared:
        c.start()
    for e in range(1, n_e):
        for c in in_copies(e):
            c.start()
    lane = lax.broadcasted_iota(jnp.int32, (SUBS, LANES), 1)
    block = lane // width
    for c in shared:
        c.wait()

    def place(e, index):
        packed = table_ref[(first + e) * used + index]
        shift = side.bit_length() - 1
        return packed >> (2 * shift), (packed >> shift) & (side - 1), packed & (side - 1)

    def merge(parts):
        out = parts[0]
        for n in range(1, fold):
            out = jnp.where(block == n, parts[n], out)
        return out

    def row_of(ref, *index):
        return jnp.broadcast_to(ref[index], (SUBS, LANES))

    def product(x, w_ref):
        hi, lo = split_bf16(x)
        wide = jnp.concatenate([hi, lo, hi], axis=1)
        return jnp.dot(wide, w_ref[...], preferred_element_type=jnp.float32)

    def energy(e, carry):
        for acc in sums:
            acc[...] = jnp.zeros_like(acc)
        for c in in_copies(e):
            c.wait()
        for s in range(used):
            slot, row, col = place(e, s)
            low = lane >= col
            for c in range(2):
                parts = []
                for i in range(fold):
                    at = pl.ds(row + i, SUBS, stride=fold)
                    v = jnp.where(low, obj[e, c, 0, at, :], obj[e, c, 1, at, :])
                    parts.append(pltpu.roll(v, (i * width - col) & (LANES - 1), 1))
                patch[c, s * SUBS:(s + 1) * SUBS, :] = merge(parts)
            root[s * SUBS:(s + 1) * SUBS, :] = jnp.concatenate(
                [rec[e, slot, r * SUBS:(r + 1) * SUBS, :] for r in range(fold)], axis=1
            )

        for g in range(groups):
            base = g * SUBS * SUBS
            ats = [pl.ds(base + t, SUBS, stride=SUBS) for t in range(SUBS)]
            w_re = [patch[0, at, :] for at in ats]
            w_im = [patch[1, at, :] for at in ats]
            for m in range(modes):
                x_re, x_im = [], []
                for t in range(SUBS):
                    p_re = row_of(pr_ref, e, m, pl.ds(t, 1), slice(None))
                    p_im = row_of(pi_ref, e, m, pl.ds(t, 1), slice(None))
                    x_re.append(p_re * w_re[t] - p_im * w_im[t])
                    x_im.append(p_re * w_im[t] + p_im * w_re[t])
                y_re, y_im = fft8(x_re, x_im, -1)
                for q in range(SUBS):
                    a, b = y_re[q], y_im[q]
                    if q:
                        c = row_of(tw_ref, pl.ds(q, 1), slice(None))
                        d = row_of(tw_ref, pl.ds(SUBS + q, 1), slice(None))
                        a, b = a * c - b * d, a * d + b * c
                    to = q * per_q + g * per_group + m * SUBS
                    work[to:to + SUBS, 0:LANES] = a
                    work[to:to + SUBS, LANES:2 * LANES] = b

        for part in range(2):
            qs = range(part * SUBS // 2, (part + 1) * SUBS // 2)
            rows = slice(qs[0] * per_q, (qs[-1] + 1) * per_q)
            z = product(work[rows, :], wf_ref)
            scaled = []
            for q in qs:
                for g in range(groups):
                    f = []
                    for m in range(modes):
                        at = (q - qs[0]) * per_q + g * per_group + m * SUBS
                        f.append((z[at:at + SUBS, 0:LANES], z[at:at + SUBS, LANES:2 * LANES]))
                    power = f[0][0] * f[0][0] + f[0][1] * f[0][1]
                    for a, b in f[1:]:
                        power = power + a * a + b * b
                    measured = root[pl.ds(g * SUBS * SUBS + q, SUBS, stride=SUBS), :]
                    factor = 1.0 - jnp.sqrt(measured) * lax.rsqrt(jnp.maximum(power, FLOOR_POWER))
                    scaled += [
                        jnp.concatenate([a * factor, b * factor], axis=1) for a, b in f
                    ]
            work[rows, :] = product(jnp.concatenate(scaled, axis=0), wb_ref)

        light = jnp.zeros((SUBS, LANES), jnp.float32)
        for m in range(modes):
            a, b = pr_ref[e, m], pi_ref[e, m]
            light = light + a * a + b * b

        for g in range(groups):
            t_re = [None] * SUBS
            t_im = [None] * SUBS
            for m in range(modes):
                x_re, x_im = [], []
                for q in range(SUBS):
                    frm = q * per_q + g * per_group + m * SUBS
                    a, b = work[frm:frm + SUBS, 0:LANES], work[frm:frm + SUBS, LANES:2 * LANES]
                    if q:
                        c = row_of(tw_ref, pl.ds(q, 1), slice(None))
                        d = row_of(tw_ref, pl.ds(SUBS + q, 1), slice(None))
                        a, b = a * c + b * d, b * c - a * d
                    x_re.append(a)
                    x_im.append(b)
                y_re, y_im = fft8(x_re, x_im, 1)
                for t in range(SUBS):
                    p_re = row_of(pr_ref, e, m, pl.ds(t, 1), slice(None))
                    p_im = row_of(pi_ref, e, m, pl.ds(t, 1), slice(None))
                    a = p_re * y_re[t] + p_im * y_im[t]
                    b = p_re * y_im[t] - p_im * y_re[t]
                    t_re[t] = a if m == 0 else t_re[t] + a
                    t_im[t] = b if m == 0 else t_im[t] + b
            for t in range(SUBS):
                at = pl.ds(g * SUBS * SUBS + t, SUBS, stride=SUBS)
                term[0, at, :] = t_re[t]
                term[1, at, :] = t_im[t]

        for s in range(used):
            _, row, col = place(e, s)
            frm = slice(s * SUBS, (s + 1) * SUBS)
            terms = (term[0, frm, :], term[1, frm, :], light)
            which = jnp.where(col <= LANES - width, 0, jnp.where(col >= LANES, 1, 2))
            start = jnp.where(col <= LANES - width, col, jnp.where(col >= LANES, col - LANES, col - LANES // 2))
            inside = (lane >= start) & (lane < start + width)
            ats = [pl.ds(row + i, SUBS, stride=fold) for i in range(fold)]
            for acc, t in zip(sums, terms):
                new = []
                for i in range(fold):
                    v = pltpu.roll(t, (start - i * width) & (LANES - 1), 1)
                    new.append(acc[which, ats[i], :] + jnp.where(inside, v, 0.0))
                for i in range(fold):
                    acc[which, ats[i], :] = new[i]

        high = lane >= LANES // 2

        def finish(k, carry):
            for u in range(SUBS):
                n = k * SUBS + u
                at = pl.ds(pl.multiple_of(n * SUBS, SUBS), SUBS)
                dest, far = n % dests, n // dests
                mid = [pltpu.roll(acc[2, at, :], LANES // 2, 1) for acc in sums]
                for h in range(2):
                    mine = high if h == 0 else ~high
                    full = [acc[h, at, :] + jnp.where(mine, m, 0.0) for acc, m in zip(sums, mid)]
                    share = 1.0 / (full[2] + REGULARIZER)
                    for c in range(2):
                        stage[e, c, dest, far, h] = obj[e, c, h, at, :] - full[c] * share
            return carry

        lax.fori_loop(0, side // SUBS // SUBS, finish, 0)
        for c in out_copies(e):
            c.start()
        return carry

    lax.fori_loop(0, n_e, energy, 0)
    for e in range(n_e):
        for c in out_copies(e):
            c.wait()


def gradient_step(objects, beams, own_rec, par_rec, table, first, n_e, used, fars):
    o_re, o_im = objects
    local, side, _ = o_re.shape
    modes, width = beams[0].shape[1], beams[0].shape[-1]
    spots = own_rec.shape[1]
    flat = width * width // LANES
    assert flat == SUBS and side == 2 * LANES and used % SUBS == 0
    wf, wb, tw = transform_tables(width)
    shaped = [b.reshape(local, modes, flat, LANES) for b in beams]
    hbm = pl.BlockSpec(memory_space=pl.ANY)
    out_shape = (side // SUBS // fars, n_e, fars, side // LANES, SUBS, LANES)
    return pl.pallas_call(
        functools.partial(step_kernel, n_e, spots, used, modes, width),
        out_shape=[jax.ShapeDtypeStruct(out_shape, jnp.float32)] * 2,
        grid_spec=pltpu.PrefetchScalarGridSpec(
            num_scalar_prefetch=2,
            grid=(1,),
            in_specs=[hbm] * 9,
            out_specs=[hbm, hbm],
            scratch_shapes=[
                pltpu.VMEM((n_e, 2, 2, side, LANES), jnp.float32),
                pltpu.VMEM((n_e, 2 * spots, width, width), jnp.float32),
                *[pltpu.VMEM((n_e, modes, flat, LANES), jnp.float32)] * 2,
                *[pltpu.VMEM(wf.shape, jnp.bfloat16)] * 2,
                pltpu.VMEM(tw.shape, jnp.float32),
                pltpu.VMEM((2, used * SUBS, LANES), jnp.float32),
                pltpu.VMEM((2, used * SUBS, LANES), jnp.float32),
                pltpu.VMEM((used * SUBS, LANES), jnp.float32),
                pltpu.VMEM((SUBS * used * modes, 2 * LANES), jnp.float32),
                *[pltpu.VMEM((3, side, LANES), jnp.float32)] * 3,
                pltpu.VMEM((n_e, 2, *(out_shape[:1] + out_shape[2:])), jnp.float32),
                pltpu.SemaphoreType.DMA((n_e, 2, 2)),
                pltpu.SemaphoreType.DMA((n_e, 2)),
                pltpu.SemaphoreType.DMA((5,)),
                pltpu.SemaphoreType.DMA((n_e, 2)),
            ],
        ),
        compiler_params=pltpu.CompilerParams(vmem_limit_bytes=LARGE),
        name="gradient_step",
    )(
        first, table, o_re, o_im, *shaped, own_rec, par_rec,
        jnp.asarray(wf), jnp.asarray(wb), jnp.asarray(tw),
    )


def slot_table(corners, counts, side, used, swap):
    local, spots, _ = corners.shape
    packed = corners[..., 0] * side + corners[..., 1]
    both = jnp.concatenate([packed, lax.ppermute(packed, "ta", swap)], axis=1)
    both = both + jnp.arange(2 * spots, dtype=jnp.int32) * (side * side)
    index = jnp.arange(used, dtype=jnp.int32)[None]
    index = index + jnp.where(index < counts, 0, spots - counts)
    chosen = index[:, :, None] == jnp.arange(2 * spots, dtype=jnp.int32)
    return jnp.sum(jnp.where(chosen, both[:, None, :], 0), axis=2).reshape(-1)


def dot3(a, b):
    ah, al = split_bf16(a)
    bh, bl = split_bf16(b)
    left = jnp.concatenate([ah, al, ah], axis=1)
    right = jnp.concatenate([bh, bh, bl], axis=0)
    return jnp.dot(left, right, preferred_element_type=jnp.float32)


def project_kernel(fars, halves, project_ref, got_ref, out_ref):
    energies = project_ref.shape[1]
    stride = got_ref.shape[0] // energies
    for f in range(fars):
        for r in range(SUBS):
            parts = [
                got_ref[pl.ds((f * halves + h) * SUBS + r, energies, stride=stride), :]
                for h in range(halves)
            ]
            at = (f * SUBS + r) * halves * LANES
            values = jnp.concatenate(parts, axis=1)
            out_ref[:, at:at + halves * LANES] = dot3(project_ref[...], values)


def partial_coefs(project, got, fars, halves):
    rows = got.shape[0]
    edges, energies = project.shape
    pixels = rows // energies * LANES
    return pl.pallas_call(
        functools.partial(project_kernel, fars, halves),
        out_shape=jax.ShapeDtypeStruct((edges, pixels), jnp.float32),
        cost_estimate=pl.CostEstimate(
            flops=6 * edges * energies * pixels, bytes_accessed=rows * LANES * 4, transcendentals=0
        ),
        compiler_params=pltpu.CompilerParams(vmem_limit_bytes=SMALL),
        name="partial_coefs",
    )(project, got)


def fit_kernel(far_ref, mine_ref, theirs_ref, basis_ref, coef_ref, fit_ref):
    energies = basis_ref.shape[0]
    own = coef_ref.shape[1]
    stride = fit_ref.shape[0] // energies
    at = pl.ds(pl.multiple_of(far_ref[0] * own, own), own)
    coef_ref[...] = mine_ref[:, at] + theirs_ref[:, at]
    wide = 2 * LANES
    for j in range(mine_ref.shape[1] // wide):
        cols = slice(j * wide, (j + 1) * wide)
        values = dot3(basis_ref[...], mine_ref[:, cols] + theirs_ref[:, cols])
        for d in range(energies // SUBS):
            for u in range(2):
                to = pl.ds(d * SUBS * stride + j * 2 + u, SUBS, stride=stride)
                fit_ref[to, :] = values[d * SUBS:(d + 1) * SUBS, u * LANES:(u + 1) * LANES]


def fitted_values(far, mine, theirs, basis, own):
    edges, pixels = mine.shape
    energies = basis.shape[0]
    vmem = pl.BlockSpec(memory_space=pltpu.VMEM)
    return pl.pallas_call(
        fit_kernel,
        out_shape=[
            jax.ShapeDtypeStruct((edges, own), jnp.float32),
            jax.ShapeDtypeStruct((energies * pixels // LANES, LANES), jnp.float32),
        ],
        in_specs=[pl.BlockSpec(memory_space=pltpu.SMEM), vmem, vmem, vmem],
        out_specs=[vmem, vmem],
        cost_estimate=pl.CostEstimate(
            flops=6 * edges * energies * pixels, bytes_accessed=energies * pixels * 4, transcendentals=0
        ),
        compiler_params=pltpu.CompilerParams(vmem_limit_bytes=SMALL),
        name="fitted_values",
    )(far, mine, theirs, basis)


def gather_kernel(part, in_ref, *refs):
    out_ref, sem = refs[-2:]
    copies = [
        pltpu.make_async_copy(in_ref.at[s], out_ref.at[part, :, :, s], sem.at[s])
        for s in range(in_ref.shape[0])
    ]
    for c in copies:
        c.start()
    for c in copies:
        c.wait()


def gather_part(part, got, out):
    senders, energies, fars, subs, _ = got.shape
    shape = (2, energies, fars, senders, subs, LANES)
    hbm = pl.BlockSpec(memory_space=pl.ANY)
    return pl.pallas_call(
        functools.partial(gather_kernel, part),
        out_shape=jax.ShapeDtypeStruct(shape, jnp.float32),
        in_specs=[pl.BlockSpec(memory_space=pltpu.VMEM)] + ([] if out is None else [hbm]),
        out_specs=hbm,
        scratch_shapes=[pltpu.SemaphoreType.DMA((senders,))],
        input_output_aliases={} if out is None else {1: 0},
        compiler_params=pltpu.CompilerParams(vmem_limit_bytes=SMALL),
        name="gather_part",
    )(*([got] if out is None else [got, out]))


def local(
    sample_inphase,
    sample_quadrature,
    beam_inphase,
    beam_quadrature,
    recorded_diffraction,
    window_corners,
    filled_tallies,
    absorption_templates,
):
    local_energies = sample_inphase.shape[0]
    side = sample_inphase.shape[1]
    spots = recorded_diffraction.shape[2]
    fars = lax.axis_size("far")
    cube = lax.axis_size("cube")
    blocks = fars * cube
    tiles = lax.axis_size("ta")
    tile = lax.axis_index("ta")
    swap = [(0, 1), (1, 0)]
    assert tiles == 2 and fars == 2
    used = spots * 3 // 2
    divided = local_energies % tiles == 0
    n_e = local_energies // tiles if divided else local_energies
    pix = side * side // (blocks * tiles)
    two_level = divided and pix == SUBS * side and local_energies == SUBS
    own_rec = recorded_diffraction[:, 0]
    first = tile * n_e if divided else jnp.zeros((), jnp.int32)
    give = lax.dynamic_slice_in_dim(own_rec, (1 - tile) * n_e, n_e, 0) if divided else own_rec
    par_rec = lax.ppermute(give, "ta", swap)
    table = slot_table(window_corners[:, 0], filled_tallies, side, used, swap)
    stepped = gradient_step(
        (sample_inphase, sample_quadrature),
        (beam_inphase, beam_quadrature),
        own_rec,
        par_rec,
        table,
        first.astype(jnp.int32)[None],
        n_e,
        used,
        fars if two_level else 1,
    )
    gram = jnp.dot(absorption_templates, absorption_templates.T, precision=HIGHEST)
    factor_low = jnp.linalg.cholesky(gram)
    project = jax.scipy.linalg.cho_solve((factor_low, True), absorption_templates)
    edges, energies = project.shape

    if two_level:
        far = lax.axis_index("far")
        near = energies // fars
        halves = side // LANES
        project_near = lax.dynamic_slice_in_dim(project, far * near, near, 1)
        basis_near = lax.dynamic_slice_in_dim(absorption_templates, far * near, near, 1).T
        far = far.astype(jnp.int32)[None]
        out, coefs = None, []
        later, project_near, basis_near = lax.optimization_barrier(
            (stepped[1], project_near, basis_near)
        )
        got = [lax.all_to_all(x, ("cube", "ta"), 0, 0, tiled=True) for x in (stepped[0], later)]
        for part in range(2):
            mine = partial_coefs(project_near, got[part].reshape(-1, LANES), fars, halves)
            theirs = lax.ppermute(mine, "far", swap)
            coef, fit = fitted_values(far, mine, theirs, basis_near, pix)
            coefs.append(coef)
            back = lax.all_to_all(
                fit.reshape(cube, local_energies, fars, pix // LANES, LANES), "cube", 0, 0, tiled=True
            )
            out = gather_part(part, back, out)
        return (out.reshape(2, local_energies, blocks, 1, pix), jnp.stack(coefs))

    flat = jnp.stack([x.transpose(1, 0, 2, 4, 3, 5) for x in stepped])
    if divided:
        flat = flat.reshape(2, n_e, blocks * tiles, pix)
        got = lax.all_to_all(flat, ("far", "cube", "ta"), 2, 1, tiled=True)
    else:
        flat = flat.reshape(2, n_e, blocks, tiles, pix)
        flat = lax.dynamic_index_in_dim(flat, tile, 3, keepdims=False)
        got = lax.all_to_all(flat, ("far", "cube"), 2, 1, tiled=True)
    values = got.reshape(2, -1, pix)
    coefs = jnp.einsum("ke,cen->ckn", project, values, precision=HIGHEST)
    fitted_here = jnp.einsum("ke,ckn->cen", absorption_templates, coefs, precision=HIGHEST)
    returned = lax.all_to_all(
        fitted_here[:, :, None, :], ("far", "cube"), split_axis=1, concat_axis=2, tiled=True
    )
    return (returned[:, :, :, None, :], coefs)


def solution(mesh):
    blocks, tiles = mesh.shape["ea"], mesh.shape["ta"]
    mesh = Mesh(mesh.devices.reshape(2, blocks // 2, tiles), ("far", "cube", "ta"))
    ea = ("far", "cube")
    in_specs = (
        P(ea, None, None),
        P(ea, None, None),
        P(ea, None, None, None),
        P(ea, None, None, None),
        P(ea, "ta", None, None, None),
        P(ea, "ta", None, None),
        P(ea, "ta"),
        P(),
    )
    out_specs = (P(None, ea, None, "ta", None), P(None, None, (*ea, "ta")))
    return jax.shard_map(local, mesh=mesh, in_specs=in_specs, out_specs=out_specs, check_vma=False)
```

```python
import functools

import jax
import jax.numpy as jnp
import numpy as np
from jax import lax
from jax.experimental import pallas as pl
from jax.experimental.pallas import tpu as pltpu
from jax.sharding import Mesh
from jax.sharding import PartitionSpec as P

HIGHEST = lax.Precision.HIGHEST
FLOOR_POWER = 0.5
REGULARIZER = 1.0
LANES = 128
SUBS = 8
SMALL = 12 << 20
LARGE = 52 << 20


def split_bf16(x):
    hi = x.astype(jnp.bfloat16)
    lo = (x - hi.astype(jnp.float32)).astype(jnp.bfloat16)
    return hi, lo


def transform_tables(width):
    fold = LANES // width
    i = np.arange(LANES) // width
    k = np.arange(LANES) % width
    phase = np.outer(i, i) / fold + np.outer(k, k) / width
    m = np.exp(-2j * np.pi * phase) / width
    real = np.block([[m.real, m.imag], [-m.imag, m.real]])
    q = np.arange(SUBS)
    tw = np.exp(-2j * np.pi * np.outer(q, i) / width)
    tw = np.concatenate([tw.real, tw.imag]).astype(np.float32)

    def halves(a):
        hi = a.astype(jnp.bfloat16)
        lo = (a - hi.astype(np.float64)).astype(jnp.bfloat16)
        return np.concatenate([hi, hi, lo])

    return halves(real), halves(real.T.copy()), tw


def fft8(re, im, sign):
    def butterfly(a, b):
        return (a[0] + b[0], a[1] + b[1]), (a[0] - b[0], a[1] - b[1])

    def turn(a):
        return (-a[1], a[0]) if sign > 0 else (a[1], -a[0])

    h = np.float32(np.sqrt(0.5))

    def eighth(a):
        if sign > 0:
            return ((a[0] - a[1]) * h, (a[0] + a[1]) * h)
        return ((a[0] + a[1]) * h, (a[1] - a[0]) * h)

    def fft4(x):
        s0, d0 = butterfly(x[0], x[2])
        s1, d1 = butterfly(x[1], x[3])
        d1 = turn(d1)
        y0, y2 = butterfly(s0, s1)
        y1, y3 = butterfly(d0, d1)
        return [y0, y1, y2, y3]

    x = list(zip(re, im))
    e = fft4(x[0::2])
    o = fft4(x[1::2])
    o = [o[0], eighth(o[1]), turn(o[2]), turn(eighth(o[3]))]
    pairs = [butterfly(e[n], o[n]) for n in range(4)]
    out = [p[0] for p in pairs] + [p[1] for p in pairs]
    return [y[0] for y in out], [y[1] for y in out]


def step_kernel(
    n_e, spots, used, modes, width,
    table_ref,
    o_re, o_im, pr_hbm, pi_hbm, own_rec, par_rec, wf_hbm, wb_hbm, tw_hbm,
    out_re, out_im,
    obj, rec, beam, probe, wf_ref, wb_ref, tw_ref, patch, term, root, work, sum_re, sum_im, sum_light, stage,
    obj_sem, rec_sem, shared_sem, out_sem,
):
    fold = LANES // width
    groups = used // SUBS
    per_group = modes * SUBS
    per_q = groups * per_group
    side = obj.shape[3]
    first = table_ref[0] >> (2 * side.bit_length() - 2 + spots.bit_length())
    dests = out_re.shape[0]
    sums = (sum_re, sum_im, sum_light)

    def in_copies(e):
        return [
            pltpu.make_async_copy(
                ref.at[first + e, :, pl.ds(h * LANES, LANES)], obj.at[e, c, h], obj_sem.at[e, c, h]
            )
            for c, ref in enumerate((o_re, o_im))
            for h in range(2)
        ] + [
            pltpu.make_async_copy(own_rec.at[first + e], rec.at[e, pl.ds(0, spots)], rec_sem.at[e, 0]),
            pltpu.make_async_copy(par_rec.at[e], rec.at[e, pl.ds(spots, spots)], rec_sem.at[e, 1]),
        ]

    def out_copies(e):
        return [
            pltpu.make_async_copy(stage.at[e, c], ref.at[:, e], out_sem.at[e, c])
            for c, ref in enumerate((out_re, out_im))
        ]

    shared = [
        pltpu.make_async_copy(src, dst, shared_sem.at[n])
        for n, (src, dst) in enumerate(
            (
                (pr_hbm.at[pl.ds(first, n_e)], beam.at[0]),
                (pi_hbm.at[pl.ds(first, n_e)], beam.at[1]),
                (tw_hbm, tw_ref),
                (wf_hbm, wf_ref),
                (wb_hbm, wb_ref),
            )
        )
    ]
    for c in in_copies(0) + shared:
        c.start()
    lane = lax.broadcasted_iota(jnp.int32, (SUBS, LANES), 1)
    block = lane // width
    for c in shared:
        c.wait()

    def place(e, index):
        packed = table_ref[e * used + index]
        shift = side.bit_length() - 1
        return (packed >> (2 * shift)) & (2 * spots - 1), (packed >> shift) & (side - 1), packed & (side - 1)

    def merge(parts):
        out = parts[0]
        for n in range(1, fold):
            out = jnp.where(block == n, parts[n], out)
        return out

    def row_of(ref, *index):
        return jnp.broadcast_to(ref[index], (SUBS, LANES))

    def product(x, w_ref):
        hi, lo = split_bf16(x)
        wide = jnp.concatenate([hi, lo, hi], axis=1)
        return jnp.dot(wide, w_ref[...], preferred_element_type=jnp.float32)

    def energy(e, carry):
        for acc in sums:
            acc[...] = jnp.zeros_like(acc)
        for c in in_copies(e):
            c.wait()

        @pl.when(e + 1 < n_e)
        def _():
            for c in in_copies(e + 1):
                c.start()

        for c in range(2):
            for m in range(modes):
                probe[c, m] = jnp.concatenate(
                    [beam[c, e, m, pl.ds(i, SUBS, stride=fold), :] for i in range(fold)], axis=1
                )
        for s in range(used):
            slot, row, col = place(e, s)
            low = lane >= col
            for c in range(2):
                parts = []
                for i in range(fold):
                    at = pl.ds(row + i, SUBS, stride=fold)
                    v = jnp.where(low, obj[e, c, 0, at, :], obj[e, c, 1, at, :])
                    parts.append(pltpu.roll(v, (i * width - col) & (LANES - 1), 1))
                patch[c, s * SUBS:(s + 1) * SUBS, :] = merge(parts)
            root[s * SUBS:(s + 1) * SUBS, :] = jnp.concatenate(
                [rec[e, slot, r * SUBS:(r + 1) * SUBS, :] for r in range(fold)], axis=1
            )

        for g in range(groups):
            base = g * SUBS * SUBS
            ats = [pl.ds(base + t, SUBS, stride=SUBS) for t in range(SUBS)]
            w_re = [patch[0, at, :] for at in ats]
            w_im = [patch[1, at, :] for at in ats]
            for m in range(modes):
                x_re, x_im = [], []
                for t in range(SUBS):
                    p_re = row_of(probe, 0, m, pl.ds(t, 1), slice(None))
                    p_im = row_of(probe, 1, m, pl.ds(t, 1), slice(None))
                    x_re.append(p_re * w_re[t] - p_im * w_im[t])
                    x_im.append(p_re * w_im[t] + p_im * w_re[t])
                y_re, y_im = fft8(x_re, x_im, -1)
                for q in range(SUBS):
                    a, b = y_re[q], y_im[q]
                    if q:
                        c = row_of(tw_ref, pl.ds(q, 1), slice(None))
                        d = row_of(tw_ref, pl.ds(SUBS + q, 1), slice(None))
                        a, b = a * c - b * d, a * d + b * c
                    to = q * per_q + g * per_group + m * SUBS
                    work[to:to + SUBS, 0:LANES] = a
                    work[to:to + SUBS, LANES:2 * LANES] = b

        for part in range(2):
            qs = range(part * SUBS // 2, (part + 1) * SUBS // 2)
            rows = slice(qs[0] * per_q, (qs[-1] + 1) * per_q)
            z = product(work[rows, :], wf_ref)
            scaled = []
            for q in qs:
                for g in range(groups):
                    f = []
                    for m in range(modes):
                        at = (q - qs[0]) * per_q + g * per_group + m * SUBS
                        f.append((z[at:at + SUBS, 0:LANES], z[at:at + SUBS, LANES:2 * LANES]))
                    power = f[0][0] * f[0][0] + f[0][1] * f[0][1]
                    for a, b in f[1:]:
                        power = power + a * a + b * b
                    measured = root[pl.ds(g * SUBS * SUBS + q, SUBS, stride=SUBS), :]
                    factor = 1.0 - jnp.sqrt(measured) * lax.rsqrt(jnp.maximum(power, FLOOR_POWER))
                    scaled += [
                        jnp.concatenate([a * factor, b * factor], axis=1) for a, b in f
                    ]
            work[rows, :] = product(jnp.concatenate(scaled, axis=0), wb_ref)

        light = jnp.zeros((SUBS, LANES), jnp.float32)
        for m in range(modes):
            a, b = probe[0, m], probe[1, m]
            light = light + a * a + b * b

        for g in range(groups):
            t_re = [None] * SUBS
            t_im = [None] * SUBS
            for m in range(modes):
                x_re, x_im = [], []
                for q in range(SUBS):
                    frm = q * per_q + g * per_group + m * SUBS
                    a, b = work[frm:frm + SUBS, 0:LANES], work[frm:frm + SUBS, LANES:2 * LANES]
                    if q:
                        c = row_of(tw_ref, pl.ds(q, 1), slice(None))
                        d = row_of(tw_ref, pl.ds(SUBS + q, 1), slice(None))
                        a, b = a * c + b * d, b * c - a * d
                    x_re.append(a)
                    x_im.append(b)
                y_re, y_im = fft8(x_re, x_im, 1)
                for t in range(SUBS):
                    p_re = row_of(probe, 0, m, pl.ds(t, 1), slice(None))
                    p_im = row_of(probe, 1, m, pl.ds(t, 1), slice(None))
                    a = p_re * y_re[t] + p_im * y_im[t]
                    b = p_re * y_im[t] - p_im * y_re[t]
                    t_re[t] = a if m == 0 else t_re[t] + a
                    t_im[t] = b if m == 0 else t_im[t] + b
            for t in range(SUBS):
                at = pl.ds(g * SUBS * SUBS + t, SUBS, stride=SUBS)
                term[0, at, :] = t_re[t]
                term[1, at, :] = t_im[t]

        for s in range(used):
            _, row, col = place(e, s)
            frm = slice(s * SUBS, (s + 1) * SUBS)
            terms = (term[0, frm, :], term[1, frm, :], light)
            which = jnp.where(col <= LANES - width, 0, jnp.where(col >= LANES, 1, 2))
            start = jnp.where(col <= LANES - width, col, jnp.where(col >= LANES, col - LANES, col - LANES // 2))
            inside = (lane >= start) & (lane < start + width)
            ats = [pl.ds(row + i, SUBS, stride=fold) for i in range(fold)]
            for acc, t in zip(sums, terms):
                new = []
                for i in range(fold):
                    v = pltpu.roll(t, (start - i * width) & (LANES - 1), 1)
                    new.append(acc[which, ats[i], :] + jnp.where(inside, v, 0.0))
                for i in range(fold):
                    acc[which, ats[i], :] = new[i]

        high = lane >= LANES // 2

        def finish(k, carry):
            for u in range(SUBS):
                n = k * SUBS + u
                at = pl.ds(pl.multiple_of(n * SUBS, SUBS), SUBS)
                dest, far = n & (dests - 1), n >> (dests.bit_length() - 1)
                mid = [pltpu.roll(acc[2, at, :], LANES // 2, 1) for acc in sums]
                for h in range(2):
                    mine = high if h == 0 else ~high
                    full = [acc[h, at, :] + jnp.where(mine, m, 0.0) for acc, m in zip(sums, mid)]
                    share = 1.0 / (full[2] + REGULARIZER)
                    for c in range(2):
                        stage[e, c, dest, far, h] = obj[e, c, h, at, :] - full[c] * share
            return carry

        lax.fori_loop(0, side // SUBS // SUBS, finish, 0)
        for c in out_copies(e):
            c.start()
        return carry

    lax.fori_loop(0, n_e, energy, 0)
    for e in range(n_e):
        for c in out_copies(e):
            c.wait()


def gradient_step(objects, beams, own_rec, par_rec, table, n_e, used, fars):
    o_re, o_im = objects
    local, side, _ = o_re.shape
    modes, width = beams[0].shape[1], beams[0].shape[-1]
    spots = own_rec.shape[1]
    flat = width * width // LANES
    assert flat == SUBS and side == 2 * LANES and used % SUBS == 0
    wf, wb, tw = transform_tables(width)
    hbm = pl.BlockSpec(memory_space=pl.ANY)
    out_shape = (side // SUBS // fars, n_e, fars, side // LANES, SUBS, LANES)
    return pl.pallas_call(
        functools.partial(step_kernel, n_e, spots, used, modes, width),
        out_shape=[jax.ShapeDtypeStruct(out_shape, jnp.float32)] * 2,
        grid_spec=pltpu.PrefetchScalarGridSpec(
            num_scalar_prefetch=1,
            grid=(1,),
            in_specs=[hbm] * 9,
            out_specs=[hbm, hbm],
            scratch_shapes=[
                pltpu.VMEM((n_e, 2, 2, side, LANES), jnp.float32),
                pltpu.VMEM((n_e, 2 * spots, width, width), jnp.float32),
                pltpu.VMEM((2, n_e, modes, width, width), jnp.float32),
                pltpu.VMEM((2, modes, flat, LANES), jnp.float32),
                *[pltpu.VMEM(wf.shape, jnp.bfloat16)] * 2,
                pltpu.VMEM(tw.shape, jnp.float32),
                pltpu.VMEM((2, used * SUBS, LANES), jnp.float32),
                pltpu.VMEM((2, used * SUBS, LANES), jnp.float32),
                pltpu.VMEM((used * SUBS, LANES), jnp.float32),
                pltpu.VMEM((SUBS * used * modes, 2 * LANES), jnp.float32),
                *[pltpu.VMEM((3, side, LANES), jnp.float32)] * 3,
                pltpu.VMEM((n_e, 2, *(out_shape[:1] + out_shape[2:])), jnp.float32),
                pltpu.SemaphoreType.DMA((n_e, 2, 2)),
                pltpu.SemaphoreType.DMA((n_e, 2)),
                pltpu.SemaphoreType.DMA((5,)),
                pltpu.SemaphoreType.DMA((n_e, 2)),
            ],
        ),
        compiler_params=pltpu.CompilerParams(vmem_limit_bytes=LARGE),
        name="gradient_step",
    )(
        table, o_re, o_im, *beams, own_rec, par_rec,
        jnp.asarray(wf), jnp.asarray(wb), jnp.asarray(tw),
    )


def slot_table(corners, theirs, counts, first, n_e, side):
    spots = corners.shape[1]
    used = spots * 3 // 2
    assert side & (side - 1) == 0 and spots & (spots - 1) == 0
    both = jnp.concatenate([corners, theirs], axis=1)
    both = lax.dynamic_slice_in_dim(both, first, n_e, 0)
    counts = lax.dynamic_slice_in_dim(counts, first, n_e, 0)
    both = both[..., 0] * side + both[..., 1]
    both = both + (first * 2 * spots + jnp.arange(2 * spots, dtype=jnp.int32)) * (side * side)
    index = jnp.arange(used, dtype=jnp.int32)[None]
    index = index + jnp.where(index < counts, 0, spots - counts)
    chosen = index[:, :, None] == jnp.arange(2 * spots, dtype=jnp.int32)
    return jnp.sum(jnp.where(chosen, both[:, None, :], 0), axis=2).reshape(-1)


def dot3(a, b):
    ah, al = split_bf16(a)
    bh, bl = split_bf16(b)
    left = jnp.concatenate([ah, al, ah], axis=1)
    right = jnp.concatenate([bh, bh, bl], axis=0)
    return jnp.dot(left, right, preferred_element_type=jnp.float32)


def project_kernel(fars, halves, project_ref, got_ref, out_ref):
    energies = project_ref.shape[1]
    stride = got_ref.shape[0] // energies
    for f in range(fars):
        for r in range(SUBS):
            parts = [
                got_ref[pl.ds((f * halves + h) * SUBS + r, energies, stride=stride), :]
                for h in range(halves)
            ]
            at = (f * SUBS + r) * halves * LANES
            values = jnp.concatenate(parts, axis=1)
            out_ref[:, at:at + halves * LANES] = dot3(project_ref[...], values)


def partial_coefs(project, got, fars, halves):
    rows = got.shape[0]
    edges, energies = project.shape
    pixels = rows // energies * LANES
    return pl.pallas_call(
        functools.partial(project_kernel, fars, halves),
        out_shape=jax.ShapeDtypeStruct((edges, pixels), jnp.float32),
        cost_estimate=pl.CostEstimate(
            flops=6 * edges * energies * pixels, bytes_accessed=rows * LANES * 4, transcendentals=0
        ),
        compiler_params=pltpu.CompilerParams(vmem_limit_bytes=SMALL),
        name="partial_coefs",
    )(project, got)


def fit_kernel(far_ref, mine_ref, theirs_ref, basis_ref, coef_ref, fit_ref):
    energies = basis_ref.shape[0]
    own = coef_ref.shape[1]
    stride = fit_ref.shape[0] // energies
    at = pl.ds(pl.multiple_of(far_ref[0] * own, own), own)
    coef_ref[...] = mine_ref[:, at] + theirs_ref[:, at]
    wide = 2 * LANES
    for j in range(mine_ref.shape[1] // wide):
        cols = slice(j * wide, (j + 1) * wide)
        values = dot3(basis_ref[...], mine_ref[:, cols] + theirs_ref[:, cols])
        for d in range(energies // SUBS):
            for u in range(2):
                to = pl.ds(d * SUBS * stride + j * 2 + u, SUBS, stride=stride)
                fit_ref[to, :] = values[d * SUBS:(d + 1) * SUBS, u * LANES:(u + 1) * LANES]


def fitted_values(far, mine, theirs, basis, own):
    edges, pixels = mine.shape
    energies = basis.shape[0]
    vmem = pl.BlockSpec(memory_space=pltpu.VMEM)
    return pl.pallas_call(
        fit_kernel,
        out_shape=[
            jax.ShapeDtypeStruct((edges, own), jnp.float32),
            jax.ShapeDtypeStruct((energies * pixels // LANES, LANES), jnp.float32),
        ],
        in_specs=[pl.BlockSpec(memory_space=pltpu.SMEM), vmem, vmem, vmem],
        out_specs=[vmem, vmem],
        cost_estimate=pl.CostEstimate(
            flops=6 * edges * energies * pixels, bytes_accessed=energies * pixels * 4, transcendentals=0
        ),
        compiler_params=pltpu.CompilerParams(vmem_limit_bytes=SMALL),
        name="fitted_values",
    )(far, mine, theirs, basis)


def gather_kernel(part, in_ref, *refs):
    out_ref, sem = refs[-2:]
    copies = [
        pltpu.make_async_copy(in_ref.at[s], out_ref.at[part, :, :, s], sem.at[s])
        for s in range(in_ref.shape[0])
    ]
    for c in copies:
        c.start()
    for c in copies:
        c.wait()


def gather_part(part, got, out):
    senders, energies, fars, subs, _ = got.shape
    shape = (2, energies, fars, senders, subs, LANES)
    hbm = pl.BlockSpec(memory_space=pl.ANY)
    return pl.pallas_call(
        functools.partial(gather_kernel, part),
        out_shape=jax.ShapeDtypeStruct(shape, jnp.float32),
        in_specs=[pl.BlockSpec(memory_space=pltpu.VMEM)] + ([] if out is None else [hbm]),
        out_specs=hbm,
        scratch_shapes=[pltpu.SemaphoreType.DMA((senders,))],
        input_output_aliases={} if out is None else {1: 0},
        compiler_params=pltpu.CompilerParams(vmem_limit_bytes=SMALL),
        name="gather_part",
    )(*([got] if out is None else [got, out]))


def local(
    sample_inphase,
    sample_quadrature,
    beam_inphase,
    beam_quadrature,
    recorded_diffraction,
    window_corners,
    filled_tallies,
    absorption_templates,
):
    local_energies = sample_inphase.shape[0]
    side = sample_inphase.shape[1]
    spots = recorded_diffraction.shape[2]
    fars = lax.axis_size("far")
    cube = lax.axis_size("cube")
    blocks = fars * cube
    tiles = lax.axis_size("ta")
    tile = lax.axis_index("ta")
    swap = [(0, 1), (1, 0)]
    assert tiles == 2 and fars == 2
    used = spots * 3 // 2
    divided = local_energies % tiles == 0
    n_e = local_energies // tiles if divided else local_energies
    pix = side * side // (blocks * tiles)
    two_level = divided and pix == SUBS * side and local_energies == SUBS
    own_rec = recorded_diffraction[:, 0]
    first = tile * n_e if divided else jnp.zeros((), jnp.int32)
    theirs = lax.ppermute(window_corners, "ta", swap)
    give = lax.dynamic_slice_in_dim(own_rec, (1 - tile) * n_e, n_e, 0) if divided else own_rec
    par_rec = lax.ppermute(give, "ta", swap)
    table = slot_table(
        window_corners[:, 0], theirs[:, 0], filled_tallies, first.astype(jnp.int32), n_e, side
    )
    stepped = gradient_step(
        (sample_inphase, sample_quadrature),
        (beam_inphase, beam_quadrature),
        own_rec,
        par_rec,
        table,
        n_e,
        used,
        fars if two_level else 1,
    )
    gram = jnp.dot(absorption_templates, absorption_templates.T, precision=HIGHEST)
    factor_low = jnp.linalg.cholesky(gram)
    project = jax.scipy.linalg.cho_solve((factor_low, True), absorption_templates)
    edges, energies = project.shape

    if two_level:
        far = lax.axis_index("far")
        near = energies // fars
        halves = side // LANES
        project_near = lax.dynamic_slice_in_dim(project, far * near, near, 1)
        basis_near = lax.dynamic_slice_in_dim(absorption_templates, far * near, near, 1).T
        far = far.astype(jnp.int32)[None]
        out, coefs = None, []
        later, project_near, basis_near = lax.optimization_barrier(
            (stepped[1], project_near, basis_near)
        )
        got = [lax.all_to_all(x, ("cube", "ta"), 0, 0, tiled=True) for x in (stepped[0], later)]
        for part in range(2):
            mine = partial_coefs(project_near, got[part].reshape(-1, LANES), fars, halves)
            theirs = lax.ppermute(mine, "far", swap)
            coef, fit = fitted_values(far, mine, theirs, basis_near, pix)
            coefs.append(coef)
            back = lax.all_to_all(
                fit.reshape(cube, local_energies, fars, pix // LANES, LANES), "cube", 0, 0, tiled=True
            )
            out = gather_part(part, back, out)
        return (out.reshape(2, local_energies, blocks, 1, pix), jnp.stack(coefs))

    flat = jnp.stack([x.transpose(1, 0, 2, 4, 3, 5) for x in stepped])
    if divided:
        flat = flat.reshape(2, n_e, blocks * tiles, pix)
        got = lax.all_to_all(flat, ("far", "cube", "ta"), 2, 1, tiled=True)
    else:
        flat = flat.reshape(2, n_e, blocks, tiles, pix)
        flat = lax.dynamic_index_in_dim(flat, tile, 3, keepdims=False)
        got = lax.all_to_all(flat, ("far", "cube"), 2, 1, tiled=True)
    values = got.reshape(2, -1, pix)
    coefs = jnp.einsum("ke,cen->ckn", project, values, precision=HIGHEST)
    fitted_here = jnp.einsum("ke,ckn->cen", absorption_templates, coefs, precision=HIGHEST)
    returned = lax.all_to_all(
        fitted_here[:, :, None, :], ("far", "cube"), split_axis=1, concat_axis=2, tiled=True
    )
    return (returned[:, :, :, None, :], coefs)


def solution(mesh):
    blocks, tiles = mesh.shape["ea"], mesh.shape["ta"]
    mesh = Mesh(mesh.devices.reshape(2, blocks // 2, tiles), ("far", "cube", "ta"))
    ea = ("far", "cube")
    in_specs = (
        P(ea, None, None),
        P(ea, None, None),
        P(ea, None, None, None),
        P(ea, None, None, None),
        P(ea, "ta", None, None, None),
        P(ea, "ta", None, None),
        P(ea, "ta"),
        P(),
    )
    out_specs = (P(None, ea, None, "ta", None), P(None, None, (*ea, "ta")))
    return jax.shard_map(local, mesh=mesh, in_specs=in_specs, out_specs=out_specs, check_vma=False)
```

```python
import functools

import jax
import jax.numpy as jnp
import numpy as np
from jax import lax
from jax.experimental import pallas as pl
from jax.experimental.pallas import tpu as pltpu
from jax.sharding import Mesh
from jax.sharding import PartitionSpec as P

HIGHEST = lax.Precision.HIGHEST
FLOOR_POWER = 0.5
REGULARIZER = 1.0
LANES = 128
SUBS = 8
SMALL = 12 << 20
LARGE = 52 << 20


def split_bf16(x):
    hi = x.astype(jnp.bfloat16)
    lo = (x - hi.astype(jnp.float32)).astype(jnp.bfloat16)
    return hi, lo


def transform_tables(width):
    fold = LANES // width
    i = np.arange(LANES) // width
    k = np.arange(LANES) % width
    phase = np.outer(i, i) / fold + np.outer(k, k) / width
    m = np.exp(-2j * np.pi * phase) / width
    real = np.block([[m.real, m.imag], [-m.imag, m.real]])
    q = np.arange(SUBS)
    tw = np.exp(-2j * np.pi * np.outer(q, i) / width)
    tw = np.concatenate([tw.real, tw.imag]).astype(np.float32)

    def halves(a):
        hi = a.astype(jnp.bfloat16)
        lo = (a - hi.astype(np.float64)).astype(jnp.bfloat16)
        return np.concatenate([hi, hi, lo])

    return halves(real), halves(real.T.copy()), tw


def fft8(re, im, sign):
    def butterfly(a, b):
        return (a[0] + b[0], a[1] + b[1]), (a[0] - b[0], a[1] - b[1])

    def turn(a):
        return (-a[1], a[0]) if sign > 0 else (a[1], -a[0])

    h = np.float32(np.sqrt(0.5))

    def eighth(a):
        if sign > 0:
            return ((a[0] - a[1]) * h, (a[0] + a[1]) * h)
        return ((a[0] + a[1]) * h, (a[1] - a[0]) * h)

    def fft4(x):
        s0, d0 = butterfly(x[0], x[2])
        s1, d1 = butterfly(x[1], x[3])
        d1 = turn(d1)
        y0, y2 = butterfly(s0, s1)
        y1, y3 = butterfly(d0, d1)
        return [y0, y1, y2, y3]

    x = list(zip(re, im))
    e = fft4(x[0::2])
    o = fft4(x[1::2])
    o = [o[0], eighth(o[1]), turn(o[2]), turn(eighth(o[3]))]
    pairs = [butterfly(e[n], o[n]) for n in range(4)]
    out = [p[0] for p in pairs] + [p[1] for p in pairs]
    return [y[0] for y in out], [y[1] for y in out]


def step_kernel(
    n_e, spots, used, modes, width, dests, tiles,
    table_ref,
    o_re, o_im, pr_hbm, pi_hbm, own_rec, par_rec, wf_hbm, wb_hbm, tw_hbm,
    *refs,
):
    outs = refs[:dests], refs[dests:2 * dests]
    (
        obj, rec, beam, probe, wf_ref, wb_ref, tw_ref, patch, term, root, work,
        sum_re, sum_im, sum_light, stage, obj_sem, rec_sem, shared_sem, out_sem,
    ) = refs[2 * dests:]
    fold = LANES // width
    groups = used // SUBS
    per_group = modes * SUBS
    per_q = groups * per_group
    side = obj.shape[3]
    lead = table_ref[0] >> (2 * side.bit_length() - 2 + spots.bit_length())
    local = o_re.shape[0]
    first, me = lead & (local - 1), lead >> (local.bit_length() - 1)
    sums = (sum_re, sum_im, sum_light)

    def in_copies(e):
        return [
            pltpu.make_async_copy(
                ref.at[first + e, :, pl.ds(h * LANES, LANES)], obj.at[e, c, h], obj_sem.at[e, c, h]
            )
            for c, ref in enumerate((o_re, o_im))
            for h in range(2)
        ] + [
            pltpu.make_async_copy(own_rec.at[first + e], rec.at[e, pl.ds(0, spots)], rec_sem.at[e, 0]),
            pltpu.make_async_copy(par_rec.at[e], rec.at[e, pl.ds(spots, spots)], rec_sem.at[e, 1]),
        ]

    out_copies = [
        pltpu.make_async_copy(stage.at[c, d], outs[c][d], out_sem.at[c, d])
        for c in range(2)
        for d in range(dests)
    ]

    shared = [
        pltpu.make_async_copy(src, dst, shared_sem.at[n])
        for n, (src, dst) in enumerate(
            (
                (pr_hbm.at[pl.ds(first, n_e)], beam.at[0]),
                (pi_hbm.at[pl.ds(first, n_e)], beam.at[1]),
                (tw_hbm, tw_ref),
                (wf_hbm, wf_ref),
                (wb_hbm, wb_ref),
            )
        )
    ]
    for c in in_copies(0) + shared:
        c.start()
    lane = lax.broadcasted_iota(jnp.int32, (SUBS, LANES), 1)
    block = lane // width
    for c in shared:
        c.wait()

    def place(e, index):
        packed = table_ref[e * used + index]
        shift = side.bit_length() - 1
        return (packed >> (2 * shift)) & (2 * spots - 1), (packed >> shift) & (side - 1), packed & (side - 1)

    def merge(parts):
        out = parts[0]
        for n in range(1, fold):
            out = jnp.where(block == n, parts[n], out)
        return out

    def row_of(ref, *index):
        return jnp.broadcast_to(ref[index], (SUBS, LANES))

    def product(x, w_ref):
        hi, lo = split_bf16(x)
        wide = jnp.concatenate([hi, lo, hi], axis=1)
        return jnp.dot(wide, w_ref[...], preferred_element_type=jnp.float32)

    def energy(e, carry):
        for acc in sums:
            acc[...] = jnp.zeros_like(acc)
        for c in in_copies(e):
            c.wait()

        @pl.when(e + 1 < n_e)
        def _():
            for c in in_copies(e + 1):
                c.start()

        for c in range(2):
            for m in range(modes):
                probe[c, m] = jnp.concatenate(
                    [beam[c, e, m, pl.ds(i, SUBS, stride=fold), :] for i in range(fold)], axis=1
                )
        for s in range(used):
            slot, row, col = place(e, s)
            low = lane >= col
            for c in range(2):
                parts = []
                for i in range(fold):
                    at = pl.ds(row + i, SUBS, stride=fold)
                    v = jnp.where(low, obj[e, c, 0, at, :], obj[e, c, 1, at, :])
                    parts.append(pltpu.roll(v, (i * width - col) & (LANES - 1), 1))
                patch[c, s * SUBS:(s + 1) * SUBS, :] = merge(parts)
            root[s * SUBS:(s + 1) * SUBS, :] = jnp.concatenate(
                [rec[e, slot, r * SUBS:(r + 1) * SUBS, :] for r in range(fold)], axis=1
            )

        for g in range(groups):
            base = g * SUBS * SUBS
            ats = [pl.ds(base + t, SUBS, stride=SUBS) for t in range(SUBS)]
            w_re = [patch[0, at, :] for at in ats]
            w_im = [patch[1, at, :] for at in ats]
            for m in range(modes):
                x_re, x_im = [], []
                for t in range(SUBS):
                    p_re = row_of(probe, 0, m, pl.ds(t, 1), slice(None))
                    p_im = row_of(probe, 1, m, pl.ds(t, 1), slice(None))
                    x_re.append(p_re * w_re[t] - p_im * w_im[t])
                    x_im.append(p_re * w_im[t] + p_im * w_re[t])
                y_re, y_im = fft8(x_re, x_im, -1)
                for q in range(SUBS):
                    a, b = y_re[q], y_im[q]
                    if q:
                        c = row_of(tw_ref, pl.ds(q, 1), slice(None))
                        d = row_of(tw_ref, pl.ds(SUBS + q, 1), slice(None))
                        a, b = a * c - b * d, a * d + b * c
                    to = q * per_q + g * per_group + m * SUBS
                    work[to:to + SUBS, 0:LANES] = a
                    work[to:to + SUBS, LANES:2 * LANES] = b

        for part in range(2):
            qs = range(part * SUBS // 2, (part + 1) * SUBS // 2)
            rows = slice(qs[0] * per_q, (qs[-1] + 1) * per_q)
            z = product(work[rows, :], wf_ref)
            scaled = []
            for q in qs:
                for g in range(groups):
                    f = []
                    for m in range(modes):
                        at = (q - qs[0]) * per_q + g * per_group + m * SUBS
                        f.append((z[at:at + SUBS, 0:LANES], z[at:at + SUBS, LANES:2 * LANES]))
                    power = f[0][0] * f[0][0] + f[0][1] * f[0][1]
                    for a, b in f[1:]:
                        power = power + a * a + b * b
                    measured = root[pl.ds(g * SUBS * SUBS + q, SUBS, stride=SUBS), :]
                    factor = 1.0 - jnp.sqrt(measured) * lax.rsqrt(jnp.maximum(power, FLOOR_POWER))
                    scaled += [
                        jnp.concatenate([a * factor, b * factor], axis=1) for a, b in f
                    ]
            work[rows, :] = product(jnp.concatenate(scaled, axis=0), wb_ref)

        light = jnp.zeros((SUBS, LANES), jnp.float32)
        for m in range(modes):
            a, b = probe[0, m], probe[1, m]
            light = light + a * a + b * b

        for g in range(groups):
            t_re = [None] * SUBS
            t_im = [None] * SUBS
            for m in range(modes):
                x_re, x_im = [], []
                for q in range(SUBS):
                    frm = q * per_q + g * per_group + m * SUBS
                    a, b = work[frm:frm + SUBS, 0:LANES], work[frm:frm + SUBS, LANES:2 * LANES]
                    if q:
                        c = row_of(tw_ref, pl.ds(q, 1), slice(None))
                        d = row_of(tw_ref, pl.ds(SUBS + q, 1), slice(None))
                        a, b = a * c + b * d, b * c - a * d
                    x_re.append(a)
                    x_im.append(b)
                y_re, y_im = fft8(x_re, x_im, 1)
                for t in range(SUBS):
                    p_re = row_of(probe, 0, m, pl.ds(t, 1), slice(None))
                    p_im = row_of(probe, 1, m, pl.ds(t, 1), slice(None))
                    a = p_re * y_re[t] + p_im * y_im[t]
                    b = p_re * y_im[t] - p_im * y_re[t]
                    t_re[t] = a if m == 0 else t_re[t] + a
                    t_im[t] = b if m == 0 else t_im[t] + b
            for t in range(SUBS):
                at = pl.ds(g * SUBS * SUBS + t, SUBS, stride=SUBS)
                term[0, at, :] = t_re[t]
                term[1, at, :] = t_im[t]

        for s in range(used):
            _, row, col = place(e, s)
            frm = slice(s * SUBS, (s + 1) * SUBS)
            terms = (term[0, frm, :], term[1, frm, :], light)
            which = jnp.where(col <= LANES - width, 0, jnp.where(col >= LANES, 1, 2))
            start = jnp.where(col <= LANES - width, col, jnp.where(col >= LANES, col - LANES, col - LANES // 2))
            inside = (lane >= start) & (lane < start + width)
            ats = [pl.ds(row + i, SUBS, stride=fold) for i in range(fold)]
            for acc, t in zip(sums, terms):
                new = []
                for i in range(fold):
                    v = pltpu.roll(t, (start - i * width) & (LANES - 1), 1)
                    new.append(acc[which, ats[i], :] + jnp.where(inside, v, 0.0))
                for i in range(fold):
                    acc[which, ats[i], :] = new[i]

        high = lane >= LANES // 2

        def finish(k, carry):
            for u in range(SUBS):
                n = k * SUBS + u
                at = pl.ds(pl.multiple_of(n * SUBS, SUBS), SUBS)
                t, rest = n & (tiles - 1), n >> (tiles.bit_length() - 1)
                dest = (rest & (dests - 1)) ^ me
                to = (rest >> (dests.bit_length() - 1)) * tiles + t
                mid = [pltpu.roll(acc[2, at, :], LANES // 2, 1) for acc in sums]
                for h in range(2):
                    mine = high if h == 0 else ~high
                    full = [acc[h, at, :] + jnp.where(mine, m, 0.0) for acc, m in zip(sums, mid)]
                    share = 1.0 / (full[2] + REGULARIZER)
                    for c in range(2):
                        stage[c, dest, e, to, h] = obj[e, c, h, at, :] - full[c] * share
            return carry

        lax.fori_loop(0, side // SUBS // SUBS, finish, 0)
        return carry

    lax.fori_loop(0, n_e, energy, 0)
    for c in out_copies:
        c.start()
    for c in out_copies:
        c.wait()


def gradient_step(objects, beams, own_rec, par_rec, table, n_e, used, dests, tiles):
    o_re, o_im = objects
    local, side, _ = o_re.shape
    modes, width = beams[0].shape[1], beams[0].shape[-1]
    spots = own_rec.shape[1]
    flat = width * width // LANES
    assert flat == SUBS and side == 2 * LANES and used % SUBS == 0
    wf, wb, tw = transform_tables(width)
    hbm = pl.BlockSpec(memory_space=pl.ANY)
    out_shape = (n_e, side // SUBS // dests, side // LANES, SUBS, LANES)
    return pl.pallas_call(
        functools.partial(step_kernel, n_e, spots, used, modes, width, dests, tiles),
        out_shape=[jax.ShapeDtypeStruct(out_shape, jnp.float32)] * (2 * dests),
        grid_spec=pltpu.PrefetchScalarGridSpec(
            num_scalar_prefetch=1,
            grid=(1,),
            in_specs=[hbm] * 9,
            out_specs=[hbm] * (2 * dests),
            scratch_shapes=[
                pltpu.VMEM((n_e, 2, 2, side, LANES), jnp.float32),
                pltpu.VMEM((n_e, 2 * spots, width, width), jnp.float32),
                pltpu.VMEM((2, n_e, modes, width, width), jnp.float32),
                pltpu.VMEM((2, modes, flat, LANES), jnp.float32),
                *[pltpu.VMEM(wf.shape, jnp.bfloat16)] * 2,
                pltpu.VMEM(tw.shape, jnp.float32),
                pltpu.VMEM((2, used * SUBS, LANES), jnp.float32),
                pltpu.VMEM((2, used * SUBS, LANES), jnp.float32),
                pltpu.VMEM((used * SUBS, LANES), jnp.float32),
                pltpu.VMEM((SUBS * used * modes, 2 * LANES), jnp.float32),
                *[pltpu.VMEM((3, side, LANES), jnp.float32)] * 3,
                pltpu.VMEM((2, dests, *out_shape), jnp.float32),
                pltpu.SemaphoreType.DMA((n_e, 2, 2)),
                pltpu.SemaphoreType.DMA((n_e, 2)),
                pltpu.SemaphoreType.DMA((5,)),
                pltpu.SemaphoreType.DMA((2, dests)),
            ],
        ),
        compiler_params=pltpu.CompilerParams(vmem_limit_bytes=LARGE),
        name="gradient_step",
    )(
        table, o_re, o_im, *beams, own_rec, par_rec,
        jnp.asarray(wf), jnp.asarray(wb), jnp.asarray(tw),
    )


def slot_table(corners, theirs, counts, first, n_e, side, me):
    local, spots, _ = corners.shape
    lead = me * local + first
    assert local & (local - 1) == 0
    used = spots * 3 // 2
    assert side & (side - 1) == 0 and spots & (spots - 1) == 0
    both = jnp.concatenate([corners, theirs], axis=1)
    both = lax.dynamic_slice_in_dim(both, first, n_e, 0)
    counts = lax.dynamic_slice_in_dim(counts, first, n_e, 0)
    both = both[..., 0] * side + both[..., 1]
    both = both + (lead * 2 * spots + jnp.arange(2 * spots, dtype=jnp.int32)) * (side * side)
    index = jnp.arange(used, dtype=jnp.int32)[None]
    index = index + jnp.where(index < counts, 0, spots - counts)
    chosen = index[:, :, None] == jnp.arange(2 * spots, dtype=jnp.int32)
    return jnp.sum(jnp.where(chosen, both[:, None, :], 0), axis=2).reshape(-1)


def dot3(a, b):
    ah, al = split_bf16(a)
    bh, bl = split_bf16(b)
    left = jnp.concatenate([ah, al, ah], axis=1)
    right = jnp.concatenate([bh, bh, bl], axis=0)
    return jnp.dot(left, right, preferred_element_type=jnp.float32)


def solve_kernel(fars, cube, n_e, where_ref, basis_ref, project_ref, fit_ref):
    basis = basis_ref[...]
    edges, energies = basis.shape
    dot = functools.partial(lax.dot_general, precision=HIGHEST, preferred_element_type=jnp.float32)
    gram = dot(basis, basis, (((1,), (1,)), ((), ())))
    row = lax.broadcasted_iota(jnp.int32, (edges, 1), 0)
    right = basis
    for k in range(edges):
        pivot = 1.0 / gram[k:k + 1, k:k + 1]
        line, rhs = gram[k:k + 1, :] * pivot, right[k:k + 1, :] * pivot
        column = gram[:, k:k + 1]
        gram = jnp.where(row == k, line, gram - column * line)
        right = jnp.where(row == k, rhs, right - column * rhs)
    far, me, tile = where_ref[0], where_ref[1], where_ref[2]
    both = 2 * n_e

    def chosen(shape, axis, per, offset):
        n = lax.broadcasted_iota(jnp.int32, shape, axis)
        chip = (n // per) ^ me
        energy = far * (energies // fars) + chip * both + offset + n % per
        return (energy == lax.broadcasted_iota(jnp.int32, shape, 1 - axis)).astype(jnp.float32)

    project_ref[...] = dot(
        right, chosen((energies, cube * n_e), 1, n_e, tile * n_e), (((1,), (0,)), ((), ()))
    )
    fit_ref[...] = dot(
        chosen((cube * both, energies), 0, both, 0), basis, (((1,), (1,)), ((), ()))
    )


def solve_templates(where, basis, fars, cube, n_e):
    edges, energies = basis.shape
    vmem = pl.BlockSpec(memory_space=pltpu.VMEM)
    return pl.pallas_call(
        functools.partial(solve_kernel, fars, cube, n_e),
        out_shape=[
            jax.ShapeDtypeStruct((edges, cube * n_e), jnp.float32),
            jax.ShapeDtypeStruct((cube * 2 * n_e, edges), jnp.float32),
        ],
        in_specs=[pl.BlockSpec(memory_space=pltpu.SMEM), vmem],
        out_specs=[vmem] * 2,
        compiler_params=pltpu.CompilerParams(vmem_limit_bytes=SMALL),
        name="solve_templates",
    )(where, basis)


def project_kernel(fars, tiles, tile_ref, project_ref, *refs):
    *got, own_ref, other_ref, held = refs
    rows = got[0].shape[0]
    for d, ref in enumerate(got):
        held[d * rows:(d + 1) * rows, :] = ref[...]
    energies = project_ref.shape[1]
    stride = held.shape[0] // energies
    halves = stride // (fars * tiles * SUBS)
    for away, out_ref in enumerate((other_ref, own_ref)):
        tile = tile_ref[0] if away else 1 - tile_ref[0]
        for f in range(fars):
            for r in range(SUBS):
                parts = [
                    held[pl.ds(((f * tiles + tile) * halves + h) * SUBS + r, energies, stride=stride), :]
                    for h in range(halves)
                ]
                at = (f * SUBS + r) * halves * LANES
                values = jnp.concatenate(parts, axis=1)
                out_ref[:, at:at + halves * LANES] = dot3(project_ref[...], values)


def partial_coefs(tile, project, got, fars, tiles):
    rows = got[0].shape[0] * len(got)
    edges, energies = project.shape
    pixels = rows // energies // tiles * LANES
    vmem = pl.BlockSpec(memory_space=pltpu.VMEM)
    return pl.pallas_call(
        functools.partial(project_kernel, fars, tiles),
        out_shape=[jax.ShapeDtypeStruct((edges, pixels), jnp.float32)] * 2,
        in_specs=[pl.BlockSpec(memory_space=pltpu.SMEM)] + [vmem] * (1 + len(got)),
        out_specs=[vmem] * 2,
        scratch_shapes=[pltpu.VMEM((rows, LANES), jnp.float32)],
        cost_estimate=pl.CostEstimate(
            flops=6 * edges * energies * pixels, bytes_accessed=rows * LANES * 4, transcendentals=0
        ),
        compiler_params=pltpu.CompilerParams(vmem_limit_bytes=SMALL),
        name="partial_coefs",
    )(tile, project, *got)


def fit_kernel(far_ref, mine_ref, theirs_ref, basis_ref, coef_ref, *fit):
    own = coef_ref.shape[1]
    per = basis_ref.shape[0] // len(fit)
    stride = fit[0].shape[0] // per
    at = pl.ds(pl.multiple_of(far_ref[0] * own, own), own)
    coef_ref[...] = mine_ref[:, at] + theirs_ref[:, at]
    wide = 2 * LANES
    for j in range(mine_ref.shape[1] // wide):
        cols = slice(j * wide, (j + 1) * wide)
        values = dot3(basis_ref[...], mine_ref[:, cols] + theirs_ref[:, cols])
        for d, ref in enumerate(fit):
            for u in range(2):
                ref[pl.ds(j * 2 + u, per, stride=stride), :] = values[
                    d * per:(d + 1) * per, u * LANES:(u + 1) * LANES
                ]


def fitted_values(far, mine, theirs, basis, own, dests):
    edges, pixels = mine.shape
    energies = basis.shape[0]
    vmem = pl.BlockSpec(memory_space=pltpu.VMEM)
    rows = energies // dests * pixels // LANES
    out = pl.pallas_call(
        fit_kernel,
        out_shape=[jax.ShapeDtypeStruct((edges, own), jnp.float32)]
        + [jax.ShapeDtypeStruct((rows, LANES), jnp.float32)] * dests,
        in_specs=[pl.BlockSpec(memory_space=pltpu.SMEM), vmem, vmem, vmem],
        out_specs=[vmem] * (1 + dests),
        cost_estimate=pl.CostEstimate(
            flops=6 * edges * energies * pixels, bytes_accessed=energies * pixels * 4, transcendentals=0
        ),
        compiler_params=pltpu.CompilerParams(vmem_limit_bytes=SMALL),
        name="fitted_values",
    )(far, mine, theirs, basis)
    return out[0], out[1:]


def gather_kernel(part, senders, me_ref, *refs):
    got, (out_ref, sem) = refs[:senders], refs[-2:]
    copies = [
        pltpu.make_async_copy(ref, out_ref.at[part, :, :, me_ref[0] ^ d], sem.at[d])
        for d, ref in enumerate(got)
    ]
    for c in copies:
        c.start()
    for c in copies:
        c.wait()


def gather_part(part, me, got, out):
    senders = len(got)
    energies, fars, subs, _ = got[0].shape
    shape = (2, energies, fars, senders, subs, LANES)
    hbm = pl.BlockSpec(memory_space=pl.ANY)
    return pl.pallas_call(
        functools.partial(gather_kernel, part, senders),
        out_shape=jax.ShapeDtypeStruct(shape, jnp.float32),
        in_specs=[pl.BlockSpec(memory_space=pltpu.SMEM)]
        + [pl.BlockSpec(memory_space=pltpu.VMEM)] * senders
        + ([] if out is None else [hbm]),
        out_specs=hbm,
        scratch_shapes=[pltpu.SemaphoreType.DMA((senders,))],
        input_output_aliases={} if out is None else {1 + senders: 0},
        compiler_params=pltpu.CompilerParams(vmem_limit_bytes=SMALL),
        name="gather_part",
    )(me, *got, *([] if out is None else [out]))


def exchange(blocks, cube):
    return [
        b if d == 0 else lax.ppermute(b, "cube", [(i, i ^ d) for i in range(cube)])
        for d, b in enumerate(blocks)
    ]


def local(
    sample_inphase,
    sample_quadrature,
    beam_inphase,
    beam_quadrature,
    recorded_diffraction,
    window_corners,
    filled_tallies,
    absorption_templates,
):
    local_energies = sample_inphase.shape[0]
    side = sample_inphase.shape[1]
    spots = recorded_diffraction.shape[2]
    fars = lax.axis_size("far")
    cube = lax.axis_size("cube")
    blocks = fars * cube
    tiles = lax.axis_size("ta")
    tile = lax.axis_index("ta")
    swap = [(0, 1), (1, 0)]
    assert tiles == 2 and fars == 2
    used = spots * 3 // 2
    divided = local_energies % tiles == 0
    n_e = local_energies // tiles if divided else local_energies
    pix = side * side // (blocks * tiles)
    two_level = divided and pix == SUBS * side and local_energies == SUBS and cube & (cube - 1) == 0
    own_rec = recorded_diffraction[:, 0]
    first = tile * n_e if divided else jnp.zeros((), jnp.int32)
    theirs = lax.ppermute(window_corners, "ta", swap)
    give = lax.dynamic_slice_in_dim(own_rec, (1 - tile) * n_e, n_e, 0) if divided else own_rec
    par_rec = lax.ppermute(give, "ta", swap)
    table = slot_table(
        window_corners[:, 0], theirs[:, 0], filled_tallies, first.astype(jnp.int32), n_e, side,
        lax.axis_index("cube").astype(jnp.int32) if two_level else 0,
    )
    stepped = gradient_step(
        (sample_inphase, sample_quadrature),
        (beam_inphase, beam_quadrature),
        own_rec,
        par_rec,
        table,
        n_e,
        used,
        cube if two_level else 1,
        tiles,
    )

    if two_level:
        far = lax.axis_index("far").astype(jnp.int32)
        me = lax.axis_index("cube").astype(jnp.int32)
        where = jnp.stack([far, me, tile.astype(jnp.int32)])
        project_near, basis_near = solve_templates(where, absorption_templates, fars, cube, n_e)
        out, coefs = None, []
        parts = stepped[:cube], stepped[cube:]
        got = [exchange(blocks, cube) for blocks in parts]
        for part in range(2):
            blocks = [x.reshape(-1, LANES) for x in got[part]]
            kept, given = partial_coefs(tile.astype(jnp.int32)[None], project_near, blocks, fars, tiles)
            share = kept + lax.ppermute(given, "ta", swap)
            theirs = lax.ppermute(share, "far", swap)
            coef, fit = fitted_values(far[None], share, theirs, basis_near, pix, cube)
            coefs.append(coef)
            back = exchange(
                [x.reshape(local_energies, fars, pix // LANES, LANES) for x in fit], cube
            )
            out = gather_part(part, me[None], back, out)
        return (out.reshape(2, local_energies, cube * fars, 1, pix), jnp.stack(coefs))

    gram = jnp.dot(absorption_templates, absorption_templates.T, precision=HIGHEST)
    factor_low = jnp.linalg.cholesky(gram)
    project = jax.scipy.linalg.cho_solve((factor_low, True), absorption_templates)
    flat = jnp.stack([x.transpose(0, 1, 3, 2, 4) for x in stepped])
    if divided:
        flat = flat.reshape(2, n_e, blocks * tiles, pix)
        got = lax.all_to_all(flat, ("far", "cube", "ta"), 2, 1, tiled=True)
    else:
        flat = flat.reshape(2, n_e, blocks, tiles, pix)
        flat = lax.dynamic_index_in_dim(flat, tile, 3, keepdims=False)
        got = lax.all_to_all(flat, ("far", "cube"), 2, 1, tiled=True)
    values = got.reshape(2, -1, pix)
    coefs = jnp.einsum("ke,cen->ckn", project, values, precision=HIGHEST)
    fitted_here = jnp.einsum("ke,ckn->cen", absorption_templates, coefs, precision=HIGHEST)
    returned = lax.all_to_all(
        fitted_here[:, :, None, :], ("far", "cube"), split_axis=1, concat_axis=2, tiled=True
    )
    return (returned[:, :, :, None, :], coefs)


def solution(mesh):
    blocks, tiles = mesh.shape["ea"], mesh.shape["ta"]
    mesh = Mesh(mesh.devices.reshape(2, blocks // 2, tiles), ("far", "cube", "ta"))
    ea = ("far", "cube")
    in_specs = (
        P(ea, None, None),
        P(ea, None, None),
        P(ea, None, None, None),
        P(ea, None, None, None),
        P(ea, "ta", None, None, None),
        P(ea, "ta", None, None),
        P(ea, "ta"),
        P(),
    )
    out_specs = (P(None, ea, None, "ta", None), P(None, None, (*ea, "ta")))
    return jax.shard_map(local, mesh=mesh, in_specs=in_specs, out_specs=out_specs, check_vma=False)
```

```python
import functools

import jax
import jax.numpy as jnp
import numpy as np
from jax import lax
from jax.experimental import pallas as pl
from jax.experimental.pallas import tpu as pltpu
from jax.sharding import Mesh
from jax.sharding import PartitionSpec as P

HIGHEST = lax.Precision.HIGHEST
FLOOR_POWER = 0.5
REGULARIZER = 1.0
LANES = 128
SUBS = 8
SMALL = 12 << 20
LARGE = 50 << 20


def split_bf16(x):
    hi = x.astype(jnp.bfloat16)
    lo = (x - hi.astype(jnp.float32)).astype(jnp.bfloat16)
    return hi, lo


def transform_tables(width):
    fold = LANES // width
    i = np.arange(LANES) // width
    k = np.arange(LANES) % width
    phase = np.outer(i, i) / fold + np.outer(k, k) / width
    m = np.exp(-2j * np.pi * phase) / width
    real = np.block([[m.real, m.imag], [-m.imag, m.real]])
    q = np.arange(SUBS)
    tw = np.exp(-2j * np.pi * np.outer(q, i) / width)
    tw = np.concatenate([tw.real, tw.imag]).astype(np.float32)

    def halves(a):
        hi = a.astype(jnp.bfloat16)
        lo = (a - hi.astype(np.float64)).astype(jnp.bfloat16)
        return np.concatenate([hi, hi, lo])

    return halves(real), halves(real.T.copy()), tw


def fft8(re, im, sign):
    def butterfly(a, b):
        return (a[0] + b[0], a[1] + b[1]), (a[0] - b[0], a[1] - b[1])

    def turn(a):
        return (-a[1], a[0]) if sign > 0 else (a[1], -a[0])

    h = np.float32(np.sqrt(0.5))

    def eighth(a):
        if sign > 0:
            return ((a[0] - a[1]) * h, (a[0] + a[1]) * h)
        return ((a[0] + a[1]) * h, (a[1] - a[0]) * h)

    def fft4(x):
        s0, d0 = butterfly(x[0], x[2])
        s1, d1 = butterfly(x[1], x[3])
        d1 = turn(d1)
        y0, y2 = butterfly(s0, s1)
        y1, y3 = butterfly(d0, d1)
        return [y0, y1, y2, y3]

    x = list(zip(re, im))
    e = fft4(x[0::2])
    o = fft4(x[1::2])
    o = [o[0], eighth(o[1]), turn(o[2]), turn(eighth(o[3]))]
    pairs = [butterfly(e[n], o[n]) for n in range(4)]
    out = [p[0] for p in pairs] + [p[1] for p in pairs]
    return [y[0] for y in out], [y[1] for y in out]


def step_kernel(
    n_e, spots, used, modes, width, dests, tiles,
    table_ref,
    o_re, o_im, pr_hbm, pi_hbm, own_rec, par_rec, wf_hbm, wb_hbm, tw_hbm,
    *refs,
):
    outs = refs[:dests], refs[dests:2 * dests]
    (
        obj, rec, beam, probe, wf_ref, wb_ref, tw_ref, patch, term, root, work,
        sum_re, sum_im, sum_light, stage, obj_sem, rec_sem, shared_sem, out_sem,
    ) = refs[2 * dests:]
    fold = LANES // width
    groups = used // SUBS
    per_group = modes * SUBS
    per_q = groups * per_group
    side = obj.shape[3]
    lead = table_ref[0] >> (2 * side.bit_length() - 2 + spots.bit_length())
    local = o_re.shape[0]
    first, me = lead & (local - 1), lead >> (local.bit_length() - 1)
    sums = (sum_re, sum_im, sum_light)

    def in_copies(e):
        return [
            pltpu.make_async_copy(
                ref.at[first + e, :, pl.ds(h * LANES, LANES)], obj.at[e, c, h], obj_sem.at[e, c, h]
            )
            for c, ref in enumerate((o_re, o_im))
            for h in range(2)
        ] + [
            pltpu.make_async_copy(own_rec.at[first + e], rec.at[e, pl.ds(0, spots)], rec_sem.at[e, 0]),
            pltpu.make_async_copy(par_rec.at[e], rec.at[e, pl.ds(spots, spots)], rec_sem.at[e, 1]),
        ]

    out_copies = [
        pltpu.make_async_copy(stage.at[c, d], outs[c][d], out_sem.at[c, d])
        for c in range(2)
        for d in range(dests)
    ]

    shared = [
        pltpu.make_async_copy(src, dst, shared_sem.at[n])
        for n, (src, dst) in enumerate(
            (
                (pr_hbm.at[pl.ds(first, n_e)], beam.at[0]),
                (pi_hbm.at[pl.ds(first, n_e)], beam.at[1]),
                (tw_hbm, tw_ref),
                (wf_hbm, wf_ref),
                (wb_hbm, wb_ref),
            )
        )
    ]
    for c in in_copies(0) + shared:
        c.start()
    lane = lax.broadcasted_iota(jnp.int32, (SUBS, LANES), 1)
    block = lane // width
    for c in shared:
        c.wait()

    def place(e, index):
        packed = table_ref[e * used + index]
        shift = side.bit_length() - 1
        return (packed >> (2 * shift)) & (2 * spots - 1), (packed >> shift) & (side - 1), packed & (side - 1)

    def merge(parts):
        out = parts[0]
        for n in range(1, fold):
            out = jnp.where(block == n, parts[n], out)
        return out

    def row_of(ref, *index):
        return jnp.broadcast_to(ref[index], (SUBS, LANES))

    def product(x, w_ref):
        hi, lo = split_bf16(x)
        wide = jnp.concatenate([hi, lo, hi], axis=1)
        return jnp.dot(wide, w_ref[...], preferred_element_type=jnp.float32)

    def energy(e, carry):
        for acc in sums:
            acc[...] = jnp.zeros_like(acc)
        for c in in_copies(e):
            c.wait()

        @pl.when(e + 1 < n_e)
        def _():
            for c in in_copies(e + 1):
                c.start()

        for c in range(2):
            for m in range(modes):
                probe[c, m] = jnp.concatenate(
                    [beam[c, e, m, pl.ds(i, SUBS, stride=fold), :] for i in range(fold)], axis=1
                )
        for s in range(used):
            slot, row, col = place(e, s)
            low = lane >= col
            for c in range(2):
                parts = []
                for i in range(fold):
                    at = pl.ds(row + i, SUBS, stride=fold)
                    v = jnp.where(low, obj[e, c, 0, at, :], obj[e, c, 1, at, :])
                    parts.append(pltpu.roll(v, (i * width - col) & (LANES - 1), 1))
                patch[c, s * SUBS:(s + 1) * SUBS, :] = merge(parts)
            root[s * SUBS:(s + 1) * SUBS, :] = jnp.concatenate(
                [rec[e, slot, r * SUBS:(r + 1) * SUBS, :] for r in range(fold)], axis=1
            )

        for g in range(groups):
            base = g * SUBS * SUBS
            ats = [pl.ds(base + t, SUBS, stride=SUBS) for t in range(SUBS)]
            w_re = [patch[0, at, :] for at in ats]
            w_im = [patch[1, at, :] for at in ats]
            for m in range(modes):
                x_re, x_im = [], []
                for t in range(SUBS):
                    p_re = row_of(probe, 0, m, pl.ds(t, 1), slice(None))
                    p_im = row_of(probe, 1, m, pl.ds(t, 1), slice(None))
                    x_re.append(p_re * w_re[t] - p_im * w_im[t])
                    x_im.append(p_re * w_im[t] + p_im * w_re[t])
                y_re, y_im = fft8(x_re, x_im, -1)
                for q in range(SUBS):
                    a, b = y_re[q], y_im[q]
                    if q:
                        c = row_of(tw_ref, pl.ds(q, 1), slice(None))
                        d = row_of(tw_ref, pl.ds(SUBS + q, 1), slice(None))
                        a, b = a * c - b * d, a * d + b * c
                    to = q * per_q + g * per_group + m * SUBS
                    work[to:to + SUBS, 0:LANES] = a
                    work[to:to + SUBS, LANES:2 * LANES] = b

        for part in range(2):
            qs = range(part * SUBS // 2, (part + 1) * SUBS // 2)
            rows = slice(qs[0] * per_q, (qs[-1] + 1) * per_q)
            z = product(work[rows, :], wf_ref)
            scaled = []
            for q in qs:
                for g in range(groups):
                    f = []
                    for m in range(modes):
                        at = (q - qs[0]) * per_q + g * per_group + m * SUBS
                        f.append((z[at:at + SUBS, 0:LANES], z[at:at + SUBS, LANES:2 * LANES]))
                    power = f[0][0] * f[0][0] + f[0][1] * f[0][1]
                    for a, b in f[1:]:
                        power = power + a * a + b * b
                    measured = root[pl.ds(g * SUBS * SUBS + q, SUBS, stride=SUBS), :]
                    factor = 1.0 - jnp.sqrt(measured) * lax.rsqrt(jnp.maximum(power, FLOOR_POWER))
                    scaled += [
                        jnp.concatenate([a * factor, b * factor], axis=1) for a, b in f
                    ]
            work[rows, :] = product(jnp.concatenate(scaled, axis=0), wb_ref)

        light = jnp.zeros((SUBS, LANES), jnp.float32)
        for m in range(modes):
            a, b = probe[0, m], probe[1, m]
            light = light + a * a + b * b

        for g in range(groups):
            t_re = [None] * SUBS
            t_im = [None] * SUBS
            for m in range(modes):
                x_re, x_im = [], []
                for q in range(SUBS):
                    frm = q * per_q + g * per_group + m * SUBS
                    a, b = work[frm:frm + SUBS, 0:LANES], work[frm:frm + SUBS, LANES:2 * LANES]
                    if q:
                        c = row_of(tw_ref, pl.ds(q, 1), slice(None))
                        d = row_of(tw_ref, pl.ds(SUBS + q, 1), slice(None))
                        a, b = a * c + b * d, b * c - a * d
                    x_re.append(a)
                    x_im.append(b)
                y_re, y_im = fft8(x_re, x_im, 1)
                for t in range(SUBS):
                    p_re = row_of(probe, 0, m, pl.ds(t, 1), slice(None))
                    p_im = row_of(probe, 1, m, pl.ds(t, 1), slice(None))
                    a = p_re * y_re[t] + p_im * y_im[t]
                    b = p_re * y_im[t] - p_im * y_re[t]
                    t_re[t] = a if m == 0 else t_re[t] + a
                    t_im[t] = b if m == 0 else t_im[t] + b
            for t in range(SUBS):
                at = pl.ds(g * SUBS * SUBS + t, SUBS, stride=SUBS)
                term[0, at, :] = t_re[t]
                term[1, at, :] = t_im[t]

        for s in range(used):
            _, row, col = place(e, s)
            frm = slice(s * SUBS, (s + 1) * SUBS)
            terms = (term[0, frm, :], term[1, frm, :], light)
            which = jnp.where(col <= LANES - width, 0, jnp.where(col >= LANES, 1, 2))
            start = jnp.where(col <= LANES - width, col, jnp.where(col >= LANES, col - LANES, col - LANES // 2))
            inside = (lane >= start) & (lane < start + width)
            ats = [pl.ds(row + i, SUBS, stride=fold) for i in range(fold)]
            for acc, t in zip(sums, terms):
                new = []
                for i in range(fold):
                    v = pltpu.roll(t, (start - i * width) & (LANES - 1), 1)
                    new.append(acc[which, ats[i], :] + jnp.where(inside, v, 0.0))
                for i in range(fold):
                    acc[which, ats[i], :] = new[i]

        high = lane >= LANES // 2

        def finish(k, carry):
            for u in range(SUBS):
                n = k * SUBS + u
                at = pl.ds(pl.multiple_of(n * SUBS, SUBS), SUBS)
                t, rest = n & (tiles - 1), n >> (tiles.bit_length() - 1)
                dest = (rest & (dests - 1)) ^ me
                to = (rest >> (dests.bit_length() - 1)) * tiles + t
                mid = [pltpu.roll(acc[2, at, :], LANES // 2, 1) for acc in sums]
                for h in range(2):
                    mine = high if h == 0 else ~high
                    full = [acc[h, at, :] + jnp.where(mine, m, 0.0) for acc, m in zip(sums, mid)]
                    share = 1.0 / (full[2] + REGULARIZER)
                    for c in range(2):
                        stage[c, dest, e, to, h] = obj[e, c, h, at, :] - full[c] * share
            return carry

        lax.fori_loop(0, side // SUBS // SUBS, finish, 0)
        return carry

    lax.fori_loop(0, n_e, energy, 0)
    for c in out_copies:
        c.start()
    for c in out_copies:
        c.wait()


def gradient_step(objects, beams, own_rec, par_rec, table, n_e, used, dests, tiles):
    o_re, o_im = objects
    _, side, _ = o_re.shape
    modes, width = beams[0].shape[1], beams[0].shape[-1]
    spots = own_rec.shape[1]
    flat = width * width // LANES
    assert flat == SUBS and side == 2 * LANES and used % SUBS == 0
    wf, wb, tw = transform_tables(width)
    hbm = pl.BlockSpec(memory_space=pl.ANY)
    out_shape = (n_e, side // SUBS // dests, side // LANES, SUBS, LANES)
    return pl.pallas_call(
        functools.partial(step_kernel, n_e, spots, used, modes, width, dests, tiles),
        out_shape=[jax.ShapeDtypeStruct(out_shape, jnp.float32)] * (2 * dests),
        grid_spec=pltpu.PrefetchScalarGridSpec(
            num_scalar_prefetch=1,
            grid=(1,),
            in_specs=[hbm] * 9,
            out_specs=[hbm] * (2 * dests),
            scratch_shapes=[
                pltpu.VMEM((n_e, 2, 2, side, LANES), jnp.float32),
                pltpu.VMEM((n_e, 2 * spots, width, width), jnp.float32),
                pltpu.VMEM((2, n_e, modes, width, width), jnp.float32),
                pltpu.VMEM((2, modes, flat, LANES), jnp.float32),
                *[pltpu.VMEM(wf.shape, jnp.bfloat16)] * 2,
                pltpu.VMEM(tw.shape, jnp.float32),
                pltpu.VMEM((2, used * SUBS, LANES), jnp.float32),
                pltpu.VMEM((2, used * SUBS, LANES), jnp.float32),
                pltpu.VMEM((used * SUBS, LANES), jnp.float32),
                pltpu.VMEM((SUBS * used * modes, 2 * LANES), jnp.float32),
                *[pltpu.VMEM((3, side, LANES), jnp.float32)] * 3,
                pltpu.VMEM((2, dests, *out_shape), jnp.float32),
                pltpu.SemaphoreType.DMA((n_e, 2, 2)),
                pltpu.SemaphoreType.DMA((n_e, 2)),
                pltpu.SemaphoreType.DMA((5,)),
                pltpu.SemaphoreType.DMA((2, dests)),
            ],
        ),
        compiler_params=pltpu.CompilerParams(vmem_limit_bytes=LARGE),
        name="gradient_step",
    )(
        table, o_re, o_im, *beams, own_rec, par_rec,
        jnp.asarray(wf), jnp.asarray(wb), jnp.asarray(tw),
    )


def slot_table(corners, theirs, counts, first, n_e, side, me):
    local, spots, _ = corners.shape
    lead = me * local + first
    assert local & (local - 1) == 0
    used = spots * 3 // 2
    assert side & (side - 1) == 0 and spots & (spots - 1) == 0
    both = jnp.concatenate([corners, theirs], axis=1)
    both = lax.dynamic_slice_in_dim(both, first, n_e, 0)
    counts = lax.dynamic_slice_in_dim(counts, first, n_e, 0)
    both = both[..., 0] * side + both[..., 1]
    both = both + (lead * 2 * spots + jnp.arange(2 * spots, dtype=jnp.int32)) * (side * side)
    index = jnp.arange(used, dtype=jnp.int32)[None]
    index = index + jnp.where(index < counts, 0, spots - counts)
    chosen = index[:, :, None] == jnp.arange(2 * spots, dtype=jnp.int32)
    return jnp.sum(jnp.where(chosen, both[:, None, :], 0), axis=2).reshape(-1)


def dot3(a, b):
    ah, al = split_bf16(a)
    bh, bl = split_bf16(b)
    left = jnp.concatenate([ah, al, ah], axis=1)
    right = jnp.concatenate([bh, bh, bl], axis=0)
    return jnp.dot(left, right, preferred_element_type=jnp.float32)


def solve_kernel(fars, cube, n_e, where_ref, basis_ref, project_ref, fit_ref):
    basis = basis_ref[...]
    edges, energies = basis.shape
    dot = functools.partial(lax.dot_general, precision=HIGHEST, preferred_element_type=jnp.float32)
    gram = dot(basis, basis, (((1,), (1,)), ((), ())))
    row = lax.broadcasted_iota(jnp.int32, (edges, 1), 0)
    right = basis
    for k in range(edges):
        pivot = 1.0 / gram[k:k + 1, k:k + 1]
        line, rhs = gram[k:k + 1, :] * pivot, right[k:k + 1, :] * pivot
        column = gram[:, k:k + 1]
        gram = jnp.where(row == k, line, gram - column * line)
        right = jnp.where(row == k, rhs, right - column * rhs)
    far, me, tile = where_ref[0], where_ref[1], where_ref[2]
    both = 2 * n_e

    def chosen(shape, axis, per, offset):
        n = lax.broadcasted_iota(jnp.int32, shape, axis)
        chip = (n // per) ^ me
        energy = far * (energies // fars) + chip * both + offset + n % per
        return (energy == lax.broadcasted_iota(jnp.int32, shape, 1 - axis)).astype(jnp.float32)

    project_ref[...] = dot(
        right, chosen((energies, cube * n_e), 1, n_e, tile * n_e), (((1,), (0,)), ((), ()))
    )
    fit_ref[...] = dot(
        chosen((cube * both, energies), 0, both, 0), basis, (((1,), (1,)), ((), ()))
    )


def solve_templates(where, basis, fars, cube, n_e):
    edges, _ = basis.shape
    vmem = pl.BlockSpec(memory_space=pltpu.VMEM)
    return pl.pallas_call(
        functools.partial(solve_kernel, fars, cube, n_e),
        out_shape=[
            jax.ShapeDtypeStruct((edges, cube * n_e), jnp.float32),
            jax.ShapeDtypeStruct((cube * 2 * n_e, edges), jnp.float32),
        ],
        in_specs=[pl.BlockSpec(memory_space=pltpu.SMEM), vmem],
        out_specs=[vmem] * 2,
        compiler_params=pltpu.CompilerParams(vmem_limit_bytes=SMALL),
        name="solve_templates",
    )(where, basis)


def project_kernel(fars, tiles, tile_ref, project_ref, *refs):
    *got, own_ref, other_ref, held = refs
    rows = got[0].shape[0]
    for d, ref in enumerate(got):
        held[d * rows:(d + 1) * rows, :] = ref[...]
    energies = project_ref.shape[1]
    stride = held.shape[0] // energies
    halves = stride // (fars * tiles * SUBS)
    for away, out_ref in enumerate((other_ref, own_ref)):
        tile = tile_ref[0] if away else 1 - tile_ref[0]
        for f in range(fars):
            for r in range(SUBS):
                parts = [
                    held[pl.ds(((f * tiles + tile) * halves + h) * SUBS + r, energies, stride=stride), :]
                    for h in range(halves)
                ]
                at = (f * SUBS + r) * halves * LANES
                values = jnp.concatenate(parts, axis=1)
                out_ref[:, at:at + halves * LANES] = dot3(project_ref[...], values)


def partial_coefs(tile, project, got, fars, tiles):
    rows = got[0].shape[0] * len(got)
    edges, energies = project.shape
    pixels = rows // energies // tiles * LANES
    vmem = pl.BlockSpec(memory_space=pltpu.VMEM)
    return pl.pallas_call(
        functools.partial(project_kernel, fars, tiles),
        out_shape=[jax.ShapeDtypeStruct((edges, pixels), jnp.float32)] * 2,
        in_specs=[pl.BlockSpec(memory_space=pltpu.SMEM)] + [vmem] * (1 + len(got)),
        out_specs=[vmem] * 2,
        scratch_shapes=[pltpu.VMEM((rows, LANES), jnp.float32)],
        cost_estimate=pl.CostEstimate(
            flops=6 * edges * energies * pixels, bytes_accessed=rows * LANES * 4, transcendentals=0
        ),
        compiler_params=pltpu.CompilerParams(vmem_limit_bytes=SMALL),
        name="partial_coefs",
    )(tile, project, *got)


def fit_kernel(far_ref, mine_ref, theirs_ref, basis_ref, coef_ref, *fit):
    own = coef_ref.shape[1]
    per = basis_ref.shape[0] // len(fit)
    stride = fit[0].shape[0] // per
    at = pl.ds(pl.multiple_of(far_ref[0] * own, own), own)
    coef_ref[...] = mine_ref[:, at] + theirs_ref[:, at]
    wide = 2 * LANES
    for j in range(mine_ref.shape[1] // wide):
        cols = slice(j * wide, (j + 1) * wide)
        values = dot3(basis_ref[...], mine_ref[:, cols] + theirs_ref[:, cols])
        for d, ref in enumerate(fit):
            for u in range(2):
                ref[pl.ds(j * 2 + u, per, stride=stride), :] = values[
                    d * per:(d + 1) * per, u * LANES:(u + 1) * LANES
                ]


def fitted_values(far, mine, theirs, basis, own, dests):
    edges, pixels = mine.shape
    energies = basis.shape[0]
    vmem = pl.BlockSpec(memory_space=pltpu.VMEM)
    rows = energies // dests * pixels // LANES
    out = pl.pallas_call(
        fit_kernel,
        out_shape=[jax.ShapeDtypeStruct((edges, own), jnp.float32)]
        + [jax.ShapeDtypeStruct((rows, LANES), jnp.float32)] * dests,
        in_specs=[pl.BlockSpec(memory_space=pltpu.SMEM), vmem, vmem, vmem],
        out_specs=[vmem] * (1 + dests),
        cost_estimate=pl.CostEstimate(
            flops=6 * edges * energies * pixels, bytes_accessed=energies * pixels * 4, transcendentals=0
        ),
        compiler_params=pltpu.CompilerParams(vmem_limit_bytes=SMALL),
        name="fitted_values",
    )(far, mine, theirs, basis)
    return out[0], out[1:]


def gather_kernel(part, senders, me_ref, *refs):
    got, (out_ref, sem) = refs[:senders], refs[-2:]
    copies = [
        pltpu.make_async_copy(ref, out_ref.at[part, :, :, me_ref[0] ^ d], sem.at[d])
        for d, ref in enumerate(got)
    ]
    for c in copies:
        c.start()
    for c in copies:
        c.wait()


def gather_part(part, me, got, out):
    senders = len(got)
    energies, fars, subs, _ = got[0].shape
    shape = (2, energies, fars, senders, subs, LANES)
    hbm = pl.BlockSpec(memory_space=pl.ANY)
    return pl.pallas_call(
        functools.partial(gather_kernel, part, senders),
        out_shape=jax.ShapeDtypeStruct(shape, jnp.float32),
        in_specs=[pl.BlockSpec(memory_space=pltpu.SMEM)]
        + [pl.BlockSpec(memory_space=pltpu.VMEM)] * senders
        + ([] if out is None else [hbm]),
        out_specs=hbm,
        scratch_shapes=[pltpu.SemaphoreType.DMA((senders,))],
        input_output_aliases={} if out is None else {1 + senders: 0},
        compiler_params=pltpu.CompilerParams(vmem_limit_bytes=SMALL),
        name="gather_part",
    )(me, *got, *([] if out is None else [out]))


def exchange(blocks, cube):
    return [
        b if d == 0 else lax.ppermute(b, "cube", [(i, i ^ d) for i in range(cube)])
        for d, b in enumerate(blocks)
    ]


def local(
    sample_inphase,
    sample_quadrature,
    beam_inphase,
    beam_quadrature,
    recorded_diffraction,
    window_corners,
    filled_tallies,
    absorption_templates,
):
    local_energies = sample_inphase.shape[0]
    side = sample_inphase.shape[1]
    spots = recorded_diffraction.shape[2]
    fars = lax.axis_size("far")
    cube = lax.axis_size("cube")
    blocks = fars * cube
    tiles = lax.axis_size("ta")
    tile = lax.axis_index("ta")
    swap = [(0, 1), (1, 0)]
    assert tiles == 2 and fars == 2
    used = spots * 3 // 2
    divided = local_energies % tiles == 0
    n_e = local_energies // tiles if divided else local_energies
    pix = side * side // (blocks * tiles)
    two_level = divided and pix == SUBS * side and local_energies == SUBS and cube & (cube - 1) == 0
    own_rec = recorded_diffraction[:, 0]
    first = tile * n_e if divided else jnp.zeros((), jnp.int32)
    theirs = lax.ppermute(window_corners, "ta", swap)
    give = lax.dynamic_slice_in_dim(own_rec, (1 - tile) * n_e, n_e, 0) if divided else own_rec
    par_rec = lax.ppermute(give, "ta", swap)
    table = slot_table(
        window_corners[:, 0], theirs[:, 0], filled_tallies, first.astype(jnp.int32), n_e, side,
        lax.axis_index("cube").astype(jnp.int32) if two_level else 0,
    )
    stepped = gradient_step(
        (sample_inphase, sample_quadrature),
        (beam_inphase, beam_quadrature),
        own_rec,
        par_rec,
        table,
        n_e,
        used,
        cube if two_level else 1,
        tiles,
    )

    if two_level:
        far = lax.axis_index("far").astype(jnp.int32)
        me = lax.axis_index("cube").astype(jnp.int32)
        where = jnp.stack([far, me, tile.astype(jnp.int32)])
        project_near, basis_near = solve_templates(where, absorption_templates, fars, cube, n_e)
        out, coefs = None, []
        parts = stepped[:cube], stepped[cube:]
        got = []
        for part in range(2):
            got.append(exchange(parts[part], cube))
        for part in range(2):
            blocks = [x.reshape(-1, LANES) for x in got[part]]
            kept, given = partial_coefs(
                tile.astype(jnp.int32)[None], project_near, blocks, fars, tiles
            )
            share = kept + lax.ppermute(given, "ta", swap)
            theirs = lax.ppermute(share, "far", swap)
            coef, fit = fitted_values(far[None], share, theirs, basis_near, pix, cube)
            coefs.append(coef)
            fit = [x.reshape(local_energies, fars, pix // LANES, LANES) for x in fit]
            back = exchange(fit, cube)
            out = gather_part(part, me[None], back, out)
        return (out.reshape(2, local_energies, cube * fars, 1, pix), jnp.stack(coefs))

    gram = jnp.dot(absorption_templates, absorption_templates.T, precision=HIGHEST)
    factor_low = jnp.linalg.cholesky(gram)
    project = jax.scipy.linalg.cho_solve((factor_low, True), absorption_templates)
    flat = jnp.stack([x.transpose(0, 1, 3, 2, 4) for x in stepped])
    if divided:
        flat = flat.reshape(2, n_e, blocks * tiles, pix)
        got = lax.all_to_all(flat, ("far", "cube", "ta"), 2, 1, tiled=True)
    else:
        flat = flat.reshape(2, n_e, blocks, tiles, pix)
        flat = lax.dynamic_index_in_dim(flat, tile, 3, keepdims=False)
        got = lax.all_to_all(flat, ("far", "cube"), 2, 1, tiled=True)
    values = got.reshape(2, -1, pix)
    coefs = jnp.einsum("ke,cen->ckn", project, values, precision=HIGHEST)
    fitted_here = jnp.einsum("ke,ckn->cen", absorption_templates, coefs, precision=HIGHEST)
    returned = lax.all_to_all(
        fitted_here[:, :, None, :], ("far", "cube"), split_axis=1, concat_axis=2, tiled=True
    )
    return (returned[:, :, :, None, :], coefs)


def solution(mesh):
    blocks, tiles = mesh.shape["ea"], mesh.shape["ta"]
    mesh = Mesh(mesh.devices.reshape(2, blocks // 2, tiles), ("far", "cube", "ta"))
    ea = ("far", "cube")
    in_specs = (
        P(ea, None, None),
        P(ea, None, None),
        P(ea, None, None, None),
        P(ea, None, None, None),
        P(ea, "ta", None, None, None),
        P(ea, "ta", None, None),
        P(ea, "ta"),
        P(),
    )
    out_specs = (P(None, ea, None, "ta", None), P(None, None, (*ea, "ta")))
    return jax.shard_map(local, mesh=mesh, in_specs=in_specs, out_specs=out_specs, check_vma=False)
```

```python
import functools

import jax
import jax.numpy as jnp
import numpy as np
from jax import lax
from jax.experimental import pallas as pl
from jax.experimental.pallas import tpu as pltpu
from jax.sharding import Mesh
from jax.sharding import PartitionSpec as P

HIGHEST = lax.Precision.HIGHEST
FLOOR_POWER = 0.5
REGULARIZER = 1.0
LANES = 128
SUBS = 8
SMALL = 12 << 20
LARGE = 50 << 20


def split_bf16(x):
    hi = x.astype(jnp.bfloat16)
    lo = (x - hi.astype(jnp.float32)).astype(jnp.bfloat16)
    return hi, lo


def transform_tables(width):
    fold = LANES // width
    i = np.arange(LANES) // width
    k = np.arange(LANES) % width
    phase = np.outer(i, i) / fold + np.outer(k, k) / width
    m = np.exp(-2j * np.pi * phase) / width
    real = np.block([[m.real, m.imag], [-m.imag, m.real]])
    q = np.arange(SUBS)
    tw = np.exp(-2j * np.pi * np.outer(q, i) / width)
    tw = np.concatenate([tw.real, tw.imag]).astype(np.float32)

    def halves(a):
        hi = a.astype(jnp.bfloat16)
        lo = (a - hi.astype(np.float64)).astype(jnp.bfloat16)
        return np.concatenate([hi, hi, lo])

    return halves(real), halves(real.T.copy()), tw


def fft8(re, im, sign):
    def butterfly(a, b):
        return (a[0] + b[0], a[1] + b[1]), (a[0] - b[0], a[1] - b[1])

    def turn(a):
        return (-a[1], a[0]) if sign > 0 else (a[1], -a[0])

    h = np.float32(np.sqrt(0.5))

    def eighth(a):
        if sign > 0:
            return ((a[0] - a[1]) * h, (a[0] + a[1]) * h)
        return ((a[0] + a[1]) * h, (a[1] - a[0]) * h)

    def fft4(x):
        s0, d0 = butterfly(x[0], x[2])
        s1, d1 = butterfly(x[1], x[3])
        d1 = turn(d1)
        y0, y2 = butterfly(s0, s1)
        y1, y3 = butterfly(d0, d1)
        return [y0, y1, y2, y3]

    x = list(zip(re, im))
    e = fft4(x[0::2])
    o = fft4(x[1::2])
    o = [o[0], eighth(o[1]), turn(o[2]), turn(eighth(o[3]))]
    pairs = [butterfly(e[n], o[n]) for n in range(4)]
    out = [p[0] for p in pairs] + [p[1] for p in pairs]
    return [y[0] for y in out], [y[1] for y in out]


def step_kernel(
    n_e, spots, used, modes, width, dests, tiles,
    table_ref,
    o_re, o_im, pr_hbm, pi_hbm, own_rec, par_rec, wf_hbm, wb_hbm, tw_hbm,
    *refs,
):
    outs = refs[:dests], refs[dests:2 * dests]
    (
        obj, rec, beam, probe, wf_ref, wb_ref, tw_ref, patch, term, root, work,
        sum_re, sum_im, sum_light, obj_sem, rec_sem, shared_sem,
    ) = refs[2 * dests:]
    fold = LANES // width
    groups = used // SUBS
    per_group = modes * SUBS
    per_q = groups * per_group
    side = obj.shape[3]
    lead = table_ref[0] >> (2 * side.bit_length() - 2 + spots.bit_length())
    local = o_re.shape[0]
    first, me = lead & (local - 1), lead >> (local.bit_length() - 1)
    sums = (sum_re, sum_im, sum_light)

    def in_copies(e):
        return [
            pltpu.make_async_copy(
                ref.at[first + e, :, pl.ds(h * LANES, LANES)], obj.at[e, c, h], obj_sem.at[e, c, h]
            )
            for c, ref in enumerate((o_re, o_im))
            for h in range(2)
        ] + [
            pltpu.make_async_copy(own_rec.at[first + e], rec.at[e, pl.ds(0, spots)], rec_sem.at[e, 0]),
            pltpu.make_async_copy(par_rec.at[e], rec.at[e, pl.ds(spots, spots)], rec_sem.at[e, 1]),
        ]

    shared = [
        pltpu.make_async_copy(src, dst, shared_sem.at[n])
        for n, (src, dst) in enumerate(
            (
                (pr_hbm.at[pl.ds(first, n_e)], beam.at[0]),
                (pi_hbm.at[pl.ds(first, n_e)], beam.at[1]),
                (tw_hbm, tw_ref),
                (wf_hbm, wf_ref),
                (wb_hbm, wb_ref),
            )
        )
    ]
    for c in in_copies(0) + shared:
        c.start()
    lane = lax.broadcasted_iota(jnp.int32, (SUBS, LANES), 1)
    block = lane // width
    for c in shared:
        c.wait()

    def place(e, index):
        packed = table_ref[e * used + index]
        shift = side.bit_length() - 1
        return (packed >> (2 * shift)) & (2 * spots - 1), (packed >> shift) & (side - 1), packed & (side - 1)

    def merge(parts):
        out = parts[0]
        for n in range(1, fold):
            out = jnp.where(block == n, parts[n], out)
        return out

    def row_of(ref, *index):
        return jnp.broadcast_to(ref[index], (SUBS, LANES))

    def product(x, w_ref):
        hi, lo = split_bf16(x)
        wide = jnp.concatenate([hi, lo, hi], axis=1)
        return jnp.dot(wide, w_ref[...], preferred_element_type=jnp.float32)

    def energy(e, carry):
        for acc in sums:
            acc[...] = jnp.zeros_like(acc)
        for c in in_copies(e):
            c.wait()

        @pl.when(e + 1 < n_e)
        def _():
            for c in in_copies(e + 1):
                c.start()

        for c in range(2):
            for m in range(modes):
                probe[c, m] = jnp.concatenate(
                    [beam[c, e, m, pl.ds(i, SUBS, stride=fold), :] for i in range(fold)], axis=1
                )
        for s in range(used):
            slot, row, col = place(e, s)
            low = lane >= col
            for c in range(2):
                parts = []
                for i in range(fold):
                    at = pl.ds(row + i, SUBS, stride=fold)
                    v = jnp.where(low, obj[e, c, 0, at, :], obj[e, c, 1, at, :])
                    parts.append(pltpu.roll(v, (i * width - col) & (LANES - 1), 1))
                patch[c, s * SUBS:(s + 1) * SUBS, :] = merge(parts)
            root[s * SUBS:(s + 1) * SUBS, :] = jnp.concatenate(
                [rec[e, slot, r * SUBS:(r + 1) * SUBS, :] for r in range(fold)], axis=1
            )

        for g in range(groups):
            base = g * SUBS * SUBS
            ats = [pl.ds(base + t, SUBS, stride=SUBS) for t in range(SUBS)]
            w_re = [patch[0, at, :] for at in ats]
            w_im = [patch[1, at, :] for at in ats]
            for m in range(modes):
                x_re, x_im = [], []
                for t in range(SUBS):
                    p_re = row_of(probe, 0, m, pl.ds(t, 1), slice(None))
                    p_im = row_of(probe, 1, m, pl.ds(t, 1), slice(None))
                    x_re.append(p_re * w_re[t] - p_im * w_im[t])
                    x_im.append(p_re * w_im[t] + p_im * w_re[t])
                y_re, y_im = fft8(x_re, x_im, -1)
                for q in range(SUBS):
                    a, b = y_re[q], y_im[q]
                    if q:
                        c = row_of(tw_ref, pl.ds(q, 1), slice(None))
                        d = row_of(tw_ref, pl.ds(SUBS + q, 1), slice(None))
                        a, b = a * c - b * d, a * d + b * c
                    to = q * per_q + g * per_group + m * SUBS
                    work[to:to + SUBS, 0:LANES] = a
                    work[to:to + SUBS, LANES:2 * LANES] = b

        for part in range(2):
            qs = range(part * SUBS // 2, (part + 1) * SUBS // 2)
            rows = slice(qs[0] * per_q, (qs[-1] + 1) * per_q)
            z = product(work[rows, :], wf_ref)
            scaled = []
            for q in qs:
                for g in range(groups):
                    f = []
                    for m in range(modes):
                        at = (q - qs[0]) * per_q + g * per_group + m * SUBS
                        f.append((z[at:at + SUBS, 0:LANES], z[at:at + SUBS, LANES:2 * LANES]))
                    power = f[0][0] * f[0][0] + f[0][1] * f[0][1]
                    for a, b in f[1:]:
                        power = power + a * a + b * b
                    measured = root[pl.ds(g * SUBS * SUBS + q, SUBS, stride=SUBS), :]
                    factor = 1.0 - jnp.sqrt(measured) * lax.rsqrt(jnp.maximum(power, FLOOR_POWER))
                    scaled += [
                        jnp.concatenate([a * factor, b * factor], axis=1) for a, b in f
                    ]
            work[rows, :] = product(jnp.concatenate(scaled, axis=0), wb_ref)

        light = jnp.zeros((SUBS, LANES), jnp.float32)
        for m in range(modes):
            a, b = probe[0, m], probe[1, m]
            light = light + a * a + b * b

        for g in range(groups):
            t_re = [None] * SUBS
            t_im = [None] * SUBS
            for m in range(modes):
                x_re, x_im = [], []
                for q in range(SUBS):
                    frm = q * per_q + g * per_group + m * SUBS
                    a, b = work[frm:frm + SUBS, 0:LANES], work[frm:frm + SUBS, LANES:2 * LANES]
                    if q:
                        c = row_of(tw_ref, pl.ds(q, 1), slice(None))
                        d = row_of(tw_ref, pl.ds(SUBS + q, 1), slice(None))
                        a, b = a * c + b * d, b * c - a * d
                    x_re.append(a)
                    x_im.append(b)
                y_re, y_im = fft8(x_re, x_im, 1)
                for t in range(SUBS):
                    p_re = row_of(probe, 0, m, pl.ds(t, 1), slice(None))
                    p_im = row_of(probe, 1, m, pl.ds(t, 1), slice(None))
                    a = p_re * y_re[t] + p_im * y_im[t]
                    b = p_re * y_im[t] - p_im * y_re[t]
                    t_re[t] = a if m == 0 else t_re[t] + a
                    t_im[t] = b if m == 0 else t_im[t] + b
            for t in range(SUBS):
                at = pl.ds(g * SUBS * SUBS + t, SUBS, stride=SUBS)
                term[0, at, :] = t_re[t]
                term[1, at, :] = t_im[t]

        for s in range(used):
            _, row, col = place(e, s)
            frm = slice(s * SUBS, (s + 1) * SUBS)
            terms = (term[0, frm, :], term[1, frm, :], light)
            which = jnp.where(col <= LANES - width, 0, jnp.where(col >= LANES, 1, 2))
            start = jnp.where(col <= LANES - width, col, jnp.where(col >= LANES, col - LANES, col - LANES // 2))
            inside = (lane >= start) & (lane < start + width)
            ats = [pl.ds(row + i, SUBS, stride=fold) for i in range(fold)]
            for acc, t in zip(sums, terms):
                new = []
                for i in range(fold):
                    v = pltpu.roll(t, (start - i * width) & (LANES - 1), 1)
                    new.append(acc[which, ats[i], :] + jnp.where(inside, v, 0.0))
                for i in range(fold):
                    acc[which, ats[i], :] = new[i]

        high = lane >= LANES // 2

        def finish(k, carry):
            for d in range(dests):
                n = ((k >> (tiles.bit_length() - 1)) * dests + (d ^ me)) * tiles + (k & (tiles - 1))
                at = pl.ds(pl.multiple_of(n * SUBS, SUBS), SUBS)
                mid = [pltpu.roll(acc[2, at, :], LANES // 2, 1) for acc in sums]
                for h in range(2):
                    mine = high if h == 0 else ~high
                    full = [acc[h, at, :] + jnp.where(mine, m, 0.0) for acc, m in zip(sums, mid)]
                    share = 1.0 / (full[2] + REGULARIZER)
                    for c in range(2):
                        outs[c][d][e, k, h] = obj[e, c, h, at, :] - full[c] * share
            return carry

        lax.fori_loop(0, side // SUBS // dests, finish, 0)
        return carry

    lax.fori_loop(0, n_e, energy, 0)


def gradient_step(objects, beams, own_rec, par_rec, table, n_e, used, dests, tiles):
    o_re, o_im = objects
    _, side, _ = o_re.shape
    modes, width = beams[0].shape[1], beams[0].shape[-1]
    spots = own_rec.shape[1]
    flat = width * width // LANES
    assert flat == SUBS and side == 2 * LANES and used % SUBS == 0
    wf, wb, tw = transform_tables(width)
    hbm = pl.BlockSpec(memory_space=pl.ANY)
    out_shape = (n_e, side // SUBS // dests, side // LANES, SUBS, LANES)
    return pl.pallas_call(
        functools.partial(step_kernel, n_e, spots, used, modes, width, dests, tiles),
        out_shape=[jax.ShapeDtypeStruct(out_shape, jnp.float32)] * (2 * dests),
        grid_spec=pltpu.PrefetchScalarGridSpec(
            num_scalar_prefetch=1,
            grid=(1,),
            in_specs=[hbm] * 9,
            out_specs=[pl.BlockSpec(memory_space=pltpu.VMEM)] * (2 * dests),
            scratch_shapes=[
                pltpu.VMEM((n_e, 2, 2, side, LANES), jnp.float32),
                pltpu.VMEM((n_e, 2 * spots, width, width), jnp.float32),
                pltpu.VMEM((2, n_e, modes, width, width), jnp.float32),
                pltpu.VMEM((2, modes, flat, LANES), jnp.float32),
                *[pltpu.VMEM(wf.shape, jnp.bfloat16)] * 2,
                pltpu.VMEM(tw.shape, jnp.float32),
                pltpu.VMEM((2, used * SUBS, LANES), jnp.float32),
                pltpu.VMEM((2, used * SUBS, LANES), jnp.float32),
                pltpu.VMEM((used * SUBS, LANES), jnp.float32),
                pltpu.VMEM((SUBS * used * modes, 2 * LANES), jnp.float32),
                *[pltpu.VMEM((3, side, LANES), jnp.float32)] * 3,
                pltpu.SemaphoreType.DMA((n_e, 2, 2)),
                pltpu.SemaphoreType.DMA((n_e, 2)),
                pltpu.SemaphoreType.DMA((5,)),
            ],
        ),
        compiler_params=pltpu.CompilerParams(vmem_limit_bytes=LARGE),
        name="gradient_step",
    )(
        table, o_re, o_im, *beams, own_rec, par_rec,
        jnp.asarray(wf), jnp.asarray(wb), jnp.asarray(tw),
    )


def slot_table(corners, theirs, counts, first, n_e, side, me):
    local, spots, _ = corners.shape
    lead = me * local + first
    assert local & (local - 1) == 0
    used = spots * 3 // 2
    assert side & (side - 1) == 0 and spots & (spots - 1) == 0
    both = jnp.concatenate([corners, theirs], axis=1)
    both = lax.dynamic_slice_in_dim(both, first, n_e, 0)
    counts = lax.dynamic_slice_in_dim(counts, first, n_e, 0)
    both = both[..., 0] * side + both[..., 1]
    both = both + (lead * 2 * spots + jnp.arange(2 * spots, dtype=jnp.int32)) * (side * side)
    index = jnp.arange(used, dtype=jnp.int32)[None]
    index = index + jnp.where(index < counts, 0, spots - counts)
    chosen = index[:, :, None] == jnp.arange(2 * spots, dtype=jnp.int32)
    return jnp.sum(jnp.where(chosen, both[:, None, :], 0), axis=2).reshape(-1)


def dot3(a, b):
    ah, al = split_bf16(a)
    bh, bl = split_bf16(b)
    left = jnp.concatenate([ah, al, ah], axis=1)
    right = jnp.concatenate([bh, bh, bl], axis=0)
    return jnp.dot(left, right, preferred_element_type=jnp.float32)


def solve_kernel(fars, cube, n_e, where_ref, basis_ref, project_ref, fit_ref):
    basis = basis_ref[...]
    edges, energies = basis.shape
    dot = functools.partial(lax.dot_general, precision=HIGHEST, preferred_element_type=jnp.float32)
    gram = dot(basis, basis, (((1,), (1,)), ((), ())))
    row = lax.broadcasted_iota(jnp.int32, (edges, 1), 0)
    right = basis
    for k in range(edges):
        pivot = 1.0 / gram[k:k + 1, k:k + 1]
        line, rhs = gram[k:k + 1, :] * pivot, right[k:k + 1, :] * pivot
        column = gram[:, k:k + 1]
        gram = jnp.where(row == k, line, gram - column * line)
        right = jnp.where(row == k, rhs, right - column * rhs)
    far, me, tile = where_ref[0], where_ref[1], where_ref[2]
    both = 2 * n_e

    def chosen(shape, axis, per, offset):
        n = lax.broadcasted_iota(jnp.int32, shape, axis)
        chip = (n // per) ^ me
        energy = far * (energies // fars) + chip * both + offset + n % per
        return (energy == lax.broadcasted_iota(jnp.int32, shape, 1 - axis)).astype(jnp.float32)

    project_ref[...] = dot(
        right, chosen((energies, cube * n_e), 1, n_e, tile * n_e), (((1,), (0,)), ((), ()))
    )
    fit_ref[...] = dot(
        chosen((cube * both, energies), 0, both, 0), basis, (((1,), (1,)), ((), ()))
    )


def solve_templates(where, basis, fars, cube, n_e):
    edges, _ = basis.shape
    vmem = pl.BlockSpec(memory_space=pltpu.VMEM)
    return pl.pallas_call(
        functools.partial(solve_kernel, fars, cube, n_e),
        out_shape=[
            jax.ShapeDtypeStruct((edges, cube * n_e), jnp.float32),
            jax.ShapeDtypeStruct((cube * 2 * n_e, edges), jnp.float32),
        ],
        in_specs=[pl.BlockSpec(memory_space=pltpu.SMEM), vmem],
        out_specs=[vmem] * 2,
        compiler_params=pltpu.CompilerParams(vmem_limit_bytes=SMALL),
        name="solve_templates",
    )(where, basis)


def project_kernel(fars, tiles, tile_ref, project_ref, *refs):
    *got, own_ref, other_ref, held = refs
    rows = got[0].shape[0]
    for d, ref in enumerate(got):
        held[d * rows:(d + 1) * rows, :] = ref[...]
    energies = project_ref.shape[1]
    stride = held.shape[0] // energies
    halves = stride // (fars * tiles * SUBS)
    for away, out_ref in enumerate((other_ref, own_ref)):
        tile = tile_ref[0] if away else 1 - tile_ref[0]
        for f in range(fars):
            for r in range(SUBS):
                parts = [
                    held[pl.ds(((f * tiles + tile) * halves + h) * SUBS + r, energies, stride=stride), :]
                    for h in range(halves)
                ]
                at = (f * SUBS + r) * halves * LANES
                values = jnp.concatenate(parts, axis=1)
                out_ref[:, at:at + halves * LANES] = dot3(project_ref[...], values)


def partial_coefs(tile, project, got, fars, tiles):
    rows = got[0].shape[0] * len(got)
    edges, energies = project.shape
    pixels = rows // energies // tiles * LANES
    vmem = pl.BlockSpec(memory_space=pltpu.VMEM)
    return pl.pallas_call(
        functools.partial(project_kernel, fars, tiles),
        out_shape=[jax.ShapeDtypeStruct((edges, pixels), jnp.float32)] * 2,
        in_specs=[pl.BlockSpec(memory_space=pltpu.SMEM)] + [vmem] * (1 + len(got)),
        out_specs=[vmem] * 2,
        scratch_shapes=[pltpu.VMEM((rows, LANES), jnp.float32)],
        cost_estimate=pl.CostEstimate(
            flops=6 * edges * energies * pixels, bytes_accessed=rows * LANES * 4, transcendentals=0
        ),
        compiler_params=pltpu.CompilerParams(vmem_limit_bytes=SMALL),
        name="partial_coefs",
    )(tile, project, *got)


def fit_kernel(far_ref, mine_ref, theirs_ref, basis_ref, coef_ref, *fit):
    own = coef_ref.shape[1]
    per = basis_ref.shape[0] // len(fit)
    stride = fit[0].shape[0] // per
    at = pl.ds(pl.multiple_of(far_ref[0] * own, own), own)
    coef_ref[...] = mine_ref[:, at] + theirs_ref[:, at]
    wide = 2 * LANES
    for j in range(mine_ref.shape[1] // wide):
        cols = slice(j * wide, (j + 1) * wide)
        values = dot3(basis_ref[...], mine_ref[:, cols] + theirs_ref[:, cols])
        for d, ref in enumerate(fit):
            for u in range(2):
                ref[pl.ds(j * 2 + u, per, stride=stride), :] = values[
                    d * per:(d + 1) * per, u * LANES:(u + 1) * LANES
                ]


def fitted_values(far, mine, theirs, basis, own, dests):
    edges, pixels = mine.shape
    energies = basis.shape[0]
    vmem = pl.BlockSpec(memory_space=pltpu.VMEM)
    rows = energies // dests * pixels // LANES
    out = pl.pallas_call(
        fit_kernel,
        out_shape=[jax.ShapeDtypeStruct((edges, own), jnp.float32)]
        + [jax.ShapeDtypeStruct((rows, LANES), jnp.float32)] * dests,
        in_specs=[pl.BlockSpec(memory_space=pltpu.SMEM), vmem, vmem, vmem],
        out_specs=[vmem] * (1 + dests),
        cost_estimate=pl.CostEstimate(
            flops=6 * edges * energies * pixels, bytes_accessed=energies * pixels * 4, transcendentals=0
        ),
        compiler_params=pltpu.CompilerParams(vmem_limit_bytes=SMALL),
        name="fitted_values",
    )(far, mine, theirs, basis)
    return out[0], out[1:]


def gather_kernel(part, senders, me_ref, *refs):
    got, (out_ref, sem) = refs[:senders], refs[-2:]
    copies = [
        pltpu.make_async_copy(ref, out_ref.at[part, :, :, me_ref[0] ^ d], sem.at[d])
        for d, ref in enumerate(got)
    ]
    for c in copies:
        c.start()
    for c in copies:
        c.wait()


def gather_part(part, me, got, out):
    senders = len(got)
    energies, fars, subs, _ = got[0].shape
    shape = (2, energies, fars, senders, subs, LANES)
    hbm = pl.BlockSpec(memory_space=pl.ANY)
    return pl.pallas_call(
        functools.partial(gather_kernel, part, senders),
        out_shape=jax.ShapeDtypeStruct(shape, jnp.float32),
        in_specs=[pl.BlockSpec(memory_space=pltpu.SMEM)]
        + [pl.BlockSpec(memory_space=pltpu.VMEM)] * senders
        + ([] if out is None else [hbm]),
        out_specs=hbm,
        scratch_shapes=[pltpu.SemaphoreType.DMA((senders,))],
        input_output_aliases={} if out is None else {1 + senders: 0},
        compiler_params=pltpu.CompilerParams(vmem_limit_bytes=SMALL),
        name="gather_part",
    )(me, *got, *([] if out is None else [out]))


def exchange(blocks, cube):
    got = list(blocks)
    for d in sorted(range(1, cube), key=lambda d: (-d.bit_count(), -d)):
        got[d] = lax.ppermute(blocks[d], "cube", [(i, i ^ d) for i in range(cube)])
    return got


def local(
    sample_inphase,
    sample_quadrature,
    beam_inphase,
    beam_quadrature,
    recorded_diffraction,
    window_corners,
    filled_tallies,
    absorption_templates,
):
    local_energies = sample_inphase.shape[0]
    side = sample_inphase.shape[1]
    spots = recorded_diffraction.shape[2]
    fars = lax.axis_size("far")
    cube = lax.axis_size("cube")
    blocks = fars * cube
    tiles = lax.axis_size("ta")
    tile = lax.axis_index("ta")
    swap = [(0, 1), (1, 0)]
    assert tiles == 2 and fars == 2
    used = spots * 3 // 2
    divided = local_energies % tiles == 0
    n_e = local_energies // tiles if divided else local_energies
    pix = side * side // (blocks * tiles)
    two_level = divided and pix == SUBS * side and local_energies == SUBS and cube & (cube - 1) == 0
    own_rec = recorded_diffraction[:, 0]
    first = tile * n_e if divided else jnp.zeros((), jnp.int32)
    theirs = lax.ppermute(window_corners, "ta", swap)
    give = lax.dynamic_slice_in_dim(own_rec, (1 - tile) * n_e, n_e, 0) if divided else own_rec
    par_rec = lax.ppermute(give, "ta", swap)
    table = slot_table(
        window_corners[:, 0], theirs[:, 0], filled_tallies, first.astype(jnp.int32), n_e, side,
        lax.axis_index("cube").astype(jnp.int32) if two_level else 0,
    )
    stepped = gradient_step(
        (sample_inphase, sample_quadrature),
        (beam_inphase, beam_quadrature),
        own_rec,
        par_rec,
        table,
        n_e,
        used,
        cube if two_level else 1,
        tiles,
    )

    if two_level:
        far = lax.axis_index("far").astype(jnp.int32)
        me = lax.axis_index("cube").astype(jnp.int32)
        where = jnp.stack([far, me, tile.astype(jnp.int32)])
        project_near, basis_near = solve_templates(where, absorption_templates, fars, cube, n_e)
        out, coefs = None, []
        parts = stepped[:cube], stepped[cube:]
        got = []
        for part in range(2):
            got.append(exchange(parts[part], cube))
        for part in range(2):
            blocks = [x.reshape(-1, LANES) for x in got[part]]
            kept, given = partial_coefs(
                tile.astype(jnp.int32)[None], project_near, blocks, fars, tiles
            )
            share = kept + lax.ppermute(given, "ta", swap)
            theirs = lax.ppermute(share, "far", swap)
            coef, fit = fitted_values(far[None], share, theirs, basis_near, pix, cube)
            coefs.append(coef)
            fit = [x.reshape(local_energies, fars, pix // LANES, LANES) for x in fit]
            back = exchange(fit, cube)
            out = gather_part(part, me[None], back, out)
        return (out.reshape(2, local_energies, cube * fars, 1, pix), jnp.stack(coefs))

    gram = jnp.dot(absorption_templates, absorption_templates.T, precision=HIGHEST)
    factor_low = jnp.linalg.cholesky(gram)
    project = jax.scipy.linalg.cho_solve((factor_low, True), absorption_templates)
    flat = jnp.stack([x.transpose(0, 1, 3, 2, 4) for x in stepped])
    if divided:
        flat = flat.reshape(2, n_e, blocks * tiles, pix)
        got = lax.all_to_all(flat, ("far", "cube", "ta"), 2, 1, tiled=True)
    else:
        flat = flat.reshape(2, n_e, blocks, tiles, pix)
        flat = lax.dynamic_index_in_dim(flat, tile, 3, keepdims=False)
        got = lax.all_to_all(flat, ("far", "cube"), 2, 1, tiled=True)
    values = got.reshape(2, -1, pix)
    coefs = jnp.einsum("ke,cen->ckn", project, values, precision=HIGHEST)
    fitted_here = jnp.einsum("ke,ckn->cen", absorption_templates, coefs, precision=HIGHEST)
    returned = lax.all_to_all(
        fitted_here[:, :, None, :], ("far", "cube"), split_axis=1, concat_axis=2, tiled=True
    )
    return (returned[:, :, :, None, :], coefs)


def solution(mesh):
    blocks, tiles = mesh.shape["ea"], mesh.shape["ta"]
    mesh = Mesh(mesh.devices.reshape(2, blocks // 2, tiles), ("far", "cube", "ta"))
    ea = ("far", "cube")
    in_specs = (
        P(ea, None, None),
        P(ea, None, None),
        P(ea, None, None, None),
        P(ea, None, None, None),
        P(ea, "ta", None, None, None),
        P(ea, "ta", None, None),
        P(ea, "ta"),
        P(),
    )
    out_specs = (P(None, ea, None, "ta", None), P(None, None, (*ea, "ta")))
    return jax.shard_map(local, mesh=mesh, in_specs=in_specs, out_specs=out_specs, check_vma=False)
```

```python
import functools

import jax
import jax.numpy as jnp
import numpy as np
from jax import lax
from jax.experimental import pallas as pl
from jax.experimental.pallas import tpu as pltpu
from jax.sharding import Mesh
from jax.sharding import PartitionSpec as P

HIGHEST = lax.Precision.HIGHEST
FLOOR_POWER = 0.5
REGULARIZER = 1.0
LANES = 128
SUBS = 8
SMALL = 12 << 20
LARGE = 50 << 20


def split_bf16(x):
    hi = x.astype(jnp.bfloat16)
    lo = (x - hi.astype(jnp.float32)).astype(jnp.bfloat16)
    return hi, lo


def transform_tables(width):
    fold = LANES // width
    i = np.arange(LANES) // width
    k = np.arange(LANES) % width
    phase = np.outer(i, i) / fold + np.outer(k, k) / width
    m = np.exp(-2j * np.pi * phase) / width
    real = np.block([[m.real, m.imag], [-m.imag, m.real]])
    q = np.arange(SUBS)
    tw = np.exp(-2j * np.pi * np.outer(q, i) / width)
    tw = np.concatenate([tw.real, tw.imag]).astype(np.float32)

    def halves(a):
        hi = a.astype(jnp.bfloat16)
        lo = (a - hi.astype(np.float64)).astype(jnp.bfloat16)
        return np.concatenate([hi, hi, lo])

    return halves(real), halves(real.T.copy()), tw


def fft8(re, im, sign):
    def butterfly(a, b):
        return (a[0] + b[0], a[1] + b[1]), (a[0] - b[0], a[1] - b[1])

    def turn(a):
        return (-a[1], a[0]) if sign > 0 else (a[1], -a[0])

    h = np.float32(np.sqrt(0.5))

    def eighth(a):
        if sign > 0:
            return ((a[0] - a[1]) * h, (a[0] + a[1]) * h)
        return ((a[0] + a[1]) * h, (a[1] - a[0]) * h)

    def fft4(x):
        s0, d0 = butterfly(x[0], x[2])
        s1, d1 = butterfly(x[1], x[3])
        d1 = turn(d1)
        y0, y2 = butterfly(s0, s1)
        y1, y3 = butterfly(d0, d1)
        return [y0, y1, y2, y3]

    x = list(zip(re, im))
    e = fft4(x[0::2])
    o = fft4(x[1::2])
    o = [o[0], eighth(o[1]), turn(o[2]), turn(eighth(o[3]))]
    pairs = [butterfly(e[n], o[n]) for n in range(4)]
    out = [p[0] for p in pairs] + [p[1] for p in pairs]
    return [y[0] for y in out], [y[1] for y in out]


def step_kernel(
    n_e, spots, used, modes, width, dests, tiles,
    table_ref,
    o_re, o_im, pr_hbm, pi_hbm, own_rec, par_rec, wf_hbm, wb_hbm, tw_hbm,
    *refs,
):
    outs = refs[:dests], refs[dests:2 * dests]
    (
        obj, rec, beam, probe, wf_ref, wb_ref, tw_ref, patch, term, root, work,
        sum_re, sum_im, sum_light, obj_sem, rec_sem, shared_sem,
    ) = refs[2 * dests:]
    fold = LANES // width
    groups = used // SUBS
    per_group = modes * SUBS
    per_q = groups * per_group
    side = obj.shape[3]
    lead = table_ref[0] >> (2 * side.bit_length() - 2 + spots.bit_length())
    local = o_re.shape[0]
    first, place_of = lead & (local - 1), lead >> (local.bit_length() - 1)
    me, far = place_of & (dests - 1), place_of >> (dests.bit_length() - 1)
    sums = (sum_re, sum_im, sum_light)

    def in_copies(e):
        return [
            pltpu.make_async_copy(
                ref.at[first + e, :, pl.ds(h * LANES, LANES)], obj.at[e, c, h], obj_sem.at[e, c, h]
            )
            for c, ref in enumerate((o_re, o_im))
            for h in range(2)
        ] + [
            pltpu.make_async_copy(own_rec.at[first + e], rec.at[e, pl.ds(0, spots)], rec_sem.at[e, 0]),
            pltpu.make_async_copy(par_rec.at[e], rec.at[e, pl.ds(spots, spots)], rec_sem.at[e, 1]),
        ]

    shared = [
        pltpu.make_async_copy(src, dst, shared_sem.at[n])
        for n, (src, dst) in enumerate(
            (
                (pr_hbm.at[pl.ds(first, n_e)], beam.at[0]),
                (pi_hbm.at[pl.ds(first, n_e)], beam.at[1]),
                (tw_hbm, tw_ref),
                (wf_hbm, wf_ref),
                (wb_hbm, wb_ref),
            )
        )
    ]
    for c in in_copies(0) + shared:
        c.start()
    lane = lax.broadcasted_iota(jnp.int32, (SUBS, LANES), 1)
    block = lane // width
    for c in shared:
        c.wait()

    def place(e, index):
        packed = table_ref[e * used + index]
        shift = side.bit_length() - 1
        return (packed >> (2 * shift)) & (2 * spots - 1), (packed >> shift) & (side - 1), packed & (side - 1)

    def merge(parts):
        out = parts[0]
        for n in range(1, fold):
            out = jnp.where(block == n, parts[n], out)
        return out

    def row_of(ref, *index):
        return jnp.broadcast_to(ref[index], (SUBS, LANES))

    def product(x, w_ref):
        hi, lo = split_bf16(x)
        wide = jnp.concatenate([hi, lo, hi], axis=1)
        return jnp.dot(wide, w_ref[...], preferred_element_type=jnp.float32)

    def energy(e, carry):
        for acc in sums:
            acc[...] = jnp.zeros_like(acc)
        for c in in_copies(e):
            c.wait()

        @pl.when(e + 1 < n_e)
        def _():
            for c in in_copies(e + 1):
                c.start()

        for c in range(2):
            for m in range(modes):
                probe[c, m] = jnp.concatenate(
                    [beam[c, e, m, pl.ds(i, SUBS, stride=fold), :] for i in range(fold)], axis=1
                )
        for s in range(used):
            slot, row, col = place(e, s)
            low = lane >= col
            for c in range(2):
                parts = []
                for i in range(fold):
                    at = pl.ds(row + i, SUBS, stride=fold)
                    v = jnp.where(low, obj[e, c, 0, at, :], obj[e, c, 1, at, :])
                    parts.append(pltpu.roll(v, (i * width - col) & (LANES - 1), 1))
                patch[c, s * SUBS:(s + 1) * SUBS, :] = merge(parts)
            root[s * SUBS:(s + 1) * SUBS, :] = jnp.concatenate(
                [rec[e, slot, r * SUBS:(r + 1) * SUBS, :] for r in range(fold)], axis=1
            )

        for g in range(groups):
            base = g * SUBS * SUBS
            ats = [pl.ds(base + t, SUBS, stride=SUBS) for t in range(SUBS)]
            w_re = [patch[0, at, :] for at in ats]
            w_im = [patch[1, at, :] for at in ats]
            for m in range(modes):
                x_re, x_im = [], []
                for t in range(SUBS):
                    p_re = row_of(probe, 0, m, pl.ds(t, 1), slice(None))
                    p_im = row_of(probe, 1, m, pl.ds(t, 1), slice(None))
                    x_re.append(p_re * w_re[t] - p_im * w_im[t])
                    x_im.append(p_re * w_im[t] + p_im * w_re[t])
                y_re, y_im = fft8(x_re, x_im, -1)
                for q in range(SUBS):
                    a, b = y_re[q], y_im[q]
                    if q:
                        c = row_of(tw_ref, pl.ds(q, 1), slice(None))
                        d = row_of(tw_ref, pl.ds(SUBS + q, 1), slice(None))
                        a, b = a * c - b * d, a * d + b * c
                    to = q * per_q + g * per_group + m * SUBS
                    work[to:to + SUBS, 0:LANES] = a
                    work[to:to + SUBS, LANES:2 * LANES] = b

        for part in range(2):
            qs = range(part * SUBS // 2, (part + 1) * SUBS // 2)
            rows = slice(qs[0] * per_q, (qs[-1] + 1) * per_q)
            z = product(work[rows, :], wf_ref)
            scaled = []
            for q in qs:
                for g in range(groups):
                    f = []
                    for m in range(modes):
                        at = (q - qs[0]) * per_q + g * per_group + m * SUBS
                        f.append((z[at:at + SUBS, 0:LANES], z[at:at + SUBS, LANES:2 * LANES]))
                    power = f[0][0] * f[0][0] + f[0][1] * f[0][1]
                    for a, b in f[1:]:
                        power = power + a * a + b * b
                    measured = root[pl.ds(g * SUBS * SUBS + q, SUBS, stride=SUBS), :]
                    factor = 1.0 - jnp.sqrt(measured) * lax.rsqrt(jnp.maximum(power, FLOOR_POWER))
                    scaled += [
                        jnp.concatenate([a * factor, b * factor], axis=1) for a, b in f
                    ]
            work[rows, :] = product(jnp.concatenate(scaled, axis=0), wb_ref)

        light = jnp.zeros((SUBS, LANES), jnp.float32)
        for m in range(modes):
            a, b = probe[0, m], probe[1, m]
            light = light + a * a + b * b

        for g in range(groups):
            t_re = [None] * SUBS
            t_im = [None] * SUBS
            for m in range(modes):
                x_re, x_im = [], []
                for q in range(SUBS):
                    frm = q * per_q + g * per_group + m * SUBS
                    a, b = work[frm:frm + SUBS, 0:LANES], work[frm:frm + SUBS, LANES:2 * LANES]
                    if q:
                        c = row_of(tw_ref, pl.ds(q, 1), slice(None))
                        d = row_of(tw_ref, pl.ds(SUBS + q, 1), slice(None))
                        a, b = a * c + b * d, b * c - a * d
                    x_re.append(a)
                    x_im.append(b)
                y_re, y_im = fft8(x_re, x_im, 1)
                for t in range(SUBS):
                    p_re = row_of(probe, 0, m, pl.ds(t, 1), slice(None))
                    p_im = row_of(probe, 1, m, pl.ds(t, 1), slice(None))
                    a = p_re * y_re[t] + p_im * y_im[t]
                    b = p_re * y_im[t] - p_im * y_re[t]
                    t_re[t] = a if m == 0 else t_re[t] + a
                    t_im[t] = b if m == 0 else t_im[t] + b
            for t in range(SUBS):
                at = pl.ds(g * SUBS * SUBS + t, SUBS, stride=SUBS)
                term[0, at, :] = t_re[t]
                term[1, at, :] = t_im[t]

        for s in range(used):
            _, row, col = place(e, s)
            frm = slice(s * SUBS, (s + 1) * SUBS)
            terms = (term[0, frm, :], term[1, frm, :], light)
            which = jnp.where(col <= LANES - width, 0, jnp.where(col >= LANES, 1, 2))
            start = jnp.where(col <= LANES - width, col, jnp.where(col >= LANES, col - LANES, col - LANES // 2))
            inside = (lane >= start) & (lane < start + width)
            ats = [pl.ds(row + i, SUBS, stride=fold) for i in range(fold)]
            for acc, t in zip(sums, terms):
                new = []
                for i in range(fold):
                    v = pltpu.roll(t, (start - i * width) & (LANES - 1), 1)
                    new.append(acc[which, ats[i], :] + jnp.where(inside, v, 0.0))
                for i in range(fold):
                    acc[which, ats[i], :] = new[i]

        high = lane >= LANES // 2

        def finish(k, carry):
            for d in range(dests):
                f = k >> (tiles.bit_length() - 1)
                across = jnp.where(f == far, 0, dests // 2) if dests > 1 else 0
                n = (f * dests + (d ^ me ^ across)) * tiles + (k & (tiles - 1))
                at = pl.ds(pl.multiple_of(n * SUBS, SUBS), SUBS)
                mid = [pltpu.roll(acc[2, at, :], LANES // 2, 1) for acc in sums]
                for h in range(2):
                    mine = high if h == 0 else ~high
                    full = [acc[h, at, :] + jnp.where(mine, m, 0.0) for acc, m in zip(sums, mid)]
                    share = 1.0 / (full[2] + REGULARIZER)
                    for c in range(2):
                        outs[c][d][e, k, h] = obj[e, c, h, at, :] - full[c] * share
            return carry

        lax.fori_loop(0, side // SUBS // dests, finish, 0)
        return carry

    lax.fori_loop(0, n_e, energy, 0)


def gradient_step(objects, beams, own_rec, par_rec, table, n_e, used, dests, tiles):
    o_re, o_im = objects
    _, side, _ = o_re.shape
    modes, width = beams[0].shape[1], beams[0].shape[-1]
    spots = own_rec.shape[1]
    flat = width * width // LANES
    assert flat == SUBS and side == 2 * LANES and used % SUBS == 0
    wf, wb, tw = transform_tables(width)
    hbm = pl.BlockSpec(memory_space=pl.ANY)
    out_shape = (n_e, side // SUBS // dests, side // LANES, SUBS, LANES)
    return pl.pallas_call(
        functools.partial(step_kernel, n_e, spots, used, modes, width, dests, tiles),
        out_shape=[jax.ShapeDtypeStruct(out_shape, jnp.float32)] * (2 * dests),
        grid_spec=pltpu.PrefetchScalarGridSpec(
            num_scalar_prefetch=1,
            grid=(1,),
            in_specs=[hbm] * 9,
            out_specs=[pl.BlockSpec(memory_space=pltpu.VMEM)] * (2 * dests),
            scratch_shapes=[
                pltpu.VMEM((n_e, 2, 2, side, LANES), jnp.float32),
                pltpu.VMEM((n_e, 2 * spots, width, width), jnp.float32),
                pltpu.VMEM((2, n_e, modes, width, width), jnp.float32),
                pltpu.VMEM((2, modes, flat, LANES), jnp.float32),
                *[pltpu.VMEM(wf.shape, jnp.bfloat16)] * 2,
                pltpu.VMEM(tw.shape, jnp.float32),
                pltpu.VMEM((2, used * SUBS, LANES), jnp.float32),
                pltpu.VMEM((2, used * SUBS, LANES), jnp.float32),
                pltpu.VMEM((used * SUBS, LANES), jnp.float32),
                pltpu.VMEM((SUBS * used * modes, 2 * LANES), jnp.float32),
                *[pltpu.VMEM((3, side, LANES), jnp.float32)] * 3,
                pltpu.SemaphoreType.DMA((n_e, 2, 2)),
                pltpu.SemaphoreType.DMA((n_e, 2)),
                pltpu.SemaphoreType.DMA((5,)),
            ],
        ),
        compiler_params=pltpu.CompilerParams(vmem_limit_bytes=LARGE),
        name="gradient_step",
    )(
        table, o_re, o_im, *beams, own_rec, par_rec,
        jnp.asarray(wf), jnp.asarray(wb), jnp.asarray(tw),
    )


def slot_table(corners, theirs, counts, first, n_e, side, me):
    local, spots, _ = corners.shape
    lead = me * local + first
    assert local & (local - 1) == 0
    used = spots * 3 // 2
    assert side & (side - 1) == 0 and spots & (spots - 1) == 0
    both = jnp.concatenate([corners, theirs], axis=1)
    both = lax.dynamic_slice_in_dim(both, first, n_e, 0)
    counts = lax.dynamic_slice_in_dim(counts, first, n_e, 0)
    both = both[..., 0] * side + both[..., 1]
    both = both + (lead * 2 * spots + jnp.arange(2 * spots, dtype=jnp.int32)) * (side * side)
    index = jnp.arange(used, dtype=jnp.int32)[None]
    index = index + jnp.where(index < counts, 0, spots - counts)
    chosen = index[:, :, None] == jnp.arange(2 * spots, dtype=jnp.int32)
    return jnp.sum(jnp.where(chosen, both[:, None, :], 0), axis=2).reshape(-1)


def dot3(a, b):
    ah, al = split_bf16(a)
    bh, bl = split_bf16(b)
    left = jnp.concatenate([ah, al, ah], axis=1)
    right = jnp.concatenate([bh, bh, bl], axis=0)
    return jnp.dot(left, right, preferred_element_type=jnp.float32)


def solve_kernel(fars, cube, n_e, where_ref, basis_ref, project_ref, fit_ref):
    basis = basis_ref[...]
    edges, energies = basis.shape
    dot = functools.partial(lax.dot_general, precision=HIGHEST, preferred_element_type=jnp.float32)
    gram = dot(basis, basis, (((1,), (1,)), ((), ())))
    row = lax.broadcasted_iota(jnp.int32, (edges, 1), 0)
    right = basis
    for k in range(edges):
        pivot = 1.0 / gram[k:k + 1, k:k + 1]
        line, rhs = gram[k:k + 1, :] * pivot, right[k:k + 1, :] * pivot
        column = gram[:, k:k + 1]
        gram = jnp.where(row == k, line, gram - column * line)
        right = jnp.where(row == k, rhs, right - column * rhs)
    me, far, tile = where_ref[0], where_ref[1], where_ref[2]
    both = 2 * n_e

    def chosen(shape, axis, per, offset):
        n = lax.broadcasted_iota(jnp.int32, shape, axis)
        chip = (n // per) ^ me
        energy = far * (energies // fars) + chip * both + offset + n % per
        return (energy == lax.broadcasted_iota(jnp.int32, shape, 1 - axis)).astype(jnp.float32)

    project_ref[...] = dot(
        right, chosen((energies, cube * n_e), 1, n_e, tile * n_e), (((1,), (0,)), ((), ()))
    )
    fit_ref[...] = dot(
        chosen((cube * both, energies), 0, both, 0), basis, (((1,), (1,)), ((), ()))
    )


def solve_templates(where, basis, fars, cube, n_e):
    edges, _ = basis.shape
    vmem = pl.BlockSpec(memory_space=pltpu.VMEM)
    return pl.pallas_call(
        functools.partial(solve_kernel, fars, cube, n_e),
        out_shape=[
            jax.ShapeDtypeStruct((edges, cube * n_e), jnp.float32),
            jax.ShapeDtypeStruct((cube * 2 * n_e, edges), jnp.float32),
        ],
        in_specs=[pl.BlockSpec(memory_space=pltpu.SMEM), vmem],
        out_specs=[vmem] * 2,
        compiler_params=pltpu.CompilerParams(vmem_limit_bytes=SMALL),
        name="solve_templates",
    )(where, basis)


def project_kernel(fars, tiles, tile_ref, project_ref, *refs):
    *got, own_ref, other_ref, held = refs
    rows = got[0].shape[0]
    for d, ref in enumerate(got):
        held[d * rows:(d + 1) * rows, :] = ref[...]
    energies = project_ref.shape[1]
    stride = held.shape[0] // energies
    halves = stride // (fars * tiles * SUBS)
    for away, out_ref in enumerate((other_ref, own_ref)):
        tile = tile_ref[0] if away else 1 - tile_ref[0]
        for f in range(fars):
            for r in range(SUBS):
                parts = [
                    held[pl.ds(((f * tiles + tile) * halves + h) * SUBS + r, energies, stride=stride), :]
                    for h in range(halves)
                ]
                at = (f * SUBS + r) * halves * LANES
                values = jnp.concatenate(parts, axis=1)
                out_ref[:, at:at + halves * LANES] = dot3(project_ref[...], values)


def partial_coefs(tile, project, got, fars, tiles):
    rows = got[0].shape[0] * len(got)
    edges, energies = project.shape
    pixels = rows // energies // tiles * LANES
    vmem = pl.BlockSpec(memory_space=pltpu.VMEM)
    return pl.pallas_call(
        functools.partial(project_kernel, fars, tiles),
        out_shape=[jax.ShapeDtypeStruct((edges, pixels), jnp.float32)] * 2,
        in_specs=[pl.BlockSpec(memory_space=pltpu.SMEM)] + [vmem] * (1 + len(got)),
        out_specs=[vmem] * 2,
        scratch_shapes=[pltpu.VMEM((rows, LANES), jnp.float32)],
        cost_estimate=pl.CostEstimate(
            flops=6 * edges * energies * pixels, bytes_accessed=rows * LANES * 4, transcendentals=0
        ),
        compiler_params=pltpu.CompilerParams(vmem_limit_bytes=SMALL),
        name="partial_coefs",
    )(tile, project, *got)


def fit_kernel(far_ref, mine_ref, theirs_ref, basis_ref, coef_ref, *fit):
    own = coef_ref.shape[1]
    per = basis_ref.shape[0] // len(fit)
    stride = fit[0].shape[0] // per
    at = pl.ds(pl.multiple_of(far_ref[0] * own, own), own)
    coef_ref[...] = mine_ref[:, at] + theirs_ref[:, at]
    wide = 2 * LANES
    for j in range(mine_ref.shape[1] // wide):
        cols = slice(j * wide, (j + 1) * wide)
        values = dot3(basis_ref[...], mine_ref[:, cols] + theirs_ref[:, cols])
        for d, ref in enumerate(fit):
            for u in range(2):
                ref[pl.ds(j * 2 + u, per, stride=stride), :] = values[
                    d * per:(d + 1) * per, u * LANES:(u + 1) * LANES
                ]


def fitted_values(far, mine, theirs, basis, own, dests):
    edges, pixels = mine.shape
    energies = basis.shape[0]
    vmem = pl.BlockSpec(memory_space=pltpu.VMEM)
    rows = energies // dests * pixels // LANES
    out = pl.pallas_call(
        fit_kernel,
        out_shape=[jax.ShapeDtypeStruct((edges, own), jnp.float32)]
        + [jax.ShapeDtypeStruct((rows, LANES), jnp.float32)] * dests,
        in_specs=[pl.BlockSpec(memory_space=pltpu.SMEM), vmem, vmem, vmem],
        out_specs=[vmem] * (1 + dests),
        cost_estimate=pl.CostEstimate(
            flops=6 * edges * energies * pixels, bytes_accessed=energies * pixels * 4, transcendentals=0
        ),
        compiler_params=pltpu.CompilerParams(vmem_limit_bytes=SMALL),
        name="fitted_values",
    )(far, mine, theirs, basis)
    return out[0], out[1:]


def gather_kernel(part, senders, me_ref, *refs):
    got, (out_ref, sem) = refs[:senders], refs[-2:]
    copies = [
        pltpu.make_async_copy(
            ref.at[:, f],
            out_ref.at[part, :, f, me_ref[0] ^ d ^ jnp.where(me_ref[1] == f, 0, senders // 2)],
            sem.at[d, f],
        )
        for d, ref in enumerate(got)
        for f in range(ref.shape[1])
    ]
    for c in copies:
        c.start()
    for c in copies:
        c.wait()


def gather_part(part, me, got, out):
    senders = len(got)
    energies, fars, subs, _ = got[0].shape
    shape = (2, energies, fars, senders, subs, LANES)
    hbm = pl.BlockSpec(memory_space=pl.ANY)
    return pl.pallas_call(
        functools.partial(gather_kernel, part, senders),
        out_shape=jax.ShapeDtypeStruct(shape, jnp.float32),
        in_specs=[pl.BlockSpec(memory_space=pltpu.SMEM)]
        + [pl.BlockSpec(memory_space=pltpu.VMEM)] * senders
        + ([] if out is None else [hbm]),
        out_specs=hbm,
        scratch_shapes=[pltpu.SemaphoreType.DMA((senders, fars))],
        input_output_aliases={} if out is None else {1 + senders: 0},
        compiler_params=pltpu.CompilerParams(vmem_limit_bytes=SMALL),
        name="gather_part",
    )(me, *got, *([] if out is None else [out]))


def exchange(blocks, cube):
    got = list(blocks)
    for d in sorted(range(1, cube), key=lambda d: (-d.bit_count(), -d)):
        got[d] = lax.ppermute(blocks[d], "cube", [(i, i ^ d) for i in range(cube)])
    return got


def local(
    sample_inphase,
    sample_quadrature,
    beam_inphase,
    beam_quadrature,
    recorded_diffraction,
    window_corners,
    filled_tallies,
    absorption_templates,
):
    local_energies = sample_inphase.shape[0]
    side = sample_inphase.shape[1]
    spots = recorded_diffraction.shape[2]
    fars = lax.axis_size("far")
    cube = lax.axis_size("cube")
    blocks = fars * cube
    tiles = lax.axis_size("ta")
    tile = lax.axis_index("ta")
    swap = [(0, 1), (1, 0)]
    assert tiles == 2 and fars == 2
    used = spots * 3 // 2
    divided = local_energies % tiles == 0
    n_e = local_energies // tiles if divided else local_energies
    pix = side * side // (blocks * tiles)
    two_level = divided and pix == SUBS * side and local_energies == SUBS and cube & (cube - 1) == 0
    own_rec = recorded_diffraction[:, 0]
    first = tile * n_e if divided else jnp.zeros((), jnp.int32)
    theirs = lax.ppermute(window_corners, "ta", swap)
    give = lax.dynamic_slice_in_dim(own_rec, (1 - tile) * n_e, n_e, 0) if divided else own_rec
    par_rec = lax.ppermute(give, "ta", swap)
    table = slot_table(
        window_corners[:, 0], theirs[:, 0], filled_tallies, first.astype(jnp.int32), n_e, side,
        (lax.axis_index("far") * cube + lax.axis_index("cube")).astype(jnp.int32) if two_level else 0,
    )
    stepped = gradient_step(
        (sample_inphase, sample_quadrature),
        (beam_inphase, beam_quadrature),
        own_rec,
        par_rec,
        table,
        n_e,
        used,
        cube if two_level else 1,
        tiles,
    )

    if two_level:
        far = lax.axis_index("far").astype(jnp.int32)
        me = lax.axis_index("cube").astype(jnp.int32)
        where = jnp.stack([me, far, tile.astype(jnp.int32)])
        project_near, basis_near = solve_templates(where, absorption_templates, fars, cube, n_e)
        opposite = [
            (f * cube + c, (1 - f) * cube + (c ^ (cube // 2))) for f in range(2) for c in range(cube)
        ]
        out, coefs = None, []
        parts = stepped[:cube], stepped[cube:]
        got = []
        for part in range(2):
            got.append(exchange(parts[part], cube))
        for part in range(2):
            blocks = [x.reshape(-1, LANES) for x in got[part]]
            kept, given = partial_coefs(
                tile.astype(jnp.int32)[None], project_near, blocks, fars, tiles
            )
            share = kept + lax.ppermute(given, "ta", swap)
            theirs = lax.ppermute(share, ("far", "cube"), opposite)
            coef, fit = fitted_values(far[None], share, theirs, basis_near, pix, cube)
            coefs.append(coef)
            fit = [x.reshape(local_energies, fars, pix // LANES, LANES) for x in fit]
            back = exchange(fit, cube)
            out = gather_part(part, where[:2], back, out)
        return (out.reshape(2, local_energies, cube * fars, 1, pix), jnp.stack(coefs))

    gram = jnp.dot(absorption_templates, absorption_templates.T, precision=HIGHEST)
    factor_low = jnp.linalg.cholesky(gram)
    project = jax.scipy.linalg.cho_solve((factor_low, True), absorption_templates)
    flat = jnp.stack([x.transpose(0, 1, 3, 2, 4) for x in stepped])
    if divided:
        flat = flat.reshape(2, n_e, blocks * tiles, pix)
        got = lax.all_to_all(flat, ("far", "cube", "ta"), 2, 1, tiled=True)
    else:
        flat = flat.reshape(2, n_e, blocks, tiles, pix)
        flat = lax.dynamic_index_in_dim(flat, tile, 3, keepdims=False)
        got = lax.all_to_all(flat, ("far", "cube"), 2, 1, tiled=True)
    values = got.reshape(2, -1, pix)
    coefs = jnp.einsum("ke,cen->ckn", project, values, precision=HIGHEST)
    fitted_here = jnp.einsum("ke,ckn->cen", absorption_templates, coefs, precision=HIGHEST)
    returned = lax.all_to_all(
        fitted_here[:, :, None, :], ("far", "cube"), split_axis=1, concat_axis=2, tiled=True
    )
    return (returned[:, :, :, None, :], coefs)


def solution(mesh):
    blocks, tiles = mesh.shape["ea"], mesh.shape["ta"]
    mesh = Mesh(mesh.devices.reshape(2, blocks // 2, tiles), ("far", "cube", "ta"))
    ea = ("far", "cube")
    in_specs = (
        P(ea, None, None),
        P(ea, None, None),
        P(ea, None, None, None),
        P(ea, None, None, None),
        P(ea, "ta", None, None, None),
        P(ea, "ta", None, None),
        P(ea, "ta"),
        P(),
    )
    out_specs = (P(None, ea, None, "ta", None), P(None, None, (*ea, "ta")))
    return jax.shard_map(local, mesh=mesh, in_specs=in_specs, out_specs=out_specs, check_vma=False)
```
